32 devices in a mesh: ens: 8 (over z, x), mesh: 4 (over y, core).
Axes of the slice: x: 2, y: 2, z: 4, core: 2. Of those that a mesh axis runs over, the one named last changes fastest.
Arguments:
- inputs: bfloat16 [8, 1024, 512], P('ens', 'mesh'), may hold values from -6 to 6
- cotangent: bfloat16 [8, 1024, 512], P('ens', 'mesh'), may hold values from -6 to 6
- noise_level: float32 [8], P('ens'), may hold values from 0.02 to 80
- neighbours: int32 [1024, 32], P('mesh'), may hold values from 0 to 1023, as said below
- live_slots: int32 [1024, 32], P('mesh'), may hold values from 0 to 1
- projections: bfloat16 [2, 4, 512, 512], replicated, may hold values from -4 to 4
- film_weights: float32 [2, 32, 1024], replicated, may hold values from -0.5 to 0.5
Outputs:
- grad_input: bfloat16 [8, 1024, 512], P('ens', 'mesh')
- grad_projections: float32 [2, 4, 512, 512], P(None, None, 'ens', 'mesh')
- grad_film: float32 [2, 32, 1024], P(None, None, 'mesh')
The draws below stay inside these ranges and needn't reach their ends.
Inputs may be any that keep to these rules, and one draw needn't show every extreme that they name: `neighbours`: slot 0 of node i names i and is live. The live slots of a node name distinct nodes within 128 of it; every node at least 128 from both ends of the numbering has a live slot exactly 128 away. Padded slots name the node itself.
All inputs are finite; a program needn't handle non-finite values.
Results may differ from the reference program's by a relative error of at most 0.028.
Values may be sent and summed in bfloat16 or wider, within the bound.
No kernel may reach another device: no remote copies, remote signals or barrier semaphores. Data moves between devices by JAX's collectives and lax.ppermute only.
A program may use at most 64 MiB of HBM per device.

```python
import math
import jax
import jax.numpy as jnp
from jax import lax

D = 512
HEADS = 4
HEAD = 128
SLOTS = 32
NOISE_FREQ = 16
LAYERS = 2
REACH = 128
MEMBERS = 8
NODES = 1024


def graph_tables(key):
    node_ids = jnp.arange(NODES)[:, None]
    candidates = jnp.concatenate([jnp.arange(-REACH, 0), jnp.arange(1, REACH + 1)])
    score_key, side_key, count_key = jax.random.split(jax.random.fold_in(key, 7), 3)
    raw_scores = jax.random.randint(score_key, (NODES, 2 * REACH), 0, 1 << 20)
    rank_scores = raw_scores * (2 * REACH) + jnp.arange(2 * REACH)[None, :]
    far_side = jax.random.randint(side_key, (NODES,), 0, 2)
    far_slot = jnp.where(far_side == 0, 0, 2 * REACH - 1)
    rank_scores = jnp.where(jnp.arange(2 * REACH)[None, :] == far_slot[:, None], 1 << 30, rank_scores)
    picked = lax.top_k(rank_scores, SLOTS - 1)[1]
    offsets = jnp.concatenate([jnp.zeros((NODES, 1), jnp.int32), candidates[picked].astype(jnp.int32)], axis=1)
    targets = node_ids + offsets
    inside = (targets >= 0) & (targets < NODES)
    counts = jax.random.randint(count_key, (NODES, 1), SLOTS // 2, SLOTS + 1)
    live_flags = inside & (jnp.arange(SLOTS)[None, :] < counts)
    neighbours = jnp.where(live_flags, targets, node_ids)
    return (neighbours.astype(jnp.int32), live_flags.astype(jnp.int32))


def draw_neighbours(key, part):
    return graph_tables(key)[0]


def draw_live_slots(key, part):
    return graph_tables(key)[1]


def draw_projections(key, part):
    base_key = jax.random.fold_in(jax.random.fold_in(key, 11), 0)
    base_draw = jax.random.normal(base_key, (LAYERS, 4, D, D), jnp.float32) / math.sqrt(D)
    return jnp.clip(base_draw, -4.0, 4.0).astype(jnp.bfloat16)


def steps_of(own_key, dims, cuts, smallest, high):
    level = 1.0
    for dim, blocks in cuts:
        draws = jax.random.uniform(jax.random.fold_in(jax.random.fold_in(own_key, 6), dim), (blocks,), jnp.float32, smallest / len(cuts), high / len(cuts))
        level = level * jnp.repeat(jnp.exp(draws), dims[dim] // blocks).reshape((-1,) + (1,) * (len(dims) - 1 - dim))
    return level


def scatter_about(own_key, dims, width, limit, cuts=(), held_as=jnp.bfloat16):
    factor_of = steps_of(own_key, dims, cuts, -0.22, 0.18) if cuts else 1.0
    values = jax.random.normal(own_key, dims, jnp.float32) * width * factor_of
    return jnp.minimum(jnp.maximum(values, -limit), limit).astype(held_as)


def setup_inputs(seed: int = 0) -> dict:
    keys = jax.random.split(jax.random.key(seed), 8)
    return {
        "inputs": scatter_about(keys[0], (MEMBERS, NODES, D), 1.0, 6.0, ((0, 8), (1, 4))),
        "cotangent": scatter_about(keys[1], (MEMBERS, NODES, D), 1.0, 6.0, ((0, 8), (1, 4))),
        "noise_level": jnp.clip(jnp.exp(math.log(80.0) - 8.2940497 * jax.random.uniform(keys[2], (MEMBERS,), jnp.float32) ** steps_of(keys[2], (MEMBERS,), ((0, 8),), -0.2, 0.2)), 0.02, 80.0),
        "neighbours": draw_neighbours(jax.random.fold_in(keys[7], 71), 0),
        "live_slots": draw_live_slots(jax.random.fold_in(keys[7], 71), 0),
        "projections": draw_projections(jax.random.fold_in(keys[7], 71), 0),
        "film_weights": scatter_about(keys[6], (LAYERS, 2 * NOISE_FREQ, 2 * D), 0.1, 0.5, (), jnp.float32),
    }


epsilon = 1e-05

def noise_features(noise_level):
    frequency = jnp.arange(1, NOISE_FREQ + 1).astype(jnp.float32)
    angles = jnp.log(noise_level)[:, None] * frequency[None, :]
    return jnp.concatenate([jnp.sin(angles), jnp.cos(angles)], axis=1)

def project(left_side, right_side):
    return jnp.dot(left_side, right_side, preferred_element_type=jnp.float32)

def contract_rows(left_side, right_side):
    return lax.dot_general(left_side, right_side, (((0,), (0,)), ((), ())), preferred_element_type=jnp.float32)

def contract_cols(left_side, right_side):
    return lax.dot_general(left_side, right_side, (((1,), (1,)), ((), ())), preferred_element_type=jnp.float32)

def normalize(states, film_row):
    values = states.astype(jnp.float32)
    centre = lax.optimization_barrier(jnp.mean(values, axis=1, keepdims=True))
    spread = lax.optimization_barrier(jnp.mean(jnp.square(values - centre), axis=1, keepdims=True))
    inverse = lax.rsqrt(spread + epsilon)
    unit_rows = (values - centre) * inverse
    normed = (unit_rows * (1.0 + film_row[:D]) + film_row[D:]).astype(jnp.bfloat16)
    return (unit_rows, inverse, normed)

def gather_heads(rows, neighbours, head_index):
    return rows[:, head_index * HEAD:(head_index + 1) * HEAD][neighbours].astype(jnp.float32)

def slot_attention(query_head, key_slots, live_mask):
    scores = jnp.einsum('nc,nsc->ns', query_head, key_slots) / math.sqrt(HEAD)
    scores = jnp.where(live_mask, scores, -jnp.inf)
    row_peak = lax.optimization_barrier(jnp.max(scores, axis=1, keepdims=True))
    weights = jnp.where(live_mask, jnp.exp(scores - row_peak), 0.0)
    return weights / lax.optimization_barrier(jnp.sum(weights, axis=1, keepdims=True))

def forward_layer(states, film_row, weights, neighbours, live_mask):
    unit_rows, inverse, normed = normalize(states, film_row)
    queries = project(normed, weights[0]).astype(jnp.bfloat16)
    key_rows = project(normed, weights[1]).astype(jnp.bfloat16)
    value_rows = project(normed, weights[2]).astype(jnp.bfloat16)
    pieces = []
    for head_index in range(HEADS):
        head_cols = slice(head_index * HEAD, (head_index + 1) * HEAD)
        attention = slot_attention(queries[:, head_cols].astype(jnp.float32), gather_heads(key_rows, neighbours, head_index), live_mask)
        rounded = lax.optimization_barrier(attention.astype(jnp.bfloat16)).astype(jnp.float32)
        pieces.append(jnp.einsum('ns,nsc->nc', rounded, gather_heads(value_rows, neighbours, head_index)))
    attended = jnp.concatenate(pieces, axis=1).astype(jnp.bfloat16)
    outputs = (states.astype(jnp.float32) + project(attended, weights[3])).astype(jnp.bfloat16)
    return (outputs, (unit_rows, inverse, normed, queries, key_rows, value_rows, attended))

def backward_layer(upstream, film_row, weights, stored, neighbours, live_mask):
    unit_rows, inverse, normed, queries, key_rows, value_rows, attended = stored
    node_count = upstream.shape[0]
    grad_out = contract_rows(attended, upstream)
    grad_attended = contract_cols(upstream, weights[3]).astype(jnp.bfloat16)
    query_parts, key_parts, value_parts = ([], [], [])
    for head_index in range(HEADS):
        head_cols = slice(head_index * HEAD, (head_index + 1) * HEAD)
        key_slots = gather_heads(key_rows, neighbours, head_index)
        value_slots = gather_heads(value_rows, neighbours, head_index)
        query_head = queries[:, head_cols].astype(jnp.float32)
        attention = slot_attention(query_head, key_slots, live_mask)
        rounded = lax.optimization_barrier(attention.astype(jnp.bfloat16)).astype(jnp.float32)
        grad_head = grad_attended[:, head_cols].astype(jnp.float32)
        grad_probs = jnp.einsum('nc,nsc->ns', grad_head, value_slots)
        grad_scores = attention * (grad_probs - lax.optimization_barrier(jnp.sum(attention * grad_probs, axis=1, keepdims=True))) / math.sqrt(HEAD)
        grad_scores = lax.optimization_barrier(grad_scores.astype(jnp.bfloat16)).astype(jnp.float32)
        query_parts.append(jnp.einsum('ns,nsc->nc', grad_scores, key_slots))
        key_terms = grad_scores[:, :, None] * query_head[:, None, :]
        key_parts.append(jnp.zeros((node_count, HEAD), jnp.float32).at[neighbours].add(key_terms))
        value_terms = rounded[:, :, None] * grad_head[:, None, :]
        value_parts.append(jnp.zeros((node_count, HEAD), jnp.float32).at[neighbours].add(value_terms))
    grad_queries = jnp.concatenate(query_parts, axis=1).astype(jnp.bfloat16)
    grad_keys = jnp.concatenate(key_parts, axis=1).astype(jnp.bfloat16)
    grad_values = jnp.concatenate(value_parts, axis=1).astype(jnp.bfloat16)
    grad_weights = jnp.stack([contract_rows(normed, grad_queries), contract_rows(normed, grad_keys), contract_rows(normed, grad_values), grad_out])
    grad_normed = contract_cols(grad_queries, weights[0]) + contract_cols(grad_keys, weights[1]) + contract_cols(grad_values, weights[2])
    grad_conditioning = jnp.concatenate([lax.optimization_barrier(jnp.sum(grad_normed * unit_rows, axis=0)), lax.optimization_barrier(jnp.sum(grad_normed, axis=0))])
    grad_unit = grad_normed * (1.0 + film_row[:D])
    centred = grad_unit - lax.optimization_barrier(jnp.mean(grad_unit, axis=1, keepdims=True)) - unit_rows * lax.optimization_barrier(jnp.mean(grad_unit * unit_rows, axis=1, keepdims=True))
    new_upstream = (upstream.astype(jnp.float32) + inverse * centred).astype(jnp.bfloat16)
    return (new_upstream, grad_weights, grad_conditioning)

def member_pass(states, cotangent, embedding, projections, film_weights, neighbours, live_mask):
    film_rows = [jnp.dot(embedding[None, :], film_weights[layer_number], precision=lax.Precision.HIGHEST)[0] for layer_number in range(LAYERS)]
    stored = []
    current = states
    for layer_number in range(LAYERS):
        current, saved = forward_layer(current, film_rows[layer_number], projections[layer_number], neighbours, live_mask)
        stored.append(saved)
    upstream = cotangent
    weight_list = [None] * LAYERS
    film_list = [None] * LAYERS
    for layer_number in reversed(range(LAYERS)):
        upstream, grad_weights, grad_conditioning = backward_layer(upstream, film_rows[layer_number], projections[layer_number], stored[layer_number], neighbours, live_mask)
        weight_list[layer_number] = grad_weights
        film_list[layer_number] = embedding[:, None] * grad_conditioning[None, :]
    return (upstream, jnp.stack(weight_list), jnp.stack(film_list))

def reference(inputs, cotangent, noise_level, neighbours, live_slots, projections, film_weights):
    embeddings = noise_features(noise_level)
    live_mask = live_slots > 0

    def per_member(bundle):
        return member_pass(bundle[0], bundle[1], bundle[2], projections, film_weights, neighbours, live_mask)
    grad_input, weight_all, film_all = lax.map(per_member, (inputs, cotangent, embeddings))
    return (grad_input, lax.optimization_barrier(jnp.sum(weight_all, axis=0)), lax.optimization_barrier(jnp.sum(film_all, axis=0)))
```

```python
import math

import jax
import jax.numpy as jnp
from jax import lax
from jax.experimental import pallas as pl
from jax.experimental.pallas import tpu as pltpu
from jax.sharding import PartitionSpec as P

HEADS = 4
NOISE_FREQ = 16
LAYERS = 2
LANES = 128

epsilon = 1e-05
F32 = jnp.float32
BF16 = jnp.bfloat16
ABSENT = -1e30


def mm(left_side, right_side):
    return jnp.dot(left_side, right_side, preferred_element_type=F32)


def mm_rows(left_side, right_side):
    return lax.dot_general(
        left_side, right_side, (((0,), (0,)), ((), ())), preferred_element_type=F32
    )


def mm_cols(left_side, right_side):
    return lax.dot_general(
        left_side, right_side, (((1,), (1,)), ((), ())), preferred_element_type=F32
    )


def unit_of(states):
    values = states.astype(F32)
    centre = jnp.mean(values, axis=1, keepdims=True)
    centred = values - centre
    inverse = lax.rsqrt(jnp.mean(jnp.square(centred), axis=1, keepdims=True) + epsilon)
    return centred * inverse, inverse


def normed_of(states, film_ref, layer):
    width = states.shape[1]
    unit, _ = unit_of(states)
    scale = film_ref[layer : layer + 1, :width]
    shift = film_ref[layer : layer + 1, width:]
    return (unit * (1.0 + scale) + shift).astype(BF16)


def embedding_of(noise):
    row = lax.broadcasted_iota(jnp.int32, noise.shape, 0)
    wave = row - jnp.where(row >= NOISE_FREQ, NOISE_FREQ, 0) + 1
    angle = jnp.log(noise) * wave.astype(F32)
    return jnp.where(row < NOISE_FREQ, jnp.sin(angle), jnp.cos(angle))


def project_own(normed, w_ref, layer, q_ref, k_ref, v_ref):
    for slot, out_ref in enumerate((q_ref, k_ref, v_ref)):
        out_ref[...] = mm(normed, w_ref[layer, slot]).astype(BF16)


def start_kernel(
    x_ref, near_ref, live_ref, noise_ref, film_w_ref, w_ref,
    film_ref, bias_own_ref, bias_halo_ref, normed_ref, q_ref, k_ref, v_ref,
):
    node_count, slots = near_ref.shape
    rim = node_count // 2
    place = lax.axis_index("mesh")
    parity = lax.rem(place, 2)
    embedding = embedding_of(jnp.full((2 * NOISE_FREQ, 1), noise_ref[0], F32))
    for layer in range(LAYERS):
        film_ref[layer : layer + 1, :] = jnp.sum(
            embedding * film_w_ref[layer], axis=0, keepdims=True
        )
    normed = normed_of(x_ref[...], film_ref, 0)
    normed_ref[...] = normed
    project_own(normed, w_ref, 0, q_ref, k_ref, v_ref)
    column = lax.broadcasted_iota(jnp.int32, (1, node_count), 1)
    low, high = column - node_count, column + rim
    beside = jnp.where(column < rim, high + rim, low)
    behind = jnp.where(column < rim, column - rim, high)
    halo = jnp.where(parity == 0, beside, behind)
    halo = jnp.where(column < rim,
                     jnp.where(parity == 0, column + node_count, column - rim),
                     jnp.where(parity == 0, column - node_count, column + rim))
    step = 32

    def rows(index, carry):
        start = pl.multiple_of(index * step, step)
        near = near_ref[pl.ds(start, step), :] - place * node_count
        near = jnp.where(live_ref[pl.ds(start, step), :] > 0, near, -(1 << 24))
        for ids, out_ref in ((column, bias_own_ref), (halo, bias_halo_ref)):
            bias = jnp.full((step, node_count), ABSENT, F32)
            for slot in range(slots):
                bias = jnp.where(near[:, slot : slot + 1] == ids, 0.0, bias)
            out_ref[pl.ds(start, step), :] = bias
        return carry

    lax.fori_loop(0, node_count // step, rows, 0)


def own_kernel(x_ref, cot_ref, film_ref, w_ref, normed_ref, q_ref, k_ref, v_ref, ga_ref):
    normed = normed_of(x_ref[...], film_ref, 1)
    normed_ref[...] = normed
    project_own(normed, w_ref, 1, q_ref, k_ref, v_ref)
    ga_ref[...] = mm_cols(cot_ref[...], w_ref[1, 3]).astype(BF16)


def project_halo(pair_ref, other_ref, film_ref, w_ref, layer, normed_ref, k_ref, v_ref):
    rim = pair_ref.shape[0]
    normed_ref[:rim, :] = normed_of(pair_ref[...], film_ref, layer)
    normed_ref[rim:, :] = normed_of(other_ref[...], film_ref, layer)
    normed = normed_ref[...]
    k_ref[...] = mm(normed, w_ref[layer, 1]).astype(BF16)
    v_ref[...] = mm(normed, w_ref[layer, 2]).astype(BF16)


def softmax_blocks(query, keys, biases):
    factor = 1.0 / math.sqrt(query.shape[1])
    scores = [mm_cols(query, key) * factor + bias for key, bias in zip(keys, biases)]
    peak = jnp.max(jnp.maximum(*scores), axis=1, keepdims=True)
    weights = [jnp.exp(score - peak) for score in scores]
    total = jnp.sum(weights[0] + weights[1], axis=1, keepdims=True)
    share = 1.0 / total
    return [weight * share for weight in weights]


def heads_of(width):
    head = width // HEADS
    return [slice(index * head, (index + 1) * head) for index in range(HEADS)]


def forward_kernel(
    x_ref, pair_ref, other_ref, film_ref, q_ref, k_ref, v_ref, bias_own_ref, bias_halo_ref, w_ref,
    next_ref, to_pair_ref, to_other_ref, normed_h_ref, k_h_ref, v_h_ref, p_own_ref, p_halo_ref,
    attended_ref,
):
    rim = pair_ref.shape[0]
    parity = lax.rem(lax.axis_index("mesh"), 2)
    project_halo(pair_ref, other_ref, film_ref, w_ref, 0, normed_h_ref, k_h_ref, v_h_ref)
    for index, cols in enumerate(heads_of(x_ref.shape[1])):
        own, halo = softmax_blocks(
            q_ref[:, cols],
            (k_ref[:, cols], k_h_ref[:, cols]),
            (bias_own_ref[...], bias_halo_ref[...]),
        )
        own, halo = own.astype(BF16), halo.astype(BF16)
        p_own_ref[index] = own
        p_halo_ref[index] = halo
        attended_ref[:, cols] = (mm(own, v_ref[:, cols]) + mm(halo, v_h_ref[:, cols])).astype(BF16)
    next_ref[...] = (x_ref[...].astype(F32) + mm(attended_ref[...], w_ref[0, 3])).astype(BF16)
    to_pair_ref[...] = next_ref[pl.ds(pl.multiple_of((1 - parity) * rim, rim), rim), :]
    to_other_ref[...] = next_ref[pl.ds(pl.multiple_of(parity * rim, rim), rim), :]


def head_backward(
    cols, own, halo, own16, halo16, ga_ref, q_ref, k_ref, v_ref, k_h_ref, v_h_ref,
    gq_ref, gk_ref, gv_ref, gk_h_ref, gv_h_ref,
):
    grad = ga_ref[:, cols]
    query = q_ref[:, cols]
    factor = 1.0 / math.sqrt(query.shape[1])
    probs = mm_cols(grad, v_ref[:, cols])
    probs_h = mm_cols(grad, v_h_ref[:, cols])
    middle = jnp.sum(own * probs + halo * probs_h, axis=1, keepdims=True)
    scores = (own * (probs - middle) * factor).astype(BF16)
    scores_h = (halo * (probs_h - middle) * factor).astype(BF16)
    gq_ref[:, cols] = (mm(scores, k_ref[:, cols]) + mm(scores_h, k_h_ref[:, cols])).astype(BF16)
    gk_ref[:, cols] = mm_rows(scores, query).astype(BF16)
    gk_h_ref[:, cols] = mm_rows(scores_h, query).astype(BF16)
    gv_ref[:, cols] = mm_rows(own16, grad).astype(BF16)
    gv_h_ref[:, cols] = mm_rows(halo16, grad).astype(BF16)


def grads_out(
    layer, unit, pair_ref, other_ref, w_ref, gq_ref, gk_ref, gv_ref, gk_h_ref, gv_h_ref,
    gn_ref, to_pair_ref, to_other_ref, cond_ref,
):
    rim, width = pair_ref.shape
    grad_h = mm_cols(gk_h_ref[...], w_ref[layer, 1]) + mm_cols(gv_h_ref[...], w_ref[layer, 2])
    to_pair_ref[...] = grad_h[:rim].astype(BF16)
    to_other_ref[...] = grad_h[rim:].astype(BF16)
    grad = (
        mm_cols(gq_ref[...], w_ref[layer, 0])
        + mm_cols(gk_ref[...], w_ref[layer, 1])
        + mm_cols(gv_ref[...], w_ref[layer, 2])
    )
    gn_ref[...] = grad
    pair, _ = unit_of(pair_ref[...])
    other, _ = unit_of(other_ref[...])

    def over_nodes(term):
        return jnp.sum(term, axis=0, keepdims=True)

    cond_ref[:, :width] = (
        over_nodes(grad * unit) + over_nodes(grad_h[:rim] * pair) + over_nodes(grad_h[rim:] * other)
    )
    cond_ref[:, width:] = over_nodes(grad) + over_nodes(grad_h)


def last_layer_kernel(
    x_ref, pair_ref, other_ref, film_ref, q_ref, k_ref, v_ref, ga_ref, bias_own_ref, bias_halo_ref,
    w_ref,
    normed_h_ref, attended_ref, gq_ref, gk_ref, gv_ref, gk_h_ref, gv_h_ref,
    gn_ref, to_pair_ref, to_other_ref, cond_ref,
    k_h_ref, v_h_ref,
):
    project_halo(pair_ref, other_ref, film_ref, w_ref, 1, normed_h_ref, k_h_ref, v_h_ref)
    for cols in heads_of(x_ref.shape[1]):
        own, halo = softmax_blocks(
            q_ref[:, cols],
            (k_ref[:, cols], k_h_ref[:, cols]),
            (bias_own_ref[...], bias_halo_ref[...]),
        )
        own16, halo16 = own.astype(BF16), halo.astype(BF16)
        attended_ref[:, cols] = (mm(own16, v_ref[:, cols]) + mm(halo16, v_h_ref[:, cols])).astype(BF16)
        head_backward(
            cols, own, halo, own16, halo16, ga_ref, q_ref, k_ref, v_ref, k_h_ref, v_h_ref,
            gq_ref, gk_ref, gv_ref, gk_h_ref, gv_h_ref,
        )
    unit, _ = unit_of(x_ref[...])
    grads_out(
        1, unit, pair_ref, other_ref, w_ref, gq_ref, gk_ref, gv_ref, gk_h_ref, gv_h_ref,
        gn_ref, to_pair_ref, to_other_ref, cond_ref,
    )


def upstream_of(x, up, gn_ref, pair_ref, other_ref, film_ref, layer, total_ref):
    rim, width = pair_ref.shape
    parity = lax.rem(lax.axis_index("mesh"), 2)
    total_ref[...] = gn_ref[...]
    at_pair = pl.ds(pl.multiple_of((1 - parity) * rim, rim), rim)
    at_other = pl.ds(pl.multiple_of(parity * rim, rim), rim)
    total_ref[at_pair, :] += pair_ref[...].astype(F32)
    total_ref[at_other, :] += other_ref[...].astype(F32)
    unit, inverse = unit_of(x)
    grad = total_ref[...] * (1.0 + film_ref[layer : layer + 1, :width])
    centred = (
        grad
        - jnp.mean(grad, axis=1, keepdims=True)
        - unit * jnp.mean(grad * unit, axis=1, keepdims=True)
    )
    return (up.astype(F32) + inverse * centred).astype(BF16)


def first_layer_kernel(
    next_ref, cot_ref, gn2_ref, back_pair_ref, back_other_ref, film_ref,
    x_ref, pair_ref, other_ref, q_ref, k_ref, v_ref, k_h_ref, v_h_ref, p_own_ref, p_halo_ref, w_ref,
    up_ref, gq_ref, gk_ref, gv_ref, gk_h_ref, gv_h_ref, gn_ref, to_pair_ref, to_other_ref, cond_ref,
    total_ref, ga_ref,
):
    up = upstream_of(
        next_ref[...], cot_ref[...], gn2_ref, back_pair_ref, back_other_ref, film_ref, 1, total_ref
    )
    up_ref[...] = up
    ga_ref[...] = mm_cols(up, w_ref[0, 3]).astype(BF16)
    for index, cols in enumerate(heads_of(x_ref.shape[1])):
        own16, halo16 = p_own_ref[index], p_halo_ref[index]
        head_backward(
            cols, own16.astype(F32), halo16.astype(F32), own16, halo16,
            ga_ref, q_ref, k_ref, v_ref, k_h_ref, v_h_ref,
            gq_ref, gk_ref, gv_ref, gk_h_ref, gv_h_ref,
        )
    unit, _ = unit_of(x_ref[...])
    grads_out(
        0, unit, pair_ref, other_ref, w_ref, gq_ref, gk_ref, gv_ref, gk_h_ref, gv_h_ref,
        gn_ref, to_pair_ref, to_other_ref, cond_ref,
    )


def end_kernel(x_ref, up_ref, gn_ref, pair_ref, other_ref, film_ref, out_ref, total_ref):
    out_ref[...] = upstream_of(
        x_ref[...], up_ref[...], gn_ref, pair_ref, other_ref, film_ref, 0, total_ref
    )


def weight_products(
    normed_ref, normed_h_ref, attended_ref, up_ref, gq_ref, gk_ref, gv_ref, gk_h_ref, gv_h_ref, put
):
    put(0, mm_rows(normed_ref[...], gq_ref[...]))
    put(1, mm_rows(normed_ref[...], gk_ref[...]) + mm_rows(normed_h_ref[...], gk_h_ref[...]))
    put(2, mm_rows(normed_ref[...], gv_ref[...]) + mm_rows(normed_h_ref[...], gv_h_ref[...]))
    put(3, mm_rows(attended_ref[...], up_ref[...]))


def plain_weight_kernel(*refs):
    *ins, out_ref = refs

    def put(slot, value):
        out_ref[slot] = value

    weight_products(*ins, put)


def split_weight_kernel(*refs):
    *ins, send_ref, keep_ref, total_ref = refs

    def put(slot, value):
        total_ref[slot] = value

    weight_products(*ins, put)
    _, _, _, deep, _, _ = keep_ref.shape
    rows = keep_ref.shape[4] // 2
    ens, mesh = lax.axis_index("ens"), lax.axis_index("mesh")
    for slot in range(4):
        group, inner = slot // 2, slot % 2
        spot = slice(inner * rows, (inner + 1) * rows)
        for core in range(2):
            for y in range(2):
                col = lax.bitwise_xor(mesh, y * 2 + core)
                cols = pl.ds(pl.multiple_of(col * LANES, LANES), LANES)
                for x in range(2):
                    for z in range(deep):
                        row = lax.bitwise_xor(ens, z * 2 + x)
                        at = pl.ds(pl.multiple_of(row * rows, rows), rows)
                        piece = total_ref[slot, at, cols]
                        first, second = (y, x) if group == 0 else (x, y)
                        if core:
                            send_ref[group, first, second, z, spot, :] = piece.astype(BF16)
                        else:
                            keep_ref[group, first, second, z, spot, :] = piece


def film_kernel(rows_ref, noise_ref, out_ref):
    members = rows_ref.shape[0]
    for layer in range(LAYERS):
        total = jnp.zeros(out_ref.shape[1:], F32)
        for member in range(members):
            noise = jnp.full((2 * NOISE_FREQ, 1), noise_ref[member], F32)
            total += embedding_of(noise) * rows_ref[member, layer : layer + 1, :]
        out_ref[layer] = total


def whole():
    return pl.BlockSpec(memory_space=pltpu.VMEM)


def call(kernel, name, args, outs, scratch=(), flops=0, specs=None):
    moved = sum(a.size * a.dtype.itemsize for a in args)
    moved += sum(math.prod(shape) * jnp.dtype(kind).itemsize for shape, kind in outs)
    return pl.pallas_call(
        kernel,
        name=name,
        out_shape=[jax.ShapeDtypeStruct(shape, kind) for shape, kind in outs],
        in_specs=specs or [whole() for _ in args],
        out_specs=[whole() for _ in outs],
        scratch_shapes=[pltpu.VMEM(shape, kind) for shape, kind in scratch],
        cost_estimate=pl.CostEstimate(flops=flops, bytes_accessed=moved, transcendentals=0),
    )(*args)


def swap(block, axis, bit):
    count = lax.axis_size(axis)
    return lax.ppermute(block, axis, [(i, i ^ bit) for i in range(count)])


def exchange(to_pair, to_other):
    count = lax.axis_size("mesh")
    route = []
    for i in range(1, count - 1, 2):
        route += [(i, i + 1), (i + 1, i)]
    other = lax.ppermute(to_other, "mesh", route)
    return swap(to_pair, "mesh", 1), other


def scattered_core(send):
    return swap(send, "mesh", 1)


def scatter_first(keep, send):
    held = keep + swap(send, "mesh", 1).astype(F32)
    to_y, to_x = held[0, 1].astype(BF16), held[1, 1].astype(BF16)
    return (held[0, 0], held[1, 0]), (swap(to_y, "mesh", 2), swap(to_x, "ens", 1))


def scatter_second(kept, came):
    one = kept[0] + came[0].astype(F32)
    two = kept[1] + came[1].astype(F32)
    to_x, to_y = one[1].astype(BF16), two[1].astype(BF16)
    return (one[0], two[0]), (swap(to_x, "ens", 1), swap(to_y, "mesh", 2))


def scatter_third(kept, came):
    both = jnp.stack([kept[0] + came[0].astype(F32), kept[1] + came[1].astype(F32)])
    total = both[:, 0]
    came = [swap(both[:, z].astype(BF16), "ens", 2 * z) for z in range(1, both.shape[1])]
    for part in came:
        total = total + part.astype(F32)
    return total


def film_sum(conds, noise_level, mesh_count):
    mesh = lax.axis_index("mesh")
    rows = jnp.concatenate(conds, axis=0)
    width = rows.shape[1] // mesh_count
    pieces = rows.reshape(LAYERS, mesh_count, width).transpose(1, 0, 2)
    order = lax.bitwise_xor(jnp.arange(mesh_count), mesh)
    pieces = jnp.take(pieces, order, axis=0)
    bit = 1
    while bit < mesh_count:
        pieces = pieces.reshape(-1, 2, LAYERS, width)
        pieces = pieces[:, 0] + swap(pieces[:, 1], "mesh", bit)
        bit *= 2
    row = jnp.concatenate([pieces[0], jnp.full((1, width), noise_level[0])])[None]
    bit = 1
    while bit < lax.axis_size("ens"):
        row = jnp.concatenate([row, swap(row, "ens", bit)])
        bit *= 2
    noise = row[:, LAYERS, 0]
    return call(
        film_kernel, "film", (row, noise), [((LAYERS, 2 * NOISE_FREQ, width), F32)],
        specs=[whole(), pl.BlockSpec(memory_space=pltpu.SMEM)],
    )[0]


def body(inputs, cotangent, noise_level, neighbours, live_slots, projections, film_weights):
    states, cot = inputs[0], cotangent[0]
    nodes, width = states.shape
    rim = nodes // 2
    mesh_count, ens_count = lax.axis_size("mesh"), lax.axis_size("ens")
    parity = lax.rem(lax.axis_index("mesh"), 2)
    square = 2 * nodes * width * width
    mesh_split = width // mesh_count
    split = mesh_count == 4 and mesh_split % LANES == 0 and ens_count % 2 == 0

    def full(kind=BF16):
        return ((nodes, width), kind)

    rims = [((rim, width), BF16)] * 2
    cond_shape = ((1, 2 * width), F32)
    pair1, other1 = exchange(
        lax.dynamic_slice_in_dim(states, (1 - parity) * rim, rim),
        lax.dynamic_slice_in_dim(states, parity * rim, rim),
    )
    film, bias_own, bias_halo, normed1, q1, k1, v1 = call(
        start_kernel, "start",
        (states, neighbours, live_slots, noise_level, film_weights, projections),
        [((LAYERS, 2 * width), F32), ((nodes, nodes), F32), ((nodes, nodes), F32)] + [full()] * 4,
        flops=3 * square,
        specs=[whole()] * 3 + [pl.BlockSpec(memory_space=pltpu.SMEM)] + [whole()] * 2,
    )
    probs_shape = ((HEADS, nodes, nodes), BF16)
    states2, to_pair, to_other, normed1_h, k1_h, v1_h, p_own, p_halo, attended1 = call(
        forward_kernel, "forward",
        (states, pair1, other1, film, q1, k1, v1, bias_own, bias_halo, projections),
        [full()] + rims + [full()] * 3 + [probs_shape] * 2 + [full()],
        flops=5 * square,
    )
    pair2, other2 = exchange(to_pair, to_other)
    normed2, q2, k2, v2, ga2 = call(
        own_kernel, "own", (states2, cot, film, projections), [full()] * 5, flops=4 * square
    )
    grads = [full()] * 5 + [full(F32)] + rims + [cond_shape]
    normed2_h, attended2, gq2, gk2, gv2, gk2_h, gv2_h, gn2, to_pair, to_other, cond2 = call(
        last_layer_kernel, "last",
        (states2, pair2, other2, film, q2, k2, v2, ga2, bias_own, bias_halo, projections),
        [full()] * 2 + grads,
        scratch=[full()] * 2, flops=14 * square,
    )
    back_pair, back_other = exchange(to_pair, to_other)

    def weight_grads(name, *args):
        if not split:
            return call(
                plain_weight_kernel, name, args, [((4, width, width), F32)], flops=6 * square
            )[0]
        shape = (2, 2, 2, ens_count // 2, 2 * (width // ens_count), LANES)
        return call(
            split_weight_kernel, name, args, [(shape, BF16), (shape, F32)],
            scratch=[((4, width, width), F32)], flops=6 * square,
        )

    weights2 = weight_grads(
        "weights2", normed2, normed2_h, attended2, cot, gq2, gk2, gv2, gk2_h, gv2_h
    )
    up, gq1, gk1, gv1, gk1_h, gv1_h, gn1, to_pair, to_other, cond1 = call(
        first_layer_kernel, "first",
        (states2, cot, gn2, back_pair, back_other, film,
         states, pair1, other1, q1, k1, v1, k1_h, v1_h, p_own, p_halo, projections),
        [full()] + grads,
        scratch=[full(F32), full()], flops=11 * square,
    )
    back_pair, back_other = exchange(to_pair, to_other)
    weights1 = weight_grads(
        "weights1", normed1, normed1_h, attended1, up, gq1, gk1, gv1, gk1_h, gv1_h
    )
    grad_input = call(
        end_kernel, "end", (states, up, gn1, back_pair, back_other, film), [full()],
        scratch=[full(F32)],
    )[0]
    film_out = film_sum((cond1, cond2), noise_level, mesh_count)
    if split:
        outs = []
        for send, keep in (weights1, weights2):
            kept, came = scatter_first(keep, send)
            kept, came = scatter_second(kept, came)
            total = scatter_third(kept, came)
            outs.append(total.reshape(4, width // ens_count, LANES))
        weight_out = jnp.stack(outs)
    else:
        part = jnp.stack([weights1, weights2]).astype(BF16)
        part = lax.psum_scatter(part, "ens", scatter_dimension=2, tiled=True)
        weight_out = lax.psum_scatter(part, "mesh", scatter_dimension=3, tiled=True).astype(F32)
    return (grad_input[None], weight_out, film_out)


def solution(mesh):
    placed = (
        P("ens", "mesh", None),
        P("ens", "mesh", None),
        P("ens"),
        P("mesh", None),
        P("mesh", None),
        P(),
        P(),
    )
    return jax.shard_map(
        body,
        mesh=mesh,
        in_specs=placed,
        out_specs=(P("ens", "mesh", None), P(None, None, "ens", "mesh"), P(None, None, "mesh")),
        check_vma=False,
    )
```

```python
import functools
import math

import jax
import jax.numpy as jnp
from jax import lax
from jax.experimental import pallas as pl
from jax.experimental.pallas import tpu as pltpu
from jax.sharding import PartitionSpec as P


HEADS = 4
NOISE_FREQ = 16
LAYERS = 2
LANES = 128

epsilon = 1e-05
F32 = jnp.float32
BF16 = jnp.bfloat16
ABSENT = -1e30


def mm(left_side, right_side):
    return jnp.dot(left_side, right_side, preferred_element_type=F32)


def mm_rows(left_side, right_side):
    return lax.dot_general(
        left_side, right_side, (((0,), (0,)), ((), ())), preferred_element_type=F32
    )


def mm_cols(left_side, right_side):
    return lax.dot_general(
        left_side, right_side, (((1,), (1,)), ((), ())), preferred_element_type=F32
    )


def unit_of(states):
    values = states.astype(F32)
    centre = jnp.mean(values, axis=1, keepdims=True)
    centred = values - centre
    inverse = lax.rsqrt(jnp.mean(jnp.square(centred), axis=1, keepdims=True) + epsilon)
    return centred * inverse, inverse


def normed_of(states, film_ref, layer):
    width = states.shape[1]
    unit, _ = unit_of(states)
    scale = film_ref[layer : layer + 1, :width]
    shift = film_ref[layer : layer + 1, width:]
    return (unit * (1.0 + scale) + shift).astype(BF16)


def embedding_of(noise):
    row = lax.broadcasted_iota(jnp.int32, noise.shape, 0)
    wave = row - jnp.where(row >= NOISE_FREQ, NOISE_FREQ, 0) + 1
    angle = jnp.log(noise) * wave.astype(F32)
    return jnp.where(row < NOISE_FREQ, jnp.sin(angle), jnp.cos(angle))


def project_own(normed, w_ref, layer, q_ref, k_ref, v_ref):
    for slot, out_ref in enumerate((q_ref, k_ref, v_ref)):
        out_ref[...] = mm(normed, w_ref[layer, slot]).astype(BF16)


def start_kernel(
    x_hbm, near_hbm, live_hbm, noise_ref, film_w_hbm, w_hbm,
    film_ref, bias_own_ref, bias_halo_ref, normed_ref, q_ref, k_ref, v_ref, w_ref,
    x_ref, near_ref, live_ref, film_w_ref, near_t_ref, sems,
):
    copies = [
        pltpu.make_async_copy(near_hbm, near_ref, sems.at[0]),
        pltpu.make_async_copy(live_hbm, live_ref, sems.at[1]),
        pltpu.make_async_copy(x_hbm, x_ref, sems.at[2]),
        pltpu.make_async_copy(film_w_hbm, film_w_ref, sems.at[3]),
        pltpu.make_async_copy(w_hbm, w_ref, sems.at[4]),
    ]
    for copy in copies:
        copy.start()
    slots, node_count = near_ref.shape
    rim = node_count // 2
    place = lax.axis_index("mesh")
    parity = lax.rem(place, 2)
    embedding = embedding_of(jnp.full((2 * NOISE_FREQ, 1), noise_ref[0], F32))
    column = lax.broadcasted_iota(jnp.int32, (1, node_count), 1)
    halo = jnp.where(
        column < rim,
        jnp.where(parity == 0, column + node_count, column - rim),
        jnp.where(parity == 0, column - node_count, column + rim),
    )
    copies[0].wait()
    copies[1].wait()
    near = jnp.where(live_ref[...] > 0, near_ref[...] - place * node_count, -(1 << 24))
    near_t_ref[...] = near.T
    step = 32

    def rows(index, carry):
        start = pl.multiple_of(index * step, step)
        near = near_t_ref[pl.ds(start, step), :]
        for ids, out_ref in ((column, bias_own_ref), (halo, bias_halo_ref)):
            bias = jnp.full((step, node_count), ABSENT, F32)
            for slot in range(slots):
                bias = jnp.where(near[:, slot : slot + 1] == ids, 0.0, bias)
            out_ref[pl.ds(start, step), :] = bias
        return carry

    lax.fori_loop(0, node_count // step, rows, 0)
    copies[2].wait()
    copies[3].wait()
    for layer in range(LAYERS):
        film_ref[layer : layer + 1, :] = jnp.sum(
            embedding * film_w_ref[layer], axis=0, keepdims=True
        )
    normed = normed_of(x_ref[...], film_ref, 0)
    normed_ref[...] = normed
    copies[4].wait()
    project_own(normed, w_ref, 0, q_ref, k_ref, v_ref)


def own_kernel(x_ref, cot_ref, film_ref, w_ref, normed_ref, q_ref, k_ref, v_ref, ga_ref):
    normed = normed_of(x_ref[...], film_ref, 1)
    normed_ref[...] = normed
    project_own(normed, w_ref, 1, q_ref, k_ref, v_ref)
    ga_ref[...] = mm_cols(cot_ref[...], w_ref[1, 3]).astype(BF16)


def project_halo(pair_ref, other_ref, film_ref, w_ref, layer, normed_ref, k_ref, v_ref):
    rim = pair_ref.shape[0]
    normed_ref[:rim, :] = normed_of(pair_ref[...], film_ref, layer)
    normed_ref[rim:, :] = normed_of(other_ref[...], film_ref, layer)
    normed = normed_ref[...]
    k_ref[...] = mm(normed, w_ref[layer, 1]).astype(BF16)
    v_ref[...] = mm(normed, w_ref[layer, 2]).astype(BF16)


def softmax_blocks(query, keys, biases):
    factor = 1.0 / math.sqrt(query.shape[1])
    scores = [mm_cols(query, key) * factor + bias for key, bias in zip(keys, biases)]
    peak = jnp.max(jnp.maximum(*scores), axis=1, keepdims=True)
    weights = [jnp.exp(score - peak) for score in scores]
    total = jnp.sum(weights[0] + weights[1], axis=1, keepdims=True)
    share = 1.0 / total
    return [weight * share for weight in weights]


def heads_of(width):
    head = width // HEADS
    return [slice(index * head, (index + 1) * head) for index in range(HEADS)]


def forward_kernel(
    x_ref, pair_ref, other_ref, film_ref, q_ref, k_ref, v_ref, bias_own_ref, bias_halo_ref, w_ref,
    next_ref, to_pair_ref, to_other_ref, normed_h_ref, k_h_ref, v_h_ref, p_own_ref, p_halo_ref,
    attended_ref,
):
    rim = pair_ref.shape[0]
    parity = lax.rem(lax.axis_index("mesh"), 2)
    project_halo(pair_ref, other_ref, film_ref, w_ref, 0, normed_h_ref, k_h_ref, v_h_ref)
    for index, cols in enumerate(heads_of(x_ref.shape[1])):
        own, halo = softmax_blocks(
            q_ref[:, cols],
            (k_ref[:, cols], k_h_ref[:, cols]),
            (bias_own_ref[...], bias_halo_ref[...]),
        )
        own, halo = own.astype(BF16), halo.astype(BF16)
        p_own_ref[index] = own
        p_halo_ref[index] = halo
        attended_ref[:, cols] = (mm(own, v_ref[:, cols]) + mm(halo, v_h_ref[:, cols])).astype(BF16)
    next_ref[...] = (x_ref[...].astype(F32) + mm(attended_ref[...], w_ref[0, 3])).astype(BF16)
    to_pair_ref[...] = next_ref[pl.ds(pl.multiple_of((1 - parity) * rim, rim), rim), :]
    to_other_ref[...] = next_ref[pl.ds(pl.multiple_of(parity * rim, rim), rim), :]


def head_backward(
    cols, own, halo, own16, halo16, ga_ref, q_ref, k_ref, v_ref, k_h_ref, v_h_ref,
    gq_ref, gk_ref, gv_ref, gk_h_ref, gv_h_ref,
):
    grad = ga_ref[:, cols]
    query = q_ref[:, cols]
    factor = 1.0 / math.sqrt(query.shape[1])
    probs = mm_cols(grad, v_ref[:, cols])
    probs_h = mm_cols(grad, v_h_ref[:, cols])
    middle = jnp.sum(own * probs + halo * probs_h, axis=1, keepdims=True)
    scores = (own * (probs - middle) * factor).astype(BF16)
    scores_h = (halo * (probs_h - middle) * factor).astype(BF16)
    gq_ref[:, cols] = (mm(scores, k_ref[:, cols]) + mm(scores_h, k_h_ref[:, cols])).astype(BF16)
    gk_ref[:, cols] = mm_rows(scores, query).astype(BF16)
    gk_h_ref[:, cols] = mm_rows(scores_h, query).astype(BF16)
    gv_ref[:, cols] = mm_rows(own16, grad).astype(BF16)
    gv_h_ref[:, cols] = mm_rows(halo16, grad).astype(BF16)


def grads_out(
    layer, unit, pair_ref, other_ref, w_ref, gq_ref, gk_ref, gv_ref, gk_h_ref, gv_h_ref,
    gn_ref, to_pair_ref, to_other_ref, cond_ref,
):
    rim, width = pair_ref.shape
    grad_h = mm_cols(gk_h_ref[...], w_ref[layer, 1]) + mm_cols(gv_h_ref[...], w_ref[layer, 2])
    to_pair_ref[...] = grad_h[:rim].astype(BF16)
    to_other_ref[...] = grad_h[rim:].astype(BF16)
    grad = (
        mm_cols(gq_ref[...], w_ref[layer, 0])
        + mm_cols(gk_ref[...], w_ref[layer, 1])
        + mm_cols(gv_ref[...], w_ref[layer, 2])
    )
    gn_ref[...] = grad
    pair, _ = unit_of(pair_ref[...])
    other, _ = unit_of(other_ref[...])

    def over_nodes(term):
        return jnp.sum(term, axis=0, keepdims=True)

    cond_ref[:, :width] = (
        over_nodes(grad * unit) + over_nodes(grad_h[:rim] * pair) + over_nodes(grad_h[rim:] * other)
    )
    cond_ref[:, width:] = over_nodes(grad) + over_nodes(grad_h)


def last_layer_kernel(
    x_ref, pair_ref, other_ref, film_ref, q_ref, k_ref, v_ref, ga_ref, bias_own_ref, bias_halo_ref,
    w_ref,
    normed_h_ref, attended_ref, gq_ref, gk_ref, gv_ref, gk_h_ref, gv_h_ref,
    gn_ref, to_pair_ref, to_other_ref, cond_ref,
    k_h_ref, v_h_ref,
):
    project_halo(pair_ref, other_ref, film_ref, w_ref, 1, normed_h_ref, k_h_ref, v_h_ref)
    for cols in heads_of(x_ref.shape[1]):
        own, halo = softmax_blocks(
            q_ref[:, cols],
            (k_ref[:, cols], k_h_ref[:, cols]),
            (bias_own_ref[...], bias_halo_ref[...]),
        )
        own16, halo16 = own.astype(BF16), halo.astype(BF16)
        attended_ref[:, cols] = (mm(own16, v_ref[:, cols]) + mm(halo16, v_h_ref[:, cols])).astype(BF16)
        head_backward(
            cols, own, halo, own16, halo16, ga_ref, q_ref, k_ref, v_ref, k_h_ref, v_h_ref,
            gq_ref, gk_ref, gv_ref, gk_h_ref, gv_h_ref,
        )
    unit, _ = unit_of(x_ref[...])
    grads_out(
        1, unit, pair_ref, other_ref, w_ref, gq_ref, gk_ref, gv_ref, gk_h_ref, gv_h_ref,
        gn_ref, to_pair_ref, to_other_ref, cond_ref,
    )


def upstream_of(base, x, up, gn_ref, pair_ref, other_ref, film_ref, layer, total_ref):
    rim, width = other_ref.shape
    parity = lax.rem(lax.axis_index("mesh"), 2)
    total_ref[...] = gn_ref[...]
    at_pair = pl.ds(pl.multiple_of((1 - parity) * rim, rim), rim)
    at_other = pl.ds(pl.multiple_of(parity * rim, rim), rim)
    if base is None:
        total_ref[at_pair, :] += pair_ref[...].astype(F32)
    else:
        for block in range(width // LANES):
            start = base + block * rim
            cols = slice(block * LANES, (block + 1) * LANES)
            total_ref[at_pair, cols] += pair_ref[start : start + rim, :].astype(F32)
    total_ref[at_other, :] += other_ref[...].astype(F32)
    unit, inverse = unit_of(x)
    grad = total_ref[...] * (1.0 + film_ref[layer : layer + 1, :width])
    centred = (
        grad
        - jnp.mean(grad, axis=1, keepdims=True)
        - unit * jnp.mean(grad * unit, axis=1, keepdims=True)
    )
    return (up.astype(F32) + inverse * centred).astype(BF16)


def first_layer_kernel(
    base, next_ref, cot_ref, gn2_ref, back_pair_ref, back_other_ref, film_ref,
    x_ref, pair_ref, other_ref, q_ref, k_ref, v_ref, k_h_ref, v_h_ref, p_own_ref, p_halo_ref, w_ref,
    up_ref, gq_ref, gk_ref, gv_ref, gk_h_ref, gv_h_ref, gn_ref, to_pair_ref, to_other_ref, cond_ref,
    total_ref, ga_ref,
):
    up = upstream_of(
        base, next_ref[...], cot_ref[...], gn2_ref, back_pair_ref, back_other_ref, film_ref, 1,
        total_ref,
    )
    up_ref[...] = up
    ga_ref[...] = mm_cols(up, w_ref[0, 3]).astype(BF16)
    for index, cols in enumerate(heads_of(x_ref.shape[1])):
        own16, halo16 = p_own_ref[index], p_halo_ref[index]
        head_backward(
            cols, own16.astype(F32), halo16.astype(F32), own16, halo16,
            ga_ref, q_ref, k_ref, v_ref, k_h_ref, v_h_ref,
            gq_ref, gk_ref, gv_ref, gk_h_ref, gv_h_ref,
        )
    unit, _ = unit_of(x_ref[...])
    grads_out(
        0, unit, pair_ref, other_ref, w_ref, gq_ref, gk_ref, gv_ref, gk_h_ref, gv_h_ref,
        gn_ref, to_pair_ref, to_other_ref, cond_ref,
    )


def end_kernel(base, x_ref, up_ref, gn_ref, pair_ref, other_ref, film_ref, out_ref, total_ref):
    out_ref[...] = upstream_of(
        base, x_ref[...], up_ref[...], gn_ref, pair_ref, other_ref, film_ref, 0, total_ref
    )


def weight_products(
    normed_ref, normed_h_ref, attended_ref, up_ref, gq_ref, gk_ref, gv_ref, gk_h_ref, gv_h_ref, put
):
    put(0, mm_rows(normed_ref[...], gq_ref[...]))
    put(1, mm_rows(normed_ref[...], gk_ref[...]) + mm_rows(normed_h_ref[...], gk_h_ref[...]))
    put(2, mm_rows(normed_ref[...], gv_ref[...]) + mm_rows(normed_h_ref[...], gv_h_ref[...]))
    put(3, mm_rows(attended_ref[...], up_ref[...]))


def plain_weight_kernel(*refs):
    *ins, out_ref = refs

    def put(slot, value):
        out_ref[slot] = value

    weight_products(*ins, put)


def put_pair(value, out_ref):
    high = value.astype(BF16)
    rows = value.shape[0]
    out_ref[:rows, :] = high
    out_ref[rows:, :] = (value - high.astype(F32)).astype(BF16)


def get_pair(in_ref):
    rows = in_ref.shape[0] // 2
    return in_ref[:rows, :].astype(F32) + in_ref[rows:, :].astype(F32)


def get_noise(in_ref, start):
    parts = [in_ref[start + row : start + row + 1, :].astype(F32) for row in range(3)]
    return (parts[0] + parts[1]) + parts[2]


def put_noise(value, out_ref, start):
    for row in range(3):
        part = value.astype(BF16)
        out_ref[start + row : start + row + 1, :] = part
        value = value - part.astype(F32)


def split_weight_kernel(plan, layer, *refs):
    *ins, to_pair_ref, cond_ref, other_cond_ref, send_ref, keep_ref, film_ref, total_ref = refs

    def put(slot, value):
        total_ref[slot] = value

    weight_products(*ins, put)
    rows = plan.rows // 2
    ens, mesh = lax.axis_index("ens"), lax.axis_index("mesh")
    for slot in range(4):
        group, inner = slot // 2, slot % 2
        for core in range(2):
            for y in range(2):
                col = lax.bitwise_xor(mesh, y * 2 + core)
                cols = pl.ds(pl.multiple_of(col * LANES, LANES), LANES)
                for x in range(2):
                    for z in range(plan.deep):
                        row = lax.bitwise_xor(ens, z * 2 + x)
                        at = pl.ds(pl.multiple_of(row * rows, rows), rows)
                        piece = total_ref[slot, at, cols]
                        first, second = (y, x) if group == 0 else (x, y)
                        start = plan.at(group, first, second, z) + inner * rows
                        if core:
                            send_ref[start : start + rows, :] = piece.astype(BF16)
                        else:
                            keep_ref[start : start + rows, :] = piece
    rim, width = to_pair_ref.shape
    for block in range(width // LANES):
        start = plan.weights + block * rim
        send_ref[start : start + rim, :] = to_pair_ref[:, block * LANES : (block + 1) * LANES]
    if layer:
        return
    half = plan.film_rows // LAYERS
    for core in range(2):
        for y in range(2):
            col = lax.bitwise_xor(mesh, y * 2 + core) * (half * LANES)
            rows = []
            for ref in (cond_ref, other_cond_ref):
                for part in range(half):
                    start = pl.multiple_of(col + part * LANES, LANES)
                    rows.append(ref[:, pl.ds(start, LANES)])
            for index, row in enumerate(rows):
                film_ref[y, core, index : index + 1, :] = row
    for y in range(2):
        start = plan.weights + plan.halo + y * plan.film
        put_pair(film_ref[y, 1], send_ref.at[start : start + 2 * plan.film_rows, :])


def stage_one(plan, keep_ref, came_ref, y_ref, x_ref, kept_ref):
    size = plan.weights // 4
    for group, out_ref in ((0, y_ref), (1, x_ref)):
        start = 2 * group * size
        kept_ref[group * size : (group + 1) * size, :] = keep_ref[
            start : start + size, :
        ] + came_ref[start : start + size, :].astype(F32)
        start += size
        out_ref[:size, :] = (
            keep_ref[start : start + size, :] + came_ref[start : start + size, :].astype(F32)
        ).astype(BF16)


def stage_two(plan, kept_ref, y_ref, x_ref, y_base, x_base, to_x_ref, to_y_ref, next_ref):
    size = plan.weights // 8
    for group, in_ref, base, out_ref in ((0, y_ref, y_base, to_x_ref), (1, x_ref, x_base, to_y_ref)):
        start = 2 * group * size
        next_ref[group * size : (group + 1) * size, :] = kept_ref[
            start : start + size, :
        ] + in_ref[base : base + size, :].astype(F32)
        out_ref[...] = (
            kept_ref[start + size : start + 2 * size, :]
            + in_ref[base + size : base + 2 * size, :].astype(F32)
        ).astype(BF16)


def stage_three(plan, kept_ref, x_ref, y_ref, x_base, y_base, z_refs, last_ref):
    rows = plan.rows
    for group, in_ref, base in ((0, x_ref, x_base), (1, y_ref, y_base)):
        for z in range(plan.deep):
            start = (group * plan.deep + z) * rows
            value = kept_ref[start : start + rows, :] + in_ref[
                base + z * rows : base + (z + 1) * rows, :
            ].astype(F32)
            if z:
                z_refs[z - 1][group * rows : (group + 1) * rows, :] = value.astype(BF16)
            else:
                last_ref[group * rows : (group + 1) * rows, :] = value


def start_scatter_kernel(plan, keep_ref, came_ref, y_ref, x_ref, kept_ref):
    stage_one(plan, keep_ref, came_ref, y_ref, x_ref, kept_ref)


def slot_a_kernel(
    plan, keep1_ref, film1_ref, came1_ref, kept2_ref, y2_ref, x2_ref,
    y_ref, x_ref, kept1_ref, next2_ref, film_ref,
):
    size, small = plan.weights // 4, plan.weights // 8
    stage_one(plan, keep1_ref, came1_ref, y_ref, x_ref, kept1_ref)
    stage_two(
        plan, kept2_ref, y2_ref, x2_ref, 0, 0,
        x_ref.at[size : size + small, :], y_ref.at[size : size + small, :], next2_ref,
    )
    start, end = plan.weights + plan.halo, 2 * plan.film_rows
    film_ref[...] = film1_ref[0, 0] + get_pair(came1_ref.at[start : start + end, :])
    start += plan.film
    put_pair(
        film1_ref[1, 0] + get_pair(came1_ref.at[start : start + end, :]),
        y_ref.at[size + small : size + small + end, :],
    )


def slot_b_kernel(
    plan, kept1_ref, kept2_ref, film_ref, y_ref, x_ref, noise_ref, *outs,
):
    to_x_ref, to_y_ref, next1_ref, last2_ref, *z_refs = outs
    size, small = plan.weights // 4, plan.weights // 8
    stage_two(
        plan, kept1_ref, y_ref, x_ref, 0, 0, to_x_ref.at[:small, :], to_y_ref.at[:small, :], next1_ref
    )
    stage_three(plan, kept2_ref, x_ref, y_ref, size, size, z_refs, last2_ref)
    end = 2 * plan.film_rows
    start = size + small
    total = film_ref[...] + get_pair(y_ref.at[start : start + end, :])
    put_pair(total, to_x_ref.at[small : small + end, :])
    put_noise(jnp.full((1, LANES), noise_ref[0], F32), to_x_ref, small + end)


def slot_c_kernel(plan, kept1_ref, x_ref, y_ref, mine_ref, *outs):
    last1_ref, *z_refs = outs
    stage_three(plan, kept1_ref, x_ref, y_ref, 0, 0, z_refs, last1_ref)
    small, end = plan.weights // 8, 2 * plan.rows
    for z_ref in z_refs:
        z_ref[end : end + plan.film, :] = mine_ref[small : small + plan.film, :]
        z_ref[end + plan.film :, :] = x_ref[small : small + plan.film, :]


def finish_kernel(plan, last1_ref, last2_ref, mine_ref, x_ref, *refs):
    count = plan.deep - 1
    z1_refs, z2_refs, (out_ref, film_ref) = refs[:count], refs[count : 2 * count], refs[2 * count :]
    for layer, (last_ref, z_refs) in enumerate(((last1_ref, z1_refs), (last2_ref, z2_refs))):
        rows = plan.rows // 2
        for slot in range(4):
            at = slice(slot * rows, (slot + 1) * rows)
            total = last_ref[at, :]
            for z_ref in z_refs:
                total = total + z_ref[at, :].astype(F32)
            out_ref[layer, slot] = total
    small, end = plan.weights // 8, 2 * plan.rows
    packs = [ref.at[small : small + plan.film, :] for ref in (mine_ref, x_ref)]
    for z_ref in z1_refs:
        packs += [z_ref.at[end + i * plan.film : end + (i + 1) * plan.film, :] for i in range(2)]
    lane = lax.broadcasted_iota(jnp.int32, (1, LANES), 1)
    noise = jnp.ones((1, LANES), F32)
    pair = 2 * plan.film_rows
    for member, pack in enumerate(packs):
        noise = jnp.where(lane == member, get_noise(pack, pair), noise)
    embedding = embedding_of(jnp.broadcast_to(noise, (2 * NOISE_FREQ, LANES)))
    members = [get_pair(pack.at[:pair, :]) for pack in packs]
    half = plan.film_rows // LAYERS
    for layer in range(LAYERS):
        for part in range(half):
            row = layer * half + part
            total = jnp.zeros((2 * NOISE_FREQ, LANES), F32)
            for member, value in enumerate(members):
                total += embedding[:, member : member + 1] * value[row : row + 1, :]
            film_ref[layer, :, part * LANES : (part + 1) * LANES] = total


def film_kernel(rows_ref, out_ref):
    members, _, columns = rows_ref.shape
    rows = rows_ref[...]
    lane = lax.broadcasted_iota(jnp.int32, (1, LANES), 1)
    noise = jnp.ones((1, LANES), F32)
    for member in range(members):
        noise = jnp.where(lane == member, rows[member, LAYERS:, :1], noise)
    embedding = embedding_of(jnp.broadcast_to(noise, (2 * NOISE_FREQ, LANES)))
    for layer in range(LAYERS):
        total = jnp.zeros((2 * NOISE_FREQ, columns), F32)
        for member in range(members):
            total += embedding[:, member : member + 1] * rows[member, layer : layer + 1, :]
        out_ref[layer] = total


def whole():
    return pl.BlockSpec(memory_space=pltpu.VMEM)


def apart():
    return pl.BlockSpec(memory_space=pltpu.HBM)


def call(kernel, args, outs, scratch=(), flops=0, specs=None, limit=10 << 20, sems=()):
    moved = sum(a.size * a.dtype.itemsize for a in args)
    moved += sum(math.prod(shape) * jnp.dtype(kind).itemsize for shape, kind in outs)
    return pl.pallas_call(
        kernel,
        out_shape=[jax.ShapeDtypeStruct(shape, kind) for shape, kind in outs],
        in_specs=specs or [whole() for _ in args],
        out_specs=[whole() for _ in outs],
        scratch_shapes=[pltpu.VMEM(shape, kind) for shape, kind in scratch] + list(sems),
        compiler_params=pltpu.CompilerParams(vmem_limit_bytes=limit),
        cost_estimate=pl.CostEstimate(flops=flops, bytes_accessed=moved, transcendentals=0),
    )(*args)


def swap(block, axis, bit):
    count = lax.axis_size(axis)
    return lax.ppermute(block, axis, [(i, i ^ bit) for i in range(count)])


def exchange_other(to_other):
    count = lax.axis_size("mesh")
    route = []
    for i in range(1, count - 1, 2):
        route += [(i, i + 1), (i + 1, i)]
    return lax.ppermute(to_other, "mesh", route)


def exchange(to_pair, to_other):
    other = exchange_other(to_other)
    return swap(to_pair, "mesh", 1), other


class Plan:
    def __init__(self, width, rim, ens_count, mesh_count):
        self.deep = ens_count // 2
        self.rows = 2 * width // ens_count
        self.weights = 8 * self.deep * self.rows
        self.halo = rim * width // LANES
        self.film_rows = LAYERS * (2 * width // mesh_count) // LANES
        self.film = 16 * pl.cdiv(2 * self.film_rows + 3, 16)

    def at(self, group, first, second, z):
        return (((group * 2 + first) * 2 + second) * self.deep + z) * self.rows


def film_pieces(conds, noise_level, mesh_count):
    mesh = lax.axis_index("mesh")
    rows = jnp.concatenate(conds, axis=0)
    width = rows.shape[1] // mesh_count
    pieces = rows.reshape(LAYERS, mesh_count, width).transpose(1, 0, 2)
    pieces = jnp.take(pieces, lax.bitwise_xor(jnp.arange(mesh_count), mesh), axis=0)
    noise = jnp.where(jnp.arange(mesh_count) == 0, noise_level[0], 0.0)
    noise = jnp.broadcast_to(noise[:, None, None], (mesh_count, 1, width))
    return jnp.concatenate([pieces, noise], axis=1)


def film_mesh_step(pieces, bit):
    pieces = pieces.reshape(-1, 2, *pieces.shape[1:])
    return pieces[:, 0] + swap(pieces[:, 1], "mesh", bit)


def film_ens_step(rows, bit):
    return jnp.concatenate([rows, swap(rows, "ens", bit)])


def film_end(rows):
    shape = (LAYERS, 2 * NOISE_FREQ, rows.shape[2])
    return call(film_kernel, (rows,), [(shape, F32)])[0]


def bits_of(count):
    return [1 << index for index in range(count.bit_length() - 1)]


def body(inputs, cotangent, noise_level, neighbours, live_slots, projections, film_weights):
    states, cot = inputs[0], cotangent[0]
    nodes, width = states.shape
    rim = nodes // 2
    mesh_count, ens_count = lax.axis_size("mesh"), lax.axis_size("ens")
    parity = lax.rem(lax.axis_index("mesh"), 2)
    square = 2 * nodes * width * width
    mesh_split = width // mesh_count
    split = mesh_count == 4 and mesh_split % LANES == 0 and ens_count % 2 == 0

    def full(kind=BF16):
        return ((nodes, width), kind)

    rims = [((rim, width), BF16)] * 2
    cond_shape = ((1, 2 * width), F32)
    pair1, other1 = exchange(
        lax.dynamic_slice_in_dim(states, (1 - parity) * rim, rim),
        lax.dynamic_slice_in_dim(states, parity * rim, rim),
    )
    slots = neighbours.shape[1]
    film, bias_own, bias_halo, normed1, q1, k1, v1, projections = call(
        start_kernel,
        (*(pltpu.with_memory_space_constraint(a, pltpu.HBM)
           for a in (states, neighbours.T, live_slots.T)), noise_level,
         *(pltpu.with_memory_space_constraint(a, pltpu.HBM)
           for a in (film_weights, projections))),
        [((LAYERS, 2 * width), F32), ((nodes, nodes), F32), ((nodes, nodes), F32)] + [full()] * 4
        + [(projections.shape, BF16)],
        scratch=[full(), ((slots, nodes), jnp.int32), ((slots, nodes), jnp.int32),
                 (film_weights.shape, F32), (neighbours.shape, jnp.int32)],
        sems=[pltpu.SemaphoreType.DMA((5,))], flops=3 * square,
        specs=[apart()] * 3 + [pl.BlockSpec(memory_space=pltpu.SMEM)] + [apart()] * 2,
    )
    probs_shape = ((HEADS, nodes, nodes), BF16)
    states2, to_pair, to_other, normed1_h, k1_h, v1_h, p_own, p_halo, attended1 = call(
        forward_kernel,
        (states, pair1, other1, film, q1, k1, v1, bias_own, bias_halo, projections),
        [full()] + rims + [full()] * 3 + [probs_shape] * 2 + [full()],
        flops=5 * square,
    )
    pair2, other2 = exchange(to_pair, to_other)
    normed2, q2, k2, v2, ga2 = call(
        own_kernel, (states2, cot, film, projections), [full()] * 5, flops=4 * square
    )
    grads = [full()] * 5 + [full(F32)] + rims + [cond_shape]
    normed2_h, attended2, gq2, gk2, gv2, gk2_h, gv2_h, gn2, to_pair, to_other, cond2 = call(
        last_layer_kernel,
        (states2, pair2, other2, film, q2, k2, v2, ga2, bias_own, bias_halo, projections),
        [full()] * 2 + grads,
        scratch=[full()] * 2, flops=14 * square,
    )
    plan = Plan(width, rim, ens_count, mesh_count) if split else None
    base = plan.weights if split else None
    sums = plan.weights if split else 0

    def block(rows, kind=BF16):
        return ((rows, LANES), kind)

    def weight_grads(layer, to_pair, conds, *args):
        if not split:
            out = call(plain_weight_kernel, args, [((4, width, width), F32)], flops=6 * square)
            return out[0], None, None
        film_shape = (2, 2, plan.film_rows, LANES)
        return call(
            functools.partial(split_weight_kernel, plan, layer), args + (to_pair,) + conds,
            [block(sums + plan.halo + 2 * plan.film), block(sums, F32), (film_shape, F32)],
            scratch=[((4, width, width), F32)], flops=6 * square,
        )

    back_other = exchange_other(to_other)
    weights2, keep2, _ = weight_grads(
        1, to_pair, (cond2, cond2),
        normed2, normed2_h, attended2, cot, gq2, gk2, gv2, gk2_h, gv2_h,
    )
    if split:
        back_pair = swap(weights2, "mesh", 1)
        to_y, to_x, kept2 = call(
            functools.partial(start_scatter_kernel, plan), (keep2, back_pair),
            [block(sums // 4)] * 2 + [block(sums // 2, F32)],
        )
        y2, x2 = swap(to_y, "mesh", 2), swap(to_x, "ens", 1)
    else:
        back_pair = swap(to_pair, "mesh", 1)
    up, gq1, gk1, gv1, gk1_h, gv1_h, gn1, to_pair, to_other, cond1 = call(
        functools.partial(first_layer_kernel, base),
        (states2, cot, gn2, back_pair, back_other, film,
         states, pair1, other1, q1, k1, v1, k1_h, v1_h, p_own, p_halo, projections),
        [full()] + grads,
        scratch=[full(F32), full()], flops=11 * square,
    )
    back_other = exchange_other(to_other)
    weights1, keep1, rows1 = weight_grads(
        0, to_pair, (cond1, cond2),
        normed1, normed1_h, attended1, up, gq1, gk1, gv1, gk1_h, gv1_h,
    )
    back_pair = swap(weights1 if split else to_pair, "mesh", 1)
    grad_input = call(
        functools.partial(end_kernel, base),
        (states, up, gn1, back_pair, back_other, film), [full()],
        scratch=[full(F32)],
    )[0]
    if split:
        to_y, to_x, kept1, kept2, film_mine = call(
            functools.partial(slot_a_kernel, plan),
            (keep1, rows1, back_pair, kept2, y2, x2),
            [block(sums // 4 + sums // 8 + plan.film), block(sums // 4 + sums // 8),
             block(sums // 2, F32), block(sums // 4, F32), block(plan.film_rows, F32)],
        )
        came_y, came_x = swap(to_y, "mesh", 2), swap(to_x, "ens", 1)
        others = range(1, plan.deep)
        to_x, to_y, kept1, last2, *to_z = call(
            functools.partial(slot_b_kernel, plan),
            (kept1, kept2, film_mine, came_y, came_x, noise_level),
            [block(sums // 8 + plan.film), block(sums // 8), block(sums // 4, F32),
             block(2 * plan.rows, F32)] + [block(2 * plan.rows) for _ in others],
            specs=[whole()] * 5 + [pl.BlockSpec(memory_space=pltpu.SMEM)],
        )
        came_x, came_y = swap(to_x, "ens", 1), swap(to_y, "mesh", 2)
        came_z2 = [swap(to_z[z - 1], "ens", 2 * z) for z in others]
        last1, *to_z = call(
            functools.partial(slot_c_kernel, plan), (kept1, came_x, came_y, to_x),
            [block(2 * plan.rows, F32)] + [block(2 * plan.rows + 2 * plan.film) for _ in others],
        )
        came_z1 = [swap(to_z[z - 1], "ens", 2 * z) for z in others]
        weight_out, film_out = call(
            functools.partial(finish_kernel, plan),
            (last1, last2, to_x, came_x, *came_z1, *came_z2),
            [((LAYERS, 4, width // ens_count, LANES), F32),
             ((LAYERS, 2 * NOISE_FREQ, 2 * width // mesh_count), F32)],
        )
    else:
        film_rows = film_pieces((cond1, cond2), noise_level, mesh_count)
        for bit in bits_of(mesh_count):
            film_rows = film_mesh_step(film_rows, bit)
        for bit in bits_of(ens_count):
            film_rows = film_ens_step(film_rows, bit)
        film_out = film_end(film_rows)
        part = jnp.stack([weights1, weights2]).astype(BF16)
        part = lax.psum_scatter(part, "ens", scatter_dimension=2, tiled=True)
        weight_out = lax.psum_scatter(part, "mesh", scatter_dimension=3, tiled=True).astype(F32)
    return (grad_input[None], weight_out, film_out)


def solution(mesh):
    placed = (
        P("ens", "mesh", None),
        P("ens", "mesh", None),
        P("ens"),
        P("mesh", None),
        P("mesh", None),
        P(),
        P(),
    )
    return jax.shard_map(
        body,
        mesh=mesh,
        in_specs=placed,
        out_specs=(P("ens", "mesh", None), P(None, None, "ens", "mesh"), P(None, None, "mesh")),
        check_vma=False,
    )
```

```python
import functools
import math

import jax
import jax.numpy as jnp
from jax import lax
from jax.experimental import pallas as pl
from jax.experimental.pallas import tpu as pltpu
from jax.sharding import PartitionSpec as P


HEADS = 4
NOISE_FREQ = 16
LAYERS = 2
LANES = 128

epsilon = 1e-05
F32 = jnp.float32
BF16 = jnp.bfloat16
ABSENT = -1e30


def mm(left_side, right_side):
    return jnp.dot(left_side, right_side, preferred_element_type=F32)


def mm_rows(left_side, right_side):
    return lax.dot_general(
        left_side, right_side, (((0,), (0,)), ((), ())), preferred_element_type=F32
    )


def mm_cols(left_side, right_side):
    return lax.dot_general(
        left_side, right_side, (((1,), (1,)), ((), ())), preferred_element_type=F32
    )


def unit_of(states):
    values = states.astype(F32)
    centre = jnp.mean(values, axis=1, keepdims=True)
    centred = values - centre
    inverse = lax.rsqrt(jnp.mean(jnp.square(centred), axis=1, keepdims=True) + epsilon)
    return centred * inverse, inverse


def normed_of(states, film_ref, layer):
    width = states.shape[1]
    unit, _ = unit_of(states)
    scale = film_ref[layer : layer + 1, :width]
    shift = film_ref[layer : layer + 1, width:]
    return (unit * (1.0 + scale) + shift).astype(BF16)


def embedding_of(noise):
    row = lax.broadcasted_iota(jnp.int32, noise.shape, 0)
    wave = row - jnp.where(row >= NOISE_FREQ, NOISE_FREQ, 0) + 1
    angle = jnp.log(noise) * wave.astype(F32)
    return jnp.where(row < NOISE_FREQ, jnp.sin(angle), jnp.cos(angle))


def project_own(normed, w_ref, layer):
    return [mm(normed, w_ref[layer, slot]).astype(BF16) for slot in range(3)]


def put_all(refs, values):
    for ref, value in zip(refs, values, strict=True):
        ref[...] = value


def side_by_side(parts):
    return jnp.concatenate(parts, axis=1)


def halves(parity, rim):
    return parity * rim, (1 - parity) * rim


def half_rows(ref, parity, half):
    rim = ref.shape[0] // 2
    return pl.ds(pl.multiple_of(halves(parity, rim)[half], rim), rim)


def start_kernel(
    x_o_ref, x_p_ref, near_hbm, live_hbm, noise_ref, film_w_hbm, w_hbm,
    film_ref, bias_o_ref, bias_p_ref, normed_ref, q_ref, k_ref, v_ref, w_ref,
    near_ref, live_ref, film_w_ref, near_t_ref, sems,
):
    copies = [
        pltpu.make_async_copy(near_hbm, near_ref, sems.at[0]),
        pltpu.make_async_copy(live_hbm, live_ref, sems.at[1]),
        pltpu.make_async_copy(film_w_hbm, film_w_ref, sems.at[2]),
        pltpu.make_async_copy(w_hbm.at[0], w_ref.at[0], sems.at[3]),
        pltpu.make_async_copy(w_hbm.at[1:], w_ref.at[1:], sems.at[4]),
    ]
    for copy in copies:
        copy.start()
    slots, node_count = near_ref.shape
    rim = node_count // 2
    place = lax.axis_index("mesh")
    parity = lax.rem(place, 2)
    embedding = embedding_of(jnp.full((2 * NOISE_FREQ, 1), noise_ref[0], F32))
    copies[2].wait()
    for layer in range(LAYERS):
        film_ref[layer : layer + 1, :] = jnp.sum(
            embedding * film_w_ref[layer], axis=0, keepdims=True
        )
    normed_ref[:rim, :] = normed_of(x_o_ref[...], film_ref, 0)
    normed_ref[rim:, :] = normed_of(x_p_ref[...], film_ref, 0)
    copies[0].wait()
    copies[1].wait()
    near_ref[...] = jnp.where(
        live_ref[...] > 0, near_ref[...] - place * node_count, -(1 << 24)
    )
    column = lax.broadcasted_iota(jnp.int32, (1, 3 * rim), 1)
    side_o, side_p = halves(parity, rim)
    own = jnp.where(column < rim, column + side_o, column - rim + side_p)
    halo_o = column - 2 * rim + jnp.where(parity == 0, -rim, node_count)
    halo_p = column - 2 * rim + jnp.where(parity == 0, node_count, -rim)
    ids_o = jnp.where(column < node_count, own, halo_o)
    ids_p = jnp.where(column < node_count, own, halo_p)
    step = 32
    for side, ids, out_ref in ((side_o, ids_o, bias_o_ref), (side_p, ids_p, bias_p_ref)):
        near_t_ref[...] = near_ref[:, pl.ds(pl.multiple_of(side, rim), rim)].T

        def rows(index, carry, ids=ids, out_ref=out_ref):
            start = pl.multiple_of(index * step, step)
            near = near_t_ref[pl.ds(start, step), :]
            bias = jnp.full((step, 3 * rim), ABSENT, F32)
            for slot in range(slots):
                bias = jnp.where(near[:, slot : slot + 1] == ids, 0.0, bias)
            out_ref[pl.ds(start, step), :] = bias
            return carry

        lax.fori_loop(0, rim // step, rows, 0)
    copies[3].wait()
    put_all((q_ref, k_ref, v_ref), project_own(normed_ref[...], w_ref, 0))
    copies[4].wait()


def own_kernel(
    x_o_ref, x_p_ref, cot_ref, film_ref, w_ref, normed_ref, q_ref, k_ref, v_ref, ga_ref, cot2_ref
):
    parity = lax.rem(lax.axis_index("mesh"), 2)
    cot = jnp.concatenate([cot_ref[half_rows(cot_ref, parity, half), :] for half in range(2)])
    normed = normed_of(stacked(x_o_ref, x_p_ref), film_ref, 1)
    projected = project_own(normed, w_ref, 1)
    grad = mm_cols(cot, w_ref[1, 3]).astype(BF16)
    put_all((normed_ref, q_ref, k_ref, v_ref, ga_ref, cot2_ref), (normed, *projected, grad, cot))


def project_halo(halo_ref, film_ref, w_ref, layer):
    normed = normed_of(halo_ref[...], film_ref, layer)
    key = mm(normed, w_ref[layer, 1]).astype(BF16)
    value = mm(normed, w_ref[layer, 2]).astype(BF16)
    return normed, key, value


def weigh(scores, scores_h, bias, head):
    factor = 1.0 / math.sqrt(head)
    split = scores.shape[1]
    scores = scores * factor + bias[:, :split]
    scores_h = scores_h * factor + bias[:, split:]
    peak = jnp.maximum(
        jnp.max(scores, axis=1, keepdims=True), jnp.max(scores_h, axis=1, keepdims=True)
    )
    own, halo = jnp.exp(scores - peak), jnp.exp(scores_h - peak)
    total = jnp.sum(own, axis=1, keepdims=True) + jnp.sum(halo, axis=1, keepdims=True)
    return own, halo, 1.0 / total


def heads_of(width):
    head = width // HEADS
    return [slice(index * head, (index + 1) * head) for index in range(HEADS)]


def forward_kernel(
    half, x_ref, halo_ref, film_ref, q_ref, k_ref, v_ref, bias_ref, w_ref,
    next_ref, normed_h_ref, k_h_ref, v_h_ref, p_own_ref, p_halo_ref, attended_ref,
):
    rim, width = x_ref.shape
    rows = slice(half * rim, (half + 1) * rim)
    query, key, value, bias = q_ref[rows, :], k_ref[...], v_ref[...], bias_ref[...]
    heads = heads_of(width)
    scores = [mm_cols(query[:, cols], key[:, cols]) for cols in heads]
    normed, key_h, value_h = project_halo(halo_ref, film_ref, w_ref, 0)
    scores_h = [mm_cols(query[:, cols], key_h[:, cols]) for cols in heads]
    shares, parts = [], []
    for index, cols in enumerate(heads):
        own, halo, share = weigh(scores[index], scores_h[index], bias, width // HEADS)
        own, halo = (own * share).astype(BF16), (halo * share).astype(BF16)
        shares.append((own, halo))
        parts.append((mm(own, value[:, cols]) + mm(halo, value_h[:, cols])).astype(BF16))
    attended = side_by_side(parts)
    states = (x_ref[...].astype(F32) + mm(attended, w_ref[0, 3])).astype(BF16)
    put_all(
        (next_ref, normed_h_ref, k_h_ref, v_h_ref, attended_ref),
        (states, normed, key_h, value_h, attended),
    )
    for index, (own, halo) in enumerate(shares):
        p_own_ref[index] = own
        p_halo_ref[index] = halo


def head_backward(own, halo, own16, halo16, probs, probs_h, share, grad, query, key, key_h):
    middle = jnp.sum(own * probs, axis=1, keepdims=True) + jnp.sum(
        halo * probs_h, axis=1, keepdims=True
    )
    factor = 1.0 / math.sqrt(query.shape[1])
    if share is not None:
        middle, factor = middle * share, share * factor
    scores = (own * ((probs - middle) * factor)).astype(BF16)
    scores_h = (halo * ((probs_h - middle) * factor)).astype(BF16)
    return (
        (mm(scores, key) + mm(scores_h, key_h)).astype(BF16),
        mm_rows(scores, query),
        mm_rows(own16, grad),
        mm_rows(scores_h, query).astype(BF16),
        mm_rows(halo16, grad).astype(BF16),
    )


def joined(parts, before, kind):
    gq, gk, gv, gk_h, gv_h = [side_by_side(part) for part in zip(*parts, strict=True)]
    if before:
        gk, gv = gk + before[0][...], gv + before[1][...]
    return gq, gk.astype(kind), gv.astype(kind), gk_h, gv_h


def last_layer_kernel(half, halo_ref, film_ref, q_ref, k_ref, v_ref, ga_ref, bias_ref, w_ref, *refs):
    before = refs[:2] if half == 0 else ()
    normed_h_ref, attended_ref, *outs = refs[len(before) :]
    rim, width = halo_ref.shape
    rows = slice(half * rim, (half + 1) * rim)
    query, key, value, bias = q_ref[rows, :], k_ref[...], v_ref[...], bias_ref[...]
    grad = ga_ref[rows, :]
    heads = heads_of(width)
    scores = [mm_cols(query[:, cols], key[:, cols]) for cols in heads]
    probs = [mm_cols(grad[:, cols], value[:, cols]) for cols in heads]
    normed, key_h, value_h = project_halo(halo_ref, film_ref, w_ref, 1)
    scores_h = [mm_cols(query[:, cols], key_h[:, cols]) for cols in heads]
    probs_h = [mm_cols(grad[:, cols], value_h[:, cols]) for cols in heads]
    attended, parts = [], []
    for index, cols in enumerate(heads):
        own, halo, share = weigh(scores[index], scores_h[index], bias, width // HEADS)
        own16, halo16 = (own * share).astype(BF16), (halo * share).astype(BF16)
        attended.append((mm(own16, value[:, cols]) + mm(halo16, value_h[:, cols])).astype(BF16))
        parts.append(
            head_backward(
                own, halo, own16, halo16, probs[index], probs_h[index], share,
                grad[:, cols], query[:, cols], key[:, cols], key_h[:, cols],
            )
        )
    results = joined(parts, before, outs[1].dtype)
    if half == 0:
        results += (halo_grads(w_ref, 1, *results[3:]).astype(BF16),)
    put_all((normed_h_ref, attended_ref, *outs), (normed, side_by_side(attended), *results))


def halo_grads(w_ref, layer, gk_h, gv_h):
    return mm_cols(gk_h, w_ref[layer, 1]) + mm_cols(gv_h, w_ref[layer, 2])


def grads_kernel(
    plan, layer, x_o_ref, x_p_ref, halo_o_ref, halo_p_ref, gq_o_ref, gq_p_ref, gk_ref, gv_ref,
    gk_h_ref, gv_h_ref, to_other_ref, w_ref, cond2_ref, gn_ref, to_pair_ref, cond_ref, *film_refs,
):
    rim, width = x_o_ref.shape
    grad_p = halo_grads(w_ref, layer, gk_h_ref[...], gv_h_ref[...])
    grad_own = mm_cols(gk_ref[...], w_ref[layer, 1]) + mm_cols(gv_ref[...], w_ref[layer, 2])
    grads = [to_other_ref[...].astype(F32), grad_p]
    for half, gq_ref in enumerate((gq_o_ref, gq_p_ref)):
        rows = slice(half * rim, (half + 1) * rim)
        grads.append(mm_cols(gq_ref[...], w_ref[layer, 0]) + grad_own[rows])
    scaled = jnp.zeros((1, width), F32)
    plain = jnp.zeros((1, width), F32)
    for grad, ref in zip(grads, (halo_o_ref, halo_p_ref, x_o_ref, x_p_ref)):
        scaled += jnp.sum(grad * unit_of(ref[...])[0], axis=0, keepdims=True)
        plain += jnp.sum(grad, axis=0, keepdims=True)
    to_pair_ref[...] = grad_p.astype(BF16)
    gn_ref[:rim, :], gn_ref[rim:, :] = grads[2:]
    cond_ref[:, :width] = scaled
    cond_ref[:, width:] = plain
    if not film_refs:
        return
    keep_ref, send_ref, scratch_ref = film_refs
    part_rows = plan.film_rows // LAYERS
    mesh = lax.axis_index("mesh")
    for core in range(2):
        for y in range(2):
            col = lax.bitwise_xor(mesh, y * 2 + core) * (part_rows * LANES)
            for layer_index, ref in enumerate((cond_ref, cond2_ref)):
                for part in range(part_rows):
                    start = pl.multiple_of(col + part * LANES, LANES)
                    row = layer_index * part_rows + part
                    out_ref = scratch_ref if core else keep_ref
                    out_ref[y, row : row + 1, :] = ref[:, pl.ds(start, LANES)]
    for y in range(2):
        put_pair(
            scratch_ref[y], send_ref.at[y * plan.film : y * plan.film + 2 * plan.film_rows, :]
        )


def upstream_of(states, up, grad, film_ref, layer):
    width = states.shape[1]
    unit, inverse = unit_of(states)
    grad = grad * (1.0 + film_ref[layer : layer + 1, :width])
    centred = (
        grad
        - jnp.mean(grad, axis=1, keepdims=True)
        - unit * jnp.mean(grad * unit, axis=1, keepdims=True)
    )
    return (up.astype(F32) + inverse * centred).astype(BF16)


def first_layer_kernel(
    half, next_ref, cot_ref, gn2_ref, back_ref, film_ref, q_ref, k_ref, v_ref, k_h_ref, v_h_ref,
    p_own_ref, p_halo_ref, w_ref, *refs,
):
    before = refs[:2] if half == 0 else ()
    up_ref, *outs = refs[len(before) :]
    rim, width = next_ref.shape
    rows = slice(half * rim, (half + 1) * rim)
    total = gn2_ref[rows, :] + back_ref[...].astype(F32)
    up = upstream_of(next_ref[...], cot_ref[rows, :], total, film_ref, 1)
    grad = mm_cols(up, w_ref[0, 3]).astype(BF16)
    query, key, value = q_ref[rows, :], k_ref[...], v_ref[...]
    key_h, value_h = k_h_ref[...], v_h_ref[...]
    heads = heads_of(width)
    probs = [mm_cols(grad[:, cols], value[:, cols]) for cols in heads]
    probs_h = [mm_cols(grad[:, cols], value_h[:, cols]) for cols in heads]
    parts = []
    for index, cols in enumerate(heads):
        own16, halo16 = p_own_ref[index], p_halo_ref[index]
        parts.append(
            head_backward(
                own16.astype(F32), halo16.astype(F32), own16, halo16, probs[index], probs_h[index],
                None, grad[:, cols], query[:, cols], key[:, cols], key_h[:, cols],
            )
        )
    results = joined(parts, before, outs[1].dtype)
    if half == 0:
        results += (halo_grads(w_ref, 0, *results[3:]).astype(BF16),)
    put_all((up_ref, *outs), (up, *results))


def end_kernel(
    x_o_ref, x_p_ref, up_o_ref, up_p_ref, gn_ref, back_o_ref, back_p_ref, film_ref, out_ref
):
    parity = lax.rem(lax.axis_index("mesh"), 2)
    rim = x_o_ref.shape[0]
    total = gn_ref[...] + stacked(back_o_ref, back_p_ref).astype(F32)
    grad = upstream_of(stacked(x_o_ref, x_p_ref), stacked(up_o_ref, up_p_ref), total, film_ref, 0)
    for half in range(2):
        out_ref[half_rows(out_ref, parity, half), :] = grad[half * rim : (half + 1) * rim]


def stacked(*refs):
    return jnp.concatenate([ref[...] for ref in refs], axis=0)


def weight_products(
    normed_ref, normed_o_ref, normed_p_ref, attended_o_ref, attended_p_ref, up_o_ref, up_p_ref,
    gq_o_ref, gq_p_ref, gk_ref, gk_o_ref, gk_p_ref, gv_ref, gv_o_ref, gv_p_ref, put,
):
    put(3, mm_rows(stacked(attended_o_ref, attended_p_ref), stacked(up_o_ref, up_p_ref)))
    put(0, mm_rows(normed_ref[...], stacked(gq_o_ref, gq_p_ref)))
    normed = stacked(normed_ref, normed_o_ref, normed_p_ref)
    put(1, mm_rows(normed, stacked(gk_ref, gk_o_ref, gk_p_ref)))
    put(2, mm_rows(normed, stacked(gv_ref, gv_o_ref, gv_p_ref)))


def plain_weight_kernel(*refs):
    *ins, out_ref = refs

    def put(slot, value):
        out_ref[slot] = value

    weight_products(*ins, put)


def put_pair(value, out_ref):
    high = value.astype(BF16)
    rows = value.shape[0]
    out_ref[:rows, :] = high
    out_ref[rows:, :] = (value - high.astype(F32)).astype(BF16)


def get_pair(in_ref):
    rows = in_ref.shape[0] // 2
    return in_ref[:rows, :].astype(F32) + in_ref[rows:, :].astype(F32)


def get_noise(in_ref, start):
    parts = [in_ref[start + row : start + row + 1, :].astype(F32) for row in range(3)]
    return (parts[0] + parts[1]) + parts[2]


def put_noise(value, out_ref, start):
    for row in range(3):
        part = value.astype(BF16)
        out_ref[start + row : start + row + 1, :] = part
        value = value - part.astype(F32)


def split_weight_kernel(plan, *refs):
    *ins, send_ref, keep_ref, total_ref = refs

    def put(slot, value):
        total_ref[slot] = value

    weight_products(*ins, put)
    rows = plan.rows // 2
    ens, mesh = lax.axis_index("ens"), lax.axis_index("mesh")
    for slot in range(4):
        group, inner = slot // 2, slot % 2
        for core in range(2):
            for y in range(2):
                col = lax.bitwise_xor(mesh, y * 2 + core)
                cols = pl.ds(pl.multiple_of(col * LANES, LANES), LANES)
                for x in range(2):
                    for z in range(plan.deep):
                        row = lax.bitwise_xor(ens, z * 2 + x)
                        at = pl.ds(pl.multiple_of(row * rows, rows), rows)
                        piece = total_ref[slot, at, cols]
                        first, second = (y, x) if group == 0 else (x, y)
                        start = plan.at(group, first, second, z) + inner * rows
                        if core:
                            send_ref[start : start + rows, :] = piece.astype(BF16)
                        else:
                            keep_ref[start : start + rows, :] = piece


def stage_one(plan, keep_ref, came_ref, y_ref, x_ref, kept_ref):
    size = plan.weights // 4
    for group, out_ref in ((0, y_ref), (1, x_ref)):
        start = 2 * group * size
        kept_ref[group * size : (group + 1) * size, :] = keep_ref[
            start : start + size, :
        ] + came_ref[start : start + size, :].astype(F32)
        start += size
        out_ref[:size, :] = (
            keep_ref[start : start + size, :] + came_ref[start : start + size, :].astype(F32)
        ).astype(BF16)


def stage_two(plan, kept_ref, y_ref, x_ref, y_base, x_base, to_x_ref, to_y_ref, next_ref):
    size = plan.weights // 8
    for group, in_ref, base, out_ref in ((0, y_ref, y_base, to_x_ref), (1, x_ref, x_base, to_y_ref)):
        start = 2 * group * size
        next_ref[group * size : (group + 1) * size, :] = kept_ref[
            start : start + size, :
        ] + in_ref[base : base + size, :].astype(F32)
        out_ref[...] = (
            kept_ref[start + size : start + 2 * size, :]
            + in_ref[base + size : base + 2 * size, :].astype(F32)
        ).astype(BF16)


def stage_three(plan, kept_ref, x_ref, y_ref, x_base, y_base, z_refs, last_ref):
    rows = plan.rows
    for group, in_ref, base in ((0, x_ref, x_base), (1, y_ref, y_base)):
        for z in range(plan.deep):
            start = (group * plan.deep + z) * rows
            value = kept_ref[start : start + rows, :] + in_ref[
                base + z * rows : base + (z + 1) * rows, :
            ].astype(F32)
            if z:
                z_refs[z - 1][group * rows : (group + 1) * rows, :] = value.astype(BF16)
            else:
                last_ref[group * rows : (group + 1) * rows, :] = value


def start_scatter_kernel(plan, keep_ref, came_ref, y_ref, x_ref, kept_ref):
    stage_one(plan, keep_ref, came_ref, y_ref, x_ref, kept_ref)


def slot_a_kernel(
    plan, keep1_ref, film1_ref, came1_ref, film_came_ref, kept2_ref, y2_ref, x2_ref,
    y_ref, x_ref, kept1_ref, next2_ref, film_ref,
):
    size, small = plan.weights // 4, plan.weights // 8
    stage_one(plan, keep1_ref, came1_ref, y_ref, x_ref, kept1_ref)
    stage_two(
        plan, kept2_ref, y2_ref, x2_ref, 0, 0,
        x_ref.at[size : size + small, :], y_ref.at[size : size + small, :], next2_ref,
    )
    end = 2 * plan.film_rows
    film_ref[...] = film1_ref[0] + get_pair(film_came_ref.at[:end, :])
    put_pair(
        film1_ref[1] + get_pair(film_came_ref.at[plan.film : plan.film + end, :]),
        y_ref.at[size + small : size + small + end, :],
    )


def slot_b_kernel(
    plan, kept1_ref, kept2_ref, film_ref, y_ref, x_ref, noise_ref, *outs,
):
    to_x_ref, to_y_ref, next1_ref, last2_ref, *z_refs = outs
    size, small = plan.weights // 4, plan.weights // 8
    stage_two(
        plan, kept1_ref, y_ref, x_ref, 0, 0, to_x_ref.at[:small, :], to_y_ref.at[:small, :], next1_ref
    )
    stage_three(plan, kept2_ref, x_ref, y_ref, size, size, z_refs, last2_ref)
    end = 2 * plan.film_rows
    start = size + small
    total = film_ref[...] + get_pair(y_ref.at[start : start + end, :])
    put_pair(total, to_x_ref.at[small : small + end, :])
    put_noise(jnp.full((1, LANES), noise_ref[0], F32), to_x_ref, small + end)


def slot_c_kernel(plan, kept1_ref, x_ref, y_ref, mine_ref, *outs):
    last1_ref, *z_refs = outs
    stage_three(plan, kept1_ref, x_ref, y_ref, 0, 0, z_refs, last1_ref)
    small, end = plan.weights // 8, 2 * plan.rows
    for z_ref in z_refs:
        z_ref[end : end + plan.film, :] = mine_ref[small : small + plan.film, :]
        z_ref[end + plan.film :, :] = x_ref[small : small + plan.film, :]


def finish_kernel(plan, last1_ref, last2_ref, mine_ref, x_ref, *refs):
    count = plan.deep - 1
    z1_refs, z2_refs, (out_ref, film_ref) = refs[:count], refs[count : 2 * count], refs[2 * count :]
    for layer, (last_ref, z_refs) in enumerate(((last1_ref, z1_refs), (last2_ref, z2_refs))):
        rows = plan.rows // 2
        for slot in range(4):
            at = slice(slot * rows, (slot + 1) * rows)
            total = last_ref[at, :]
            for z_ref in z_refs:
                total = total + z_ref[at, :].astype(F32)
            out_ref[layer, slot] = total
    small, end = plan.weights // 8, 2 * plan.rows
    packs = [ref.at[small : small + plan.film, :] for ref in (mine_ref, x_ref)]
    for z_ref in z1_refs:
        packs += [z_ref.at[end + i * plan.film : end + (i + 1) * plan.film, :] for i in range(2)]
    lane = lax.broadcasted_iota(jnp.int32, (1, LANES), 1)
    noise = jnp.ones((1, LANES), F32)
    pair = 2 * plan.film_rows
    for member, pack in enumerate(packs):
        noise = jnp.where(lane == member, get_noise(pack, pair), noise)
    embedding = embedding_of(jnp.broadcast_to(noise, (2 * NOISE_FREQ, LANES)))
    members = [get_pair(pack.at[:pair, :]) for pack in packs]
    half = plan.film_rows // LAYERS
    for layer in range(LAYERS):
        for part in range(half):
            row = layer * half + part
            total = jnp.zeros((2 * NOISE_FREQ, LANES), F32)
            for member, value in enumerate(members):
                total += embedding[:, member : member + 1] * value[row : row + 1, :]
            film_ref[layer, :, part * LANES : (part + 1) * LANES] = total


def film_kernel(rows_ref, out_ref):
    members, _, columns = rows_ref.shape
    rows = rows_ref[...]
    lane = lax.broadcasted_iota(jnp.int32, (1, LANES), 1)
    noise = jnp.ones((1, LANES), F32)
    for member in range(members):
        noise = jnp.where(lane == member, rows[member, LAYERS:, :1], noise)
    embedding = embedding_of(jnp.broadcast_to(noise, (2 * NOISE_FREQ, LANES)))
    for layer in range(LAYERS):
        total = jnp.zeros((2 * NOISE_FREQ, columns), F32)
        for member in range(members):
            total += embedding[:, member : member + 1] * rows[member, layer : layer + 1, :]
        out_ref[layer] = total


def whole():
    return pl.BlockSpec(memory_space=pltpu.VMEM)


def apart():
    return pl.BlockSpec(memory_space=pltpu.HBM)


def call(kernel, args, outs, scratch=(), flops=0, specs=None, limit=10 << 20, sems=()):
    moved = sum(a.size * a.dtype.itemsize for a in args)
    moved += sum(math.prod(shape) * jnp.dtype(kind).itemsize for shape, kind in outs)
    return pl.pallas_call(
        kernel,
        out_shape=[jax.ShapeDtypeStruct(shape, kind) for shape, kind in outs],
        in_specs=specs or [whole() for _ in args],
        out_specs=[whole() for _ in outs],
        scratch_shapes=[pltpu.VMEM(shape, kind) for shape, kind in scratch] + list(sems),
        compiler_params=pltpu.CompilerParams(vmem_limit_bytes=limit),
        cost_estimate=pl.CostEstimate(flops=flops, bytes_accessed=moved, transcendentals=0),
    )(*args)


def swap(block, axis, bit):
    count = lax.axis_size(axis)
    return lax.ppermute(block, axis, [(i, i ^ bit) for i in range(count)])


def exchange_other(to_other):
    count = lax.axis_size("mesh")
    route = []
    for i in range(1, count - 1, 2):
        route += [(i, i + 1), (i + 1, i)]
    return lax.ppermute(to_other, "mesh", route)


def exchange(to_pair, to_other):
    other = exchange_other(to_other)
    return swap(to_pair, "mesh", 1), other


class Plan:
    def __init__(self, width, ens_count, mesh_count):
        self.deep = ens_count // 2
        self.rows = 2 * width // ens_count
        self.weights = 8 * self.deep * self.rows
        self.film_rows = LAYERS * (2 * width // mesh_count) // LANES
        self.film = 16 * pl.cdiv(2 * self.film_rows + 3, 16)

    def at(self, group, first, second, z):
        return (((group * 2 + first) * 2 + second) * self.deep + z) * self.rows


def film_pieces(conds, noise_level, mesh_count):
    mesh = lax.axis_index("mesh")
    rows = jnp.concatenate(conds, axis=0)
    width = rows.shape[1] // mesh_count
    pieces = rows.reshape(LAYERS, mesh_count, width).transpose(1, 0, 2)
    pieces = jnp.take(pieces, lax.bitwise_xor(jnp.arange(mesh_count), mesh), axis=0)
    noise = jnp.where(jnp.arange(mesh_count) == 0, noise_level[0], 0.0)
    noise = jnp.broadcast_to(noise[:, None, None], (mesh_count, 1, width))
    return jnp.concatenate([pieces, noise], axis=1)


def film_mesh_step(pieces, bit):
    pieces = pieces.reshape(-1, 2, *pieces.shape[1:])
    return pieces[:, 0] + swap(pieces[:, 1], "mesh", bit)


def film_ens_step(rows, bit):
    return jnp.concatenate([rows, swap(rows, "ens", bit)])


def film_end(rows):
    shape = (LAYERS, 2 * NOISE_FREQ, rows.shape[2])
    return call(film_kernel, (rows,), [(shape, F32)])[0]


def bits_of(count):
    return [1 << index for index in range(count.bit_length() - 1)]


def bind(kernel, *settings):
    return functools.partial(kernel, *settings)


def body(inputs, cotangent, noise_level, neighbours, live_slots, projections, film_weights):
    states, cot = inputs[0], cotangent[0]
    nodes, width = states.shape
    rim = nodes // 2
    mesh_count, ens_count = lax.axis_size("mesh"), lax.axis_size("ens")
    side_o, side_p = halves(lax.rem(lax.axis_index("mesh"), 2), rim)
    square = 2 * nodes * width * width
    split = mesh_count == 4 and width % (mesh_count * LANES) == 0 and ens_count % 2 == 0
    plan = Plan(width, ens_count, mesh_count) if split else None

    def full(kind=BF16):
        return ((nodes, width), kind)

    def part(kind=BF16):
        return ((rim, width), kind)

    def block(rows, kind=BF16):
        return ((rows, LANES), kind)

    def hbm(value):
        return pltpu.with_memory_space_constraint(value, pltpu.HBM)

    smem = pl.BlockSpec(memory_space=pltpu.SMEM)
    cond_shape = ((1, 2 * width), F32)
    x_o = lax.dynamic_slice_in_dim(states, side_o, rim)
    x_p = lax.dynamic_slice_in_dim(states, side_p, rim)
    halo_p, halo_o = exchange(x_p, x_o)
    slots = neighbours.shape[1]
    film, bias_o, bias_p, normed1, q1, k1, v1, projections = call(
        start_kernel,
        (x_o, x_p, hbm(neighbours.T), hbm(live_slots.T), noise_level, hbm(film_weights),
         hbm(projections)),
        [((LAYERS, 2 * width), F32)] + [((rim, 3 * rim), F32)] * 2 + [full()] * 4
        + [(projections.shape, BF16)],
        scratch=[((slots, nodes), jnp.int32), ((slots, nodes), jnp.int32),
                 (film_weights.shape, F32), ((rim, slots), jnp.int32)],
        sems=[pltpu.SemaphoreType.DMA((5,))], flops=3 * square,
        specs=[whole()] * 2 + [apart()] * 2 + [smem] + [apart()] * 2,
    )
    probs_shapes = [((HEADS, rim, nodes), BF16), ((HEADS, rim, rim), BF16)]

    def forward(half, x, halo, bias):
        return call(
            bind(forward_kernel, half), (x, halo, film, q1, k1, v1, bias, projections),
            [part()] * 4 + probs_shapes + [part()], flops=2 * square,
        )

    next_o, normed1_o, k1_o, v1_o, own_o, over_o, attended1_o = forward(0, x_o, halo_o, bias_o)
    halo2_o = exchange_other(next_o)
    next_p, normed1_p, k1_p, v1_p, own_p, over_p, attended1_p = forward(1, x_p, halo_p, bias_p)
    halo2_p = swap(next_p, "mesh", 1)
    normed2, q2, k2, v2, ga2, cot2 = call(
        own_kernel, (next_o, next_p, cot, film, projections), [full()] * 6, flops=4 * square
    )

    def last(half, halo, bias, parts):
        grads = [part(), full(F32), full(F32)] if half else [part(), full(), full()]
        return call(
            bind(last_layer_kernel, half),
            (halo, film, q2, k2, v2, ga2, bias, projections, *parts),
            [part()] * 2 + grads + [part()] * (2 if half else 3),
            flops=4 * square,
        )

    normed2_p, attended2_p, gq2_p, *parts, gk2_p, gv2_p = last(1, halo2_p, bias_p, ())
    normed2_o, attended2_o, gq2_o, gk2, gv2, gk2_o, gv2_o, to_other = last(
        0, halo2_o, bias_o, parts
    )
    back_o = exchange_other(to_other)
    gn2, to_pair, cond2 = call(
        bind(grads_kernel, None, 1),
        (next_o, next_p, halo2_o, halo2_p, gq2_o, gq2_p, gk2, gv2, gk2_p, gv2_p, to_other,
         projections, film),
        [full(F32), part(), cond_shape], flops=4 * square,
    )
    back_p = swap(to_pair, "mesh", 1)

    def weight_grads(*args):
        if not split:
            return call(plain_weight_kernel, args, [((4, width, width), F32)], flops=6 * square)
        return call(
            bind(split_weight_kernel, plan), args,
            [block(plan.weights), block(plan.weights, F32)],
            scratch=[((4, width, width), F32)], flops=6 * square,
        )

    weights2 = weight_grads(
        normed2, normed2_o, normed2_p, attended2_o, attended2_p, cot2[:rim], cot2[rim:],
        gq2_o, gq2_p, gk2, gk2_o, gk2_p, gv2, gv2_o, gv2_p,
    )
    if split:
        sums = plan.weights
        came = swap(weights2[0], "mesh", 1)
        to_y, to_x, kept2 = call(
            bind(start_scatter_kernel, plan), (weights2[1], came),
            [block(sums // 4)] * 2 + [block(sums // 2, F32)],
        )
        y2, x2 = swap(to_y, "mesh", 2), swap(to_x, "ens", 1)

    def first(half, nxt, back, k_h, v_h, own, over, parts):
        grads = [part(), full(F32), full(F32)] if half else [part(), full(), full()]
        return call(
            bind(first_layer_kernel, half),
            (nxt, cot2, gn2, back, film, q1, k1, v1, k_h, v_h, own, over, projections, *parts),
            [part()] + grads + [part()] * (2 if half else 3),
            flops=4 * square,
        )

    up_p, gq1_p, *parts, gk1_p, gv1_p = first(1, next_p, back_p, k1_p, v1_p, own_p, over_p, ())
    up_o, gq1_o, gk1, gv1, gk1_o, gv1_o, to_other = first(
        0, next_o, back_o, k1_o, v1_o, own_o, over_o, parts
    )
    weights1 = weight_grads(
        normed1, normed1_o, normed1_p, attended1_o, attended1_p, up_o, up_p,
        gq1_o, gq1_p, gk1, gk1_o, gk1_p, gv1, gv1_o, gv1_p,
    )
    film_shapes = []
    if split:
        came = swap(weights1[0], "mesh", 1)
        film_shapes = [((2, plan.film_rows, LANES), F32), block(2 * plan.film)]
    back_o = exchange_other(to_other)
    gn1, to_pair, cond1, *film_parts = call(
        bind(grads_kernel, plan, 0),
        (x_o, x_p, halo_o, halo_p, gq1_o, gq1_p, gk1, gv1, gk1_p, gv1_p, to_other,
         projections, cond2),
        [full(F32), part(), cond_shape] + film_shapes,
        scratch=film_shapes[:1], flops=4 * square,
    )
    back_p = swap(to_pair, "mesh", 1)
    grad_input = call(end_kernel, (x_o, x_p, up_o, up_p, gn1, back_o, back_p, film), [full()])[0]
    if split:
        film_came = swap(film_parts[1], "mesh", 1)
        to_y, to_x, kept1, kept2, film_mine = call(
            bind(slot_a_kernel, plan),
            (weights1[1], film_parts[0], came, film_came, kept2, y2, x2),
            [block(sums // 4 + sums // 8 + plan.film), block(sums // 4 + sums // 8),
             block(sums // 2, F32), block(sums // 4, F32), block(plan.film_rows, F32)],
        )
        came_y, came_x = swap(to_y, "mesh", 2), swap(to_x, "ens", 1)
        others = range(1, plan.deep)
        to_x, to_y, kept1, last2, *to_z = call(
            bind(slot_b_kernel, plan),
            (kept1, kept2, film_mine, came_y, came_x, noise_level),
            [block(sums // 8 + plan.film), block(sums // 8), block(sums // 4, F32),
             block(2 * plan.rows, F32)] + [block(2 * plan.rows) for _ in others],
            specs=[whole()] * 5 + [smem],
        )
        came_x, came_y = swap(to_x, "ens", 1), swap(to_y, "mesh", 2)
        came_z2 = [swap(to_z[z - 1], "ens", 2 * z) for z in others]
        last1, *to_z = call(
            bind(slot_c_kernel, plan), (kept1, came_x, came_y, to_x),
            [block(2 * plan.rows, F32)] + [block(2 * plan.rows + 2 * plan.film) for _ in others],
        )
        came_z1 = [swap(to_z[z - 1], "ens", 2 * z) for z in others]
        weight_out, film_out = call(
            bind(finish_kernel, plan),
            (last1, last2, to_x, came_x, *came_z1, *came_z2),
            [((LAYERS, 4, width // ens_count, LANES), F32),
             ((LAYERS, 2 * NOISE_FREQ, 2 * width // mesh_count), F32)],
        )
    else:
        film_rows = film_pieces((cond1, cond2), noise_level, mesh_count)
        for bit in bits_of(mesh_count):
            film_rows = film_mesh_step(film_rows, bit)
        for bit in bits_of(ens_count):
            film_rows = film_ens_step(film_rows, bit)
        film_out = film_end(film_rows)
        total = jnp.stack([weights1[0], weights2[0]]).astype(BF16)
        total = lax.psum_scatter(total, "ens", scatter_dimension=2, tiled=True)
        weight_out = lax.psum_scatter(total, "mesh", scatter_dimension=3, tiled=True).astype(F32)
    return (grad_input[None], weight_out, film_out)


def solution(mesh):
    placed = (
        P("ens", "mesh", None),
        P("ens", "mesh", None),
        P("ens"),
        P("mesh", None),
        P("mesh", None),
        P(),
        P(),
    )
    return jax.shard_map(
        body,
        mesh=mesh,
        in_specs=placed,
        out_specs=(P("ens", "mesh", None), P(None, None, "ens", "mesh"), P(None, None, "mesh")),
        check_vma=False,
    )
```

```python
import functools
import math

import jax
import jax.numpy as jnp
from jax import lax
from jax.experimental import pallas as pl
from jax.experimental.pallas import tpu as pltpu
from jax.sharding import PartitionSpec as P


HEADS = 4
NOISE_FREQ = 16
LAYERS = 2
LANES = 128

epsilon = 1e-05

ENS, MESH = "ens", "mesh"
F32 = jnp.float32
BF16 = jnp.bfloat16
ABSENT = -1e30


def mm(left_side, right_side):
    return jnp.dot(left_side, right_side, preferred_element_type=F32)


def mm_rows(left_side, right_side):
    return lax.dot_general(
        left_side, right_side, (((0,), (0,)), ((), ())), preferred_element_type=F32
    )


def mm_cols(left_side, right_side):
    return lax.dot_general(
        left_side, right_side, (((1,), (1,)), ((), ())), preferred_element_type=F32
    )


def unit_of(states):
    values = states.astype(F32)
    centre = jnp.mean(values, axis=1, keepdims=True)
    centred = values - centre
    inverse = lax.rsqrt(jnp.mean(jnp.square(centred), axis=1, keepdims=True) + epsilon)
    return centred * inverse, inverse


def normed_of(states, film_ref, layer):
    width = states.shape[1]
    unit, _ = unit_of(states)
    scale = film_ref[layer : layer + 1, :width]
    shift = film_ref[layer : layer + 1, width:]
    return (unit * (1.0 + scale) + shift).astype(BF16)


def embedding_of(noise, axis):
    row = lax.broadcasted_iota(jnp.int32, noise.shape, axis)
    wave = row - jnp.where(row >= NOISE_FREQ, NOISE_FREQ, 0) + 1
    angle = jnp.log(noise) * wave.astype(F32)
    return jnp.where(row < NOISE_FREQ, jnp.sin(angle), jnp.cos(angle))


def project_own(normed, w_ref, layer):
    return [mm(normed, w_ref[layer, slot]).astype(BF16) for slot in range(3)]


def put_all(refs, values):
    for ref, value in zip(refs, values, strict=True):
        ref[...] = value


def side_by_side(parts):
    return jnp.concatenate(parts, axis=1)


def halves(parity, rim):
    return parity * rim, (1 - parity) * rim


def half_rows(ref, parity, half):
    rim = ref.shape[0] // 2
    return pl.ds(pl.multiple_of(halves(parity, rim)[half], rim), rim)


def load_kernel(
    x_hbm, near_hbm, live_hbm, film_w_hbm, noise_ref,
    x_o_ref, x_p_ref, near_ref, live_ref, film_w_ref, row_ref, sems,
):
    parity = lax.rem(lax.axis_index(MESH), 2)
    copies = [
        pltpu.make_async_copy(x_hbm.at[half_rows(x_hbm, parity, 0), :], x_o_ref, sems.at[0]),
        pltpu.make_async_copy(x_hbm.at[half_rows(x_hbm, parity, 1), :], x_p_ref, sems.at[1]),
        pltpu.make_async_copy(near_hbm, near_ref, sems.at[2]),
        pltpu.make_async_copy(live_hbm, live_ref, sems.at[3]),
        pltpu.make_async_copy(film_w_hbm, film_w_ref, sems.at[4]),
    ]
    for copy in copies:
        copy.start()
    row_ref[...] = embedding_of(jnp.full(row_ref.shape, noise_ref[0], F32), 1)
    for copy in copies:
        copy.wait()


def start_kernel(
    x_o_ref, x_p_ref, near_ref, live_ref, row_ref, film_w_ref, w_hbm,
    film_ref, bias_o_ref, bias_p_ref, normed_ref, q_ref, k_ref, v_ref, w_ref,
    near_t_ref, sems,
):
    copies = [
        pltpu.make_async_copy(w_hbm.at[0], w_ref.at[0], sems.at[0]),
        pltpu.make_async_copy(w_hbm.at[1:], w_ref.at[1:], sems.at[1]),
    ]
    for copy in copies:
        copy.start()
    slots, node_count = near_ref.shape
    rim = node_count // 2
    place = lax.axis_index(MESH)
    parity = lax.rem(place, 2)
    embedding = row_ref[...].T[: 2 * NOISE_FREQ, :1]
    for layer in range(LAYERS):
        film_ref[layer : layer + 1, :] = jnp.sum(
            embedding * film_w_ref[layer], axis=0, keepdims=True
        )
    normed_ref[:rim, :] = normed_of(x_o_ref[...], film_ref, 0)
    normed_ref[rim:, :] = normed_of(x_p_ref[...], film_ref, 0)
    kind = BF16 if rim + rim <= 256 else F32
    near = near_ref[...] - (place * node_count + rim)
    near = jnp.where(live_ref[...] > 0, near, -4 * node_count).astype(F32)
    column = lax.broadcasted_iota(jnp.int32, (1, 3 * rim), 1)
    side_o, side_p = halves(parity, rim)
    own = jnp.where(column < rim, column + side_o, column - rim + side_p)
    halo_o = column - 2 * rim + jnp.where(parity == 0, -rim, node_count)
    halo_p = column - 2 * rim + jnp.where(parity == 0, node_count, -rim)
    step = 32
    near_t_ref[...] = near.T
    for side, halo, out_ref in ((side_o, halo_o, bias_o_ref), (side_p, halo_p, bias_p_ref)):
        ids = (jnp.where(column < node_count, own, halo) - rim).astype(F32)
        ids = jnp.broadcast_to(ids, (step, 3 * rim)).astype(kind)

        def rows(index, carry, side=side, ids=ids, out_ref=out_ref):
            start = pl.multiple_of(index * step, step)
            near = near_t_ref[pl.ds(pl.multiple_of(side + start, step), step), :]
            bias = jnp.full((step, 3 * rim), ABSENT, kind)
            zero = jnp.zeros((step, 3 * rim), kind)
            for slot in range(slots):
                wide = jnp.broadcast_to(near[:, slot : slot + 1], (step, rim)).astype(kind)
                bias = jnp.where(jnp.concatenate([wide] * 3, axis=1) == ids, zero, bias)
            out_ref[pl.ds(start, step), :] = bias.astype(F32)
            return carry

        lax.fori_loop(0, rim // step, rows, 0)
    copies[0].wait()
    put_all((q_ref, k_ref, v_ref), project_own(normed_ref[...], w_ref, 0))
    copies[1].wait()


def own_kernel(
    x_o_ref, x_p_ref, cot_ref, film_ref, w_ref, normed_ref, q_ref, k_ref, v_ref, ga_ref, cot2_ref
):
    parity = lax.rem(lax.axis_index(MESH), 2)
    cot = jnp.concatenate([cot_ref[half_rows(cot_ref, parity, half), :] for half in range(2)])
    normed = normed_of(stacked(x_o_ref, x_p_ref), film_ref, 1)
    projected = project_own(normed, w_ref, 1)
    grad = mm_cols(cot, w_ref[1, 3]).astype(BF16)
    put_all((normed_ref, q_ref, k_ref, v_ref, ga_ref, cot2_ref), (normed, *projected, grad, cot))


def project_halo(halo_ref, film_ref, w_ref, layer):
    normed = normed_of(halo_ref[...], film_ref, layer)
    key = mm(normed, w_ref[layer, 1]).astype(BF16)
    value = mm(normed, w_ref[layer, 2]).astype(BF16)
    return normed, key, value


def weigh(scores, scores_h, bias, head):
    factor = 1.0 / math.sqrt(head)
    split = scores.shape[1]
    scores = scores * factor + bias[:, :split]
    scores_h = scores_h * factor + bias[:, split:]
    peak = jnp.maximum(
        jnp.max(scores, axis=1, keepdims=True), jnp.max(scores_h, axis=1, keepdims=True)
    )
    own, halo = jnp.exp(scores - peak), jnp.exp(scores_h - peak)
    total = jnp.sum(own, axis=1, keepdims=True) + jnp.sum(halo, axis=1, keepdims=True)
    return own, halo, 1.0 / total


def heads_of(width):
    head = width // HEADS
    return [slice(index * head, (index + 1) * head) for index in range(HEADS)]


def forward_kernel(
    half, x_ref, halo_ref, film_ref, q_ref, k_ref, v_ref, bias_ref, w_ref,
    next_ref, normed_h_ref, k_h_ref, v_h_ref, p_own_ref, p_halo_ref, attended_ref,
):
    rim, width = x_ref.shape
    rows = slice(half * rim, (half + 1) * rim)
    query, key, value, bias = q_ref[rows, :], k_ref[...], v_ref[...], bias_ref[...]
    heads = heads_of(width)
    scores = [mm_cols(query[:, cols], key[:, cols]) for cols in heads]
    normed, key_h, value_h = project_halo(halo_ref, film_ref, w_ref, 0)
    scores_h = [mm_cols(query[:, cols], key_h[:, cols]) for cols in heads]
    shares, parts = [], []
    for index, cols in enumerate(heads):
        own, halo, share = weigh(scores[index], scores_h[index], bias, width // HEADS)
        own, halo = (own * share).astype(BF16), (halo * share).astype(BF16)
        shares.append((own, halo))
        parts.append((mm(own, value[:, cols]) + mm(halo, value_h[:, cols])).astype(BF16))
    attended = side_by_side(parts)
    states = (x_ref[...].astype(F32) + mm(attended, w_ref[0, 3])).astype(BF16)
    put_all(
        (next_ref, normed_h_ref, k_h_ref, v_h_ref, attended_ref),
        (states, normed, key_h, value_h, attended),
    )
    for index, (own, halo) in enumerate(shares):
        p_own_ref[index] = own
        p_halo_ref[index] = halo


def head_backward(own, halo, own16, halo16, probs, probs_h, share, grad, query, key, key_h):
    middle = jnp.sum(own * probs, axis=1, keepdims=True) + jnp.sum(
        halo * probs_h, axis=1, keepdims=True
    )
    factor = 1.0 / math.sqrt(query.shape[1])
    if share is not None:
        middle, factor = middle * share, share * factor
    scores = (own * ((probs - middle) * factor)).astype(BF16)
    scores_h = (halo * ((probs_h - middle) * factor)).astype(BF16)
    return (
        (mm(scores, key) + mm(scores_h, key_h)).astype(BF16),
        mm_rows(scores, query),
        mm_rows(own16, grad),
        mm_rows(scores_h, query).astype(BF16),
        mm_rows(halo16, grad).astype(BF16),
    )


def joined(parts, before, kind):
    gq, gk, gv, gk_h, gv_h = [side_by_side(part) for part in zip(*parts, strict=True)]
    if before:
        gk, gv = gk + before[0][...], gv + before[1][...]
    return gq, gk.astype(kind), gv.astype(kind), gk_h, gv_h


def last_layer_kernel(half, halo_ref, film_ref, q_ref, k_ref, v_ref, ga_ref, bias_ref, w_ref, *refs):
    before = refs[:2] if half == 0 else ()
    normed_h_ref, attended_ref, *outs = refs[len(before) :]
    rim, width = halo_ref.shape
    rows = slice(half * rim, (half + 1) * rim)
    query, key, value, bias = q_ref[rows, :], k_ref[...], v_ref[...], bias_ref[...]
    grad = ga_ref[rows, :]
    heads = heads_of(width)
    scores = [mm_cols(query[:, cols], key[:, cols]) for cols in heads]
    probs = [mm_cols(grad[:, cols], value[:, cols]) for cols in heads]
    normed, key_h, value_h = project_halo(halo_ref, film_ref, w_ref, 1)
    scores_h = [mm_cols(query[:, cols], key_h[:, cols]) for cols in heads]
    probs_h = [mm_cols(grad[:, cols], value_h[:, cols]) for cols in heads]
    attended, parts = [], []
    for index, cols in enumerate(heads):
        own, halo, share = weigh(scores[index], scores_h[index], bias, width // HEADS)
        own16, halo16 = (own * share).astype(BF16), (halo * share).astype(BF16)
        attended.append((mm(own16, value[:, cols]) + mm(halo16, value_h[:, cols])).astype(BF16))
        parts.append(
            head_backward(
                own, halo, own16, halo16, probs[index], probs_h[index], share,
                grad[:, cols], query[:, cols], key[:, cols], key_h[:, cols],
            )
        )
    results = joined(parts, before, outs[1].dtype)
    results += (halo_grads(w_ref, 1, *results[3:]).astype(BF16),)
    put_all((normed_h_ref, attended_ref, *outs), (normed, side_by_side(attended), *results))


def halo_grads(w_ref, layer, gk_h, gv_h):
    return mm_cols(gk_h, w_ref[layer, 1]) + mm_cols(gv_h, w_ref[layer, 2])


def grads_kernel(
    layer, x_o_ref, x_p_ref, halo_o_ref, halo_p_ref, gq_o_ref, gq_p_ref, gk_ref, gv_ref,
    to_other_ref, to_pair_ref, w_ref, *refs,
):
    *before, gn_ref, cond_ref = refs
    _, width = x_o_ref.shape
    own = (
        mm_cols(stacked(gq_o_ref, gq_p_ref), w_ref[layer, 0])
        + mm_cols(gk_ref[...], w_ref[layer, 1])
        + mm_cols(gv_ref[...], w_ref[layer, 2])
    )
    grads = [to_other_ref[...].astype(F32), to_pair_ref[...].astype(F32), own]
    units = [unit_of(halo_o_ref[...])[0], unit_of(halo_p_ref[...])[0]]
    units.append(unit_of(stacked(x_o_ref, x_p_ref))[0])
    scaled = jnp.zeros((1, width), F32)
    plain = jnp.zeros((1, width), F32)
    for grad, unit in zip(grads, units, strict=True):
        scaled += jnp.sum(grad * unit, axis=0, keepdims=True)
        plain += jnp.sum(grad, axis=0, keepdims=True)
    gn_ref[...] = own
    cond_ref[:1, :width] = scaled
    cond_ref[:1, width:] = plain
    for row, ref in enumerate(before, 1):
        cond_ref[row : row + 1, :] = ref[...]


def upstream_of(states, up, grad, film_ref, layer):
    width = states.shape[1]
    unit, inverse = unit_of(states)
    grad = grad * (1.0 + film_ref[layer : layer + 1, :width])
    centred = (
        grad
        - jnp.mean(grad, axis=1, keepdims=True)
        - unit * jnp.mean(grad * unit, axis=1, keepdims=True)
    )
    return (up.astype(F32) + inverse * centred).astype(BF16)


def first_layer_kernel(
    half, next_ref, cot_ref, gn2_ref, back_ref, film_ref, q_ref, k_ref, v_ref, k_h_ref, v_h_ref,
    p_own_ref, p_halo_ref, w_ref, *refs,
):
    before = refs[:2] if half == 0 else ()
    up_ref, *outs = refs[len(before) :]
    rim, width = next_ref.shape
    rows = slice(half * rim, (half + 1) * rim)
    total = gn2_ref[rows, :] + back_ref[...].astype(F32)
    up = upstream_of(next_ref[...], cot_ref[rows, :], total, film_ref, 1)
    grad = mm_cols(up, w_ref[0, 3]).astype(BF16)
    query, key, value = q_ref[rows, :], k_ref[...], v_ref[...]
    key_h, value_h = k_h_ref[...], v_h_ref[...]
    heads = heads_of(width)
    probs = [mm_cols(grad[:, cols], value[:, cols]) for cols in heads]
    probs_h = [mm_cols(grad[:, cols], value_h[:, cols]) for cols in heads]
    parts = []
    for index, cols in enumerate(heads):
        own16, halo16 = p_own_ref[index], p_halo_ref[index]
        parts.append(
            head_backward(
                own16.astype(F32), halo16.astype(F32), own16, halo16, probs[index], probs_h[index],
                None, grad[:, cols], query[:, cols], key[:, cols], key_h[:, cols],
            )
        )
    results = joined(parts, before, outs[1].dtype)
    results += (halo_grads(w_ref, 0, *results[3:]).astype(BF16),)
    put_all((up_ref, *outs), (up, *results))


def end_kernel(
    x_o_ref, x_p_ref, up_o_ref, up_p_ref, gn_ref, back_o_ref, back_p_ref, film_ref, out_ref
):
    parity = lax.rem(lax.axis_index(MESH), 2)
    rim = x_o_ref.shape[0]
    total = gn_ref[...] + stacked(back_o_ref, back_p_ref).astype(F32)
    grad = upstream_of(stacked(x_o_ref, x_p_ref), stacked(up_o_ref, up_p_ref), total, film_ref, 0)
    for half in range(2):
        out_ref[half_rows(out_ref, parity, half), :] = grad[half * rim : (half + 1) * rim]


def stacked(*refs):
    return jnp.concatenate([ref[...] for ref in refs], axis=0)


def weight_products(
    normed_ref, normed_o_ref, normed_p_ref, attended_o_ref, attended_p_ref, up_o_ref, up_p_ref,
    gq_o_ref, gq_p_ref, gk_ref, gk_o_ref, gk_p_ref, gv_ref, gv_o_ref, gv_p_ref, put,
):
    put(3, mm_rows(stacked(attended_o_ref, attended_p_ref), stacked(up_o_ref, up_p_ref)))
    put(0, mm_rows(normed_ref[...], stacked(gq_o_ref, gq_p_ref)))
    normed = stacked(normed_ref, normed_o_ref, normed_p_ref)
    put(1, mm_rows(normed, stacked(gk_ref, gk_o_ref, gk_p_ref)))
    put(2, mm_rows(normed, stacked(gv_ref, gv_o_ref, gv_p_ref)))


def plain_weight_kernel(*refs):
    *ins, out_ref = refs

    def put(slot, value):
        out_ref[slot] = value

    weight_products(*ins, put)


def put_pair(value, out_ref):
    high = value.astype(BF16)
    rows = value.shape[0]
    out_ref[:rows, :] = high
    out_ref[rows:, :] = (value - high.astype(F32)).astype(BF16)


def get_pair(in_ref):
    rows = in_ref.shape[0] // 2
    return in_ref[:rows, :].astype(F32) + in_ref[rows:, :].astype(F32)


def get_noise(in_ref, start):
    parts = [in_ref[start + row : start + row + 1, :].astype(F32) for row in range(3)]
    return (parts[0] + parts[1]) + parts[2]


def put_noise(value, out_ref, start):
    for row in range(3):
        part = value.astype(BF16)
        out_ref[start + row : start + row + 1, :] = part
        value = value - part.astype(F32)


def split_weight_kernel(plan, *refs):
    *ins, send_ref, keep_ref, total_ref = refs

    def put(slot, value):
        total_ref[slot] = value

    weight_products(*ins, put)
    rows = plan.rows // 2
    ens, mesh = lax.axis_index(ENS), lax.axis_index(MESH)
    for slot in range(4):
        group, inner = slot // 2, slot % 2
        for core in range(2):
            for y in range(2):
                col = lax.bitwise_xor(mesh, y * 2 + core)
                cols = pl.ds(pl.multiple_of(col * LANES, LANES), LANES)
                for x in range(2):
                    for z in range(plan.deep):
                        row = lax.bitwise_xor(ens, z * 2 + x)
                        at = pl.ds(pl.multiple_of(row * rows, rows), rows)
                        piece = total_ref[slot, at, cols]
                        first, second = (y, x) if group == 0 else (x, y)
                        start = plan.at(group, first, second, z) + inner * rows
                        if core:
                            send_ref[start : start + rows, :] = piece.astype(BF16)
                        else:
                            keep_ref[start : start + rows, :] = piece


def stage_one(plan, keep_ref, came_ref, y_ref, x_ref, kept_ref):
    size = plan.weights // 4
    for group, out_ref in ((0, y_ref), (1, x_ref)):
        start = 2 * group * size
        kept_ref[group * size : (group + 1) * size, :] = keep_ref[
            start : start + size, :
        ] + came_ref[start : start + size, :].astype(F32)
        start += size
        out_ref[:size, :] = (
            keep_ref[start : start + size, :] + came_ref[start : start + size, :].astype(F32)
        ).astype(BF16)


def stage_two(plan, kept_ref, y_ref, x_ref, to_x_ref, to_y_ref, next_ref):
    size = plan.weights // 8
    for group, in_ref, out_ref in ((0, y_ref, to_x_ref), (1, x_ref, to_y_ref)):
        start = 2 * group * size
        next_ref[group * size : (group + 1) * size, :] = kept_ref[
            start : start + size, :
        ] + in_ref[:size, :].astype(F32)
        out_ref[...] = (
            kept_ref[start + size : start + 2 * size, :] + in_ref[size : 2 * size, :].astype(F32)
        ).astype(BF16)


def stage_three(plan, kept_ref, x_ref, y_ref, z_refs, last_ref):
    rows = plan.rows
    for group, in_ref in enumerate((x_ref, y_ref)):
        for z in range(plan.deep):
            start = (group * plan.deep + z) * rows
            value = kept_ref[start : start + rows, :] + in_ref[z * rows : (z + 1) * rows, :].astype(
                F32
            )
            if z:
                z_refs[z - 1][group * rows : (group + 1) * rows, :] = value.astype(BF16)
            else:
                last_ref[group * rows : (group + 1) * rows, :] = value


def stage_across(plan, kept_ref, y_ref, x_ref, z_refs, last_ref):
    rows = plan.rows
    for group, in_ref in enumerate((y_ref, x_ref)):
        for second in range(2):
            for z in range(plan.deep):
                start, inner = plan.at(0, group, second, z), plan.at(0, 0, second, z)
                value = kept_ref[start : start + rows, :] + in_ref[inner : inner + rows, :].astype(F32)
                spot = slice((group * 2 + second) * rows, (group * 2 + second + 1) * rows)
                if z:
                    z_refs[z - 1][spot, :] = value.astype(BF16)
                else:
                    last_ref[spot, :] = value


def start_scatter_kernel(plan, keep_ref, came_ref, y_ref, x_ref, kept_ref):
    stage_one(plan, keep_ref, came_ref, y_ref, x_ref, kept_ref)


def slot_a_kernel(
    plan, keep1_ref, came1_ref, conds_ref, conds_came_ref, y_ref, x_ref, kept1_ref, film_ref,
    total_ref, rows_ref,
):
    size = plan.weights // 4
    stage_one(plan, keep1_ref, came1_ref, y_ref, x_ref, kept1_ref)
    total_ref[...] = conds_ref[...] + conds_came_ref[...]
    mesh = lax.axis_index(MESH)
    part_rows = plan.film_rows // LAYERS
    for y, out_ref in enumerate((film_ref, rows_ref)):
        col = lax.bitwise_xor(mesh, y * 2) * (part_rows * LANES)
        for layer in range(LAYERS):
            for part in range(part_rows):
                start = pl.multiple_of(col + part * LANES, LANES)
                row = layer * part_rows + part
                out_ref[row : row + 1, :] = total_ref[layer : layer + 1, pl.ds(start, LANES)]
    put_pair(rows_ref[...], y_ref.at[size : size + 2 * plan.film_rows, :])


def across_kernel(plan, kept2_ref, y2_ref, x2_ref, last2_ref, *z_refs):
    stage_across(plan, kept2_ref, y2_ref, x2_ref, z_refs, last2_ref)


def slot_b_kernel(
    plan, kept1_ref, film_ref, y_ref, x_ref, embedding_ref, to_x_ref, to_y_ref, next1_ref
):
    size, small = plan.weights // 4, plan.weights // 8
    stage_two(plan, kept1_ref, y_ref, x_ref, to_x_ref.at[:small, :], to_y_ref, next1_ref)
    end = 2 * plan.film_rows
    total = film_ref[...] + get_pair(y_ref.at[size : size + end, :])
    put_pair(total, to_x_ref.at[small : small + end, :])
    put_noise(embedding_ref[:1, :], to_x_ref, small + end)


def slot_c_kernel(plan, kept1_ref, x_ref, y_ref, mine_ref, *outs):
    last1_ref, *z_refs = outs
    stage_three(plan, kept1_ref, x_ref, y_ref, z_refs, last1_ref)
    small, end = plan.weights // 8, 2 * plan.rows
    for z_ref in z_refs:
        z_ref[end : end + plan.film, :] = mine_ref[small : small + plan.film, :]
        z_ref[end + plan.film :, :] = x_ref[small : small + plan.film, :]


def late_kernel(plan, last2_ref, *refs):
    *z_refs, to_x_ref, to_y_ref, kept_ref = refs
    rows = plan.rows
    for group, out_ref in enumerate((to_x_ref, to_y_ref)):
        for second in range(2):
            spot = slice((group * 2 + second) * rows, (group * 2 + second + 1) * rows)
            total = last2_ref[spot, :]
            for z_ref in z_refs:
                total = total + z_ref[spot, :].astype(F32)
            if second:
                out_ref[...] = total.astype(BF16)
            else:
                kept_ref[group * rows : (group + 1) * rows, :] = total


def finish_kernel(plan, last1_ref, kept2_ref, late_x_ref, late_y_ref, mine_ref, x_ref, *refs):
    *z_refs, out_ref, film_ref = refs
    rows = plan.rows // 2
    for slot in range(4):
        at = slice(slot * rows, (slot + 1) * rows)
        total = last1_ref[at, :]
        for z_ref in z_refs:
            total = total + z_ref[at, :].astype(F32)
        out_ref[0, slot] = total
        late_ref = late_y_ref if slot // 2 else late_x_ref
        inner = slice(slot % 2 * rows, (slot % 2 + 1) * rows)
        out_ref[1, slot] = kept2_ref[at, :] + late_ref[inner, :].astype(F32)
    small, end = plan.weights // 8, 2 * plan.rows
    packs = [ref.at[small : small + plan.film, :] for ref in (mine_ref, x_ref)]
    for z_ref in z_refs:
        packs += [z_ref.at[end + i * plan.film : end + (i + 1) * plan.film, :] for i in range(2)]
    pair = 2 * plan.film_rows
    embedding = jnp.concatenate([get_noise(pack, pair) for pack in packs], axis=0).T
    members = [get_pair(pack.at[:pair, :]) for pack in packs]
    half = plan.film_rows // LAYERS
    for layer in range(LAYERS):
        for part in range(half):
            row = layer * half + part
            total = jnp.zeros((2 * NOISE_FREQ, LANES), F32)
            for member, value in enumerate(members):
                weight = embedding[: 2 * NOISE_FREQ, member : member + 1]
                total += weight * value[row : row + 1, :]
            film_ref[layer, :, part * LANES : (part + 1) * LANES] = total


def film_kernel(rows_ref, out_ref):
    members, _, columns = rows_ref.shape
    rows = rows_ref[...]
    lane = lax.broadcasted_iota(jnp.int32, (1, LANES), 1)
    noise = jnp.ones((1, LANES), F32)
    for member in range(members):
        noise = jnp.where(lane == member, rows[member, LAYERS:, :1], noise)
    embedding = embedding_of(jnp.broadcast_to(noise, (2 * NOISE_FREQ, LANES)), 0)
    for layer in range(LAYERS):
        total = jnp.zeros((2 * NOISE_FREQ, columns), F32)
        for member in range(members):
            total += embedding[:, member : member + 1] * rows[member, layer : layer + 1, :]
        out_ref[layer] = total


def whole():
    return pl.BlockSpec(memory_space=pltpu.VMEM)


def apart():
    return pl.BlockSpec(memory_space=pltpu.HBM)


def call(kernel, args, outs, scratch=(), flops=0, specs=None, limit=10 << 20, sems=()):
    moved = sum(a.size * a.dtype.itemsize for a in args)
    moved += sum(math.prod(shape) * jnp.dtype(kind).itemsize for shape, kind in outs)
    return pl.pallas_call(
        kernel,
        out_shape=[jax.ShapeDtypeStruct(shape, kind) for shape, kind in outs],
        in_specs=specs or [whole() for _ in args],
        out_specs=[whole() for _ in outs],
        scratch_shapes=[pltpu.VMEM(shape, kind) for shape, kind in scratch] + list(sems),
        compiler_params=pltpu.CompilerParams(vmem_limit_bytes=limit),
        cost_estimate=pl.CostEstimate(flops=flops, bytes_accessed=moved, transcendentals=0),
    )(*args)


def swap(block, axis, bit):
    count = lax.axis_size(axis)
    return lax.ppermute(block, axis, [(i, i ^ bit) for i in range(count)])


def exchange_other(to_other):
    count = lax.axis_size(MESH)
    route = []
    for i in range(1, count - 1, 2):
        route += [(i, i + 1), (i + 1, i)]
    return lax.ppermute(to_other, MESH, route)


def exchange(to_pair, to_other):
    other = exchange_other(to_other)
    return swap(to_pair, MESH, 1), other


class Plan:
    def __init__(self, width, ens_count, mesh_count):
        self.deep = ens_count // 2
        self.rows = 2 * width // ens_count
        self.weights = 8 * self.deep * self.rows
        self.film_rows = LAYERS * (2 * width // mesh_count) // LANES
        self.film = 16 * pl.cdiv(2 * self.film_rows + 3, 16)

    def at(self, group, first, second, z):
        return (((group * 2 + first) * 2 + second) * self.deep + z) * self.rows


def film_pieces(rows, noise_level, mesh_count):
    mesh = lax.axis_index(MESH)
    width = rows.shape[1] // mesh_count
    pieces = rows.reshape(LAYERS, mesh_count, width).transpose(1, 0, 2)
    pieces = jnp.take(pieces, lax.bitwise_xor(jnp.arange(mesh_count), mesh), axis=0)
    noise = jnp.where(jnp.arange(mesh_count) == 0, noise_level[0], 0.0)
    noise = jnp.broadcast_to(noise[:, None, None], (mesh_count, 1, width))
    return jnp.concatenate([pieces, noise], axis=1)


def film_mesh_step(pieces, bit):
    pieces = pieces.reshape(-1, 2, *pieces.shape[1:])
    return pieces[:, 0] + swap(pieces[:, 1], MESH, bit)


def film_ens_step(rows, bit):
    return jnp.concatenate([rows, swap(rows, ENS, bit)])


def film_end(rows):
    shape = (LAYERS, 2 * NOISE_FREQ, rows.shape[2])
    return call(film_kernel, (rows,), [(shape, F32)])[0]


def bits_of(count):
    return [1 << index for index in range(count.bit_length() - 1)]


def bind(kernel, *settings):
    return functools.partial(kernel, *settings)


def body(inputs, cotangent, noise_level, neighbours, live_slots, projections, film_weights):
    states, cot = inputs[0], cotangent[0]
    nodes, width = states.shape
    rim = nodes // 2
    mesh_count, ens_count = lax.axis_size(MESH), lax.axis_size(ENS)
    side_o, side_p = halves(lax.rem(lax.axis_index(MESH), 2), rim)
    square = 2 * nodes * width * width
    split = mesh_count == 4 and width % (mesh_count * LANES) == 0 and ens_count % 2 == 0
    plan = Plan(width, ens_count, mesh_count) if split else None

    def full(kind=BF16):
        return ((nodes, width), kind)

    def part(kind=BF16):
        return ((rim, width), kind)

    def block(rows, kind=BF16):
        return ((rows, LANES), kind)

    def hbm(value):
        return pltpu.with_memory_space_constraint(value, pltpu.HBM)

    smem = pl.BlockSpec(memory_space=pltpu.SMEM)
    cond_shape = ((1, 2 * width), F32)
    slots = neighbours.shape[1]
    table = ((slots, nodes), jnp.int32)
    x_o, x_p, near, live, film_w, emb_row = call(
        load_kernel,
        (hbm(states), hbm(neighbours.T), hbm(live_slots.T), hbm(film_weights), noise_level),
        [part(), part(), table, table, (film_weights.shape, F32), ((8, LANES), F32)],
        sems=[pltpu.SemaphoreType.DMA((5,))], specs=[apart()] * 4 + [smem],
    )
    halo_p, halo_o = exchange(x_p, x_o)
    film, bias_o, bias_p, normed1, q1, k1, v1, projections = call(
        start_kernel, (x_o, x_p, near, live, emb_row, film_w, hbm(projections)),
        [((LAYERS, 2 * width), F32)] + [((rim, 3 * rim), F32)] * 2 + [full()] * 4
        + [(projections.shape, BF16)],
        scratch=[((nodes, slots), F32)],
        sems=[pltpu.SemaphoreType.DMA((2,))], flops=3 * square,
        specs=[whole()] * 6 + [apart()],
    )
    probs_shapes = [((HEADS, rim, nodes), BF16), ((HEADS, rim, rim), BF16)]

    def forward(half, x, halo, bias):
        return call(
            bind(forward_kernel, half), (x, halo, film, q1, k1, v1, bias, projections),
            [part()] * 4 + probs_shapes + [part()], flops=2 * square,
        )

    next_o, normed1_o, k1_o, v1_o, own_o, over_o, attended1_o = forward(0, x_o, halo_o, bias_o)
    halo2_o = exchange_other(next_o)
    next_p, normed1_p, k1_p, v1_p, own_p, over_p, attended1_p = forward(1, x_p, halo_p, bias_p)
    halo2_p = swap(next_p, MESH, 1)
    normed2, q2, k2, v2, ga2, cot2 = call(
        own_kernel, (next_o, next_p, cot, film, projections), [full()] * 6, flops=4 * square
    )

    def last(half, halo, bias, parts):
        grads = [part(), full(F32), full(F32)] if half else [part(), full(), full()]
        return call(
            bind(last_layer_kernel, half),
            (halo, film, q2, k2, v2, ga2, bias, projections, *parts),
            [part()] * 2 + grads + [part()] * 3,
            flops=4 * square,
        )

    normed2_p, attended2_p, gq2_p, *parts, gk2_p, gv2_p, to_pair = last(1, halo2_p, bias_p, ())
    back_p = swap(to_pair, MESH, 1)
    normed2_o, attended2_o, gq2_o, gk2, gv2, gk2_o, gv2_o, to_other = last(
        0, halo2_o, bias_o, parts
    )
    back_o = exchange_other(to_other)
    gn2, cond2 = call(
        bind(grads_kernel, 1),
        (next_o, next_p, halo2_o, halo2_p, gq2_o, gq2_p, gk2, gv2, to_other, to_pair, projections),
        [full(F32), cond_shape], flops=4 * square,
    )

    def weight_grads(*args):
        if not split:
            return call(plain_weight_kernel, args, [((4, width, width), F32)], flops=6 * square)
        return call(
            bind(split_weight_kernel, plan), args,
            [block(plan.weights), block(plan.weights, F32)],
            scratch=[((4, width, width), F32)], flops=6 * square,
        )

    weights2 = weight_grads(
        normed2, normed2_o, normed2_p, attended2_o, attended2_p, cot2[:rim], cot2[rim:],
        gq2_o, gq2_p, gk2, gk2_o, gk2_p, gv2, gv2_o, gv2_p,
    )
    if split:
        sums = plan.weights
        came = swap(weights2[0], MESH, 1)
        to_y, to_x, kept2 = call(
            bind(start_scatter_kernel, plan), (weights2[1], came),
            [block(sums // 4)] * 2 + [block(sums // 2, F32)],
        )
        y2, x2 = swap(to_y, MESH, 2), swap(to_x, ENS, 1)

    def first(half, nxt, back, k_h, v_h, own, over, parts):
        grads = [part(), full(F32), full(F32)] if half else [part(), full(), full()]
        return call(
            bind(first_layer_kernel, half),
            (nxt, cot2, gn2, back, film, q1, k1, v1, k_h, v_h, own, over, projections, *parts),
            [part()] + grads + [part()] * 3,
            flops=4 * square,
        )

    up_p, gq1_p, *parts, gk1_p, gv1_p, to_pair = first(
        1, next_p, back_p, k1_p, v1_p, own_p, over_p, ()
    )
    up_o, gq1_o, gk1, gv1, gk1_o, gv1_o, to_other = first(
        0, next_o, back_o, k1_o, v1_o, own_o, over_o, parts
    )
    weights1 = weight_grads(
        normed1, normed1_o, normed1_p, attended1_o, attended1_p, up_o, up_p,
        gq1_o, gq1_p, gk1, gk1_o, gk1_p, gv1, gv1_o, gv1_p,
    )
    if split:
        came = swap(weights1[0], MESH, 1)
    back_o = exchange_other(to_other)
    back_p = swap(to_pair, MESH, 1)
    gn1, conds = call(
        bind(grads_kernel, 0),
        (x_o, x_p, halo_o, halo_p, gq1_o, gq1_p, gk1, gv1, to_other, to_pair, projections, cond2),
        [full(F32), ((LAYERS, 2 * width), F32)], flops=4 * square,
    )
    grad_input = call(end_kernel, (x_o, x_p, up_o, up_p, gn1, back_o, back_p, film), [full()])[0]
    if split:
        conds_came = swap(conds, MESH, 1)
        others = range(1, plan.deep)
        to_y, to_x, kept1, film_mine = call(
            bind(slot_a_kernel, plan), (weights1[1], came, conds, conds_came),
            [block(sums // 4 + plan.film), block(sums // 4), block(sums // 2, F32),
             block(plan.film_rows, F32)],
            scratch=[(conds.shape, F32), block(plan.film_rows, F32)],
        )
        came_y, came_x = swap(to_y, MESH, 2), swap(to_x, ENS, 1)
        last2, *to_z = call(
            bind(across_kernel, plan), (kept2, y2, x2),
            [block(4 * plan.rows, F32)] + [block(4 * plan.rows) for _ in others],
        )
        came_z2 = [swap(to_z[z - 1], ENS, 2 * z) for z in others]
        to_x, to_y, kept1 = call(
            bind(slot_b_kernel, plan), (kept1, film_mine, came_y, came_x, emb_row),
            [block(sums // 8 + plan.film), block(sums // 8), block(sums // 4, F32)],
        )
        came_x, came_y = swap(to_x, ENS, 1), swap(to_y, MESH, 2)
        last1, *to_z = call(
            bind(slot_c_kernel, plan), (kept1, came_x, came_y, to_x),
            [block(2 * plan.rows, F32)] + [block(2 * plan.rows + 2 * plan.film) for _ in others],
        )
        came_z1 = [swap(to_z[z - 1], ENS, 2 * z) for z in others]
        late_x, late_y, kept2 = call(
            bind(late_kernel, plan), (last2, *came_z2),
            [block(plan.rows)] * 2 + [block(2 * plan.rows, F32)],
        )
        late_x, late_y = swap(late_x, ENS, 1), swap(late_y, MESH, 2)
        weight_out, film_out = call(
            bind(finish_kernel, plan),
            (last1, kept2, late_x, late_y, to_x, came_x, *came_z1),
            [((LAYERS, 4, width // ens_count, LANES), F32),
             ((LAYERS, 2 * NOISE_FREQ, 2 * width // mesh_count), F32)],
        )
    else:
        film_rows = film_pieces(conds, noise_level, mesh_count)
        for bit in bits_of(mesh_count):
            film_rows = film_mesh_step(film_rows, bit)
        for bit in bits_of(ens_count):
            film_rows = film_ens_step(film_rows, bit)
        film_out = film_end(film_rows)
        total = jnp.stack([weights1[0], weights2[0]]).astype(BF16)
        total = lax.psum_scatter(total, ENS, scatter_dimension=2, tiled=True)
        weight_out = lax.psum_scatter(total, MESH, scatter_dimension=3, tiled=True).astype(F32)
    return (grad_input[None], weight_out, film_out)


def solution(mesh):
    placed = (
        P(ENS, MESH, None),
        P(ENS, MESH, None),
        P(ENS),
        P(MESH, None),
        P(MESH, None),
        P(),
        P(),
    )
    return jax.shard_map(
        body,
        mesh=mesh,
        in_specs=placed,
        out_specs=(P(ENS, MESH, None), P(None, None, ENS, MESH), P(None, None, MESH)),
        check_vma=False,
    )
```

```python
import functools
import math

import jax
import jax.numpy as jnp
from jax import lax
from jax.experimental import pallas as pl
from jax.experimental.pallas import tpu as pltpu
from jax.sharding import PartitionSpec as P


HEADS = 4
NOISE_FREQ = 16
LAYERS = 2
LANES = 128

epsilon = 1e-05

ENS, MESH = "ens", "mesh"
F32 = jnp.float32
BF16 = jnp.bfloat16
ABSENT = -1e30


def mm(left_side, right_side):
    return jnp.dot(left_side, right_side, preferred_element_type=F32)


def mm_rows(left_side, right_side):
    return lax.dot_general(
        left_side, right_side, (((0,), (0,)), ((), ())), preferred_element_type=F32
    )


def mm_cols(left_side, right_side):
    return lax.dot_general(
        left_side, right_side, (((1,), (1,)), ((), ())), preferred_element_type=F32
    )


def unit_of(states):
    values = states.astype(F32)
    centre = jnp.mean(values, axis=1, keepdims=True)
    centred = values - centre
    inverse = lax.rsqrt(jnp.mean(jnp.square(centred), axis=1, keepdims=True) + epsilon)
    return centred * inverse, inverse


def normed_of(states, film_ref, layer):
    width = states.shape[1]
    unit, _ = unit_of(states)
    scale = film_ref[layer : layer + 1, :width]
    shift = film_ref[layer : layer + 1, width:]
    return (unit * (1.0 + scale) + shift).astype(BF16)


def embedding_of(noise, axis):
    row = lax.broadcasted_iota(jnp.int32, noise.shape, axis)
    wave = row - jnp.where(row >= NOISE_FREQ, NOISE_FREQ, 0) + 1
    angle = jnp.log(noise) * wave.astype(F32)
    return jnp.where(row < NOISE_FREQ, jnp.sin(angle), jnp.cos(angle))


def project_own(normed, w_ref, layer):
    return [mm(normed, w_ref[layer, slot]).astype(BF16) for slot in range(3)]


def put_all(refs, values):
    for ref, value in zip(refs, values, strict=True):
        ref[...] = value


def side_by_side(parts):
    return jnp.concatenate(parts, axis=1)


def halves(parity, rim):
    return parity * rim, (1 - parity) * rim


def half_rows(ref, parity, half):
    rim = ref.shape[0] // 2
    return pl.ds(pl.multiple_of(halves(parity, rim)[half], rim), rim)


def load_kernel(
    x_hbm, near_hbm, live_hbm, film_w_hbm, noise_ref,
    x_o_ref, x_p_ref, near_ref, live_ref, film_w_ref, row_ref, sems,
):
    parity = lax.rem(lax.axis_index(MESH), 2)
    copies = [
        pltpu.make_async_copy(x_hbm.at[half_rows(x_hbm, parity, 0), :], x_o_ref, sems.at[0]),
        pltpu.make_async_copy(x_hbm.at[half_rows(x_hbm, parity, 1), :], x_p_ref, sems.at[1]),
        pltpu.make_async_copy(near_hbm, near_ref, sems.at[2]),
        pltpu.make_async_copy(live_hbm, live_ref, sems.at[3]),
        pltpu.make_async_copy(film_w_hbm, film_w_ref, sems.at[4]),
    ]
    for copy in copies:
        copy.start()
    row_ref[...] = embedding_of(jnp.full(row_ref.shape, noise_ref[0], F32), 1)
    for copy in copies:
        copy.wait()


def start_kernel(
    x_o_ref, x_p_ref, near_ref, live_ref, row_ref, film_w_ref, w_hbm,
    film_ref, bias_o_ref, bias_p_ref, normed_ref, q_ref, k_ref, v_ref, w_ref,
    near_t_ref, sems,
):
    copies = [
        pltpu.make_async_copy(w_hbm.at[0], w_ref.at[0], sems.at[0]),
        pltpu.make_async_copy(w_hbm.at[1:], w_ref.at[1:], sems.at[1]),
    ]
    for copy in copies:
        copy.start()
    slots, node_count = near_ref.shape
    rim = node_count // 2
    place = lax.axis_index(MESH)
    parity = lax.rem(place, 2)
    embedding = row_ref[...].T[: 2 * NOISE_FREQ, :1]
    for layer in range(LAYERS):
        film_ref[layer : layer + 1, :] = jnp.sum(
            embedding * film_w_ref[layer], axis=0, keepdims=True
        )
    normed_ref[:rim, :] = normed_of(x_o_ref[...], film_ref, 0)
    normed_ref[rim:, :] = normed_of(x_p_ref[...], film_ref, 0)
    kind = BF16 if rim + rim <= 256 else F32
    near = near_ref[...] - (place * node_count + rim)
    near = jnp.where(live_ref[...] > 0, near, -4 * node_count).astype(F32)
    column = lax.broadcasted_iota(jnp.int32, (1, 3 * rim), 1)
    side_o, side_p = halves(parity, rim)
    own = jnp.where(column < rim, column + side_o, column - rim + side_p)
    halo_o = column - 2 * rim + jnp.where(parity == 0, -rim, node_count)
    halo_p = column - 2 * rim + jnp.where(parity == 0, node_count, -rim)
    step = 32
    near_t_ref[...] = near.T
    for side, halo, out_ref in ((side_o, halo_o, bias_o_ref), (side_p, halo_p, bias_p_ref)):
        ids = (jnp.where(column < node_count, own, halo) - rim).astype(F32)
        ids = jnp.broadcast_to(ids, (step, 3 * rim)).astype(kind)

        def rows(index, carry, side=side, ids=ids, out_ref=out_ref):
            start = pl.multiple_of(index * step, step)
            near = near_t_ref[pl.ds(pl.multiple_of(side + start, step), step), :]
            bias = jnp.full((step, 3 * rim), ABSENT, kind)
            zero = jnp.zeros((step, 3 * rim), kind)
            for slot in range(slots):
                wide = jnp.broadcast_to(near[:, slot : slot + 1], (step, rim)).astype(kind)
                bias = jnp.where(jnp.concatenate([wide] * 3, axis=1) == ids, zero, bias)
            out_ref[pl.ds(start, step), :] = bias.astype(F32)
            return carry

        lax.fori_loop(0, rim // step, rows, 0)
    copies[0].wait()
    put_all((q_ref, k_ref, v_ref), project_own(normed_ref[...], w_ref, 0))
    copies[1].wait()


def own_kernel(
    x_o_ref, x_p_ref, cot_ref, film_ref, w_ref, normed_ref, q_ref, k_ref, v_ref, ga_ref, cot2_ref
):
    parity = lax.rem(lax.axis_index(MESH), 2)
    cot = jnp.concatenate([cot_ref[half_rows(cot_ref, parity, half), :] for half in range(2)])
    normed = normed_of(stacked(x_o_ref, x_p_ref), film_ref, 1)
    projected = project_own(normed, w_ref, 1)
    grad = mm_cols(cot, w_ref[1, 3]).astype(BF16)
    put_all((normed_ref, q_ref, k_ref, v_ref, ga_ref, cot2_ref), (normed, *projected, grad, cot))


def project_halo(halo_ref, film_ref, w_ref, layer):
    normed = normed_of(halo_ref[...], film_ref, layer)
    key = mm(normed, w_ref[layer, 1]).astype(BF16)
    value = mm(normed, w_ref[layer, 2]).astype(BF16)
    return normed, key, value


def weigh(scores, scores_h, bias, head):
    factor = 1.0 / math.sqrt(head)
    split = scores.shape[1]
    scores = scores * factor + bias[:, :split]
    scores_h = scores_h * factor + bias[:, split:]
    peak = jnp.maximum(
        jnp.max(scores, axis=1, keepdims=True), jnp.max(scores_h, axis=1, keepdims=True)
    )
    own, halo = jnp.exp(scores - peak), jnp.exp(scores_h - peak)
    total = jnp.sum(own, axis=1, keepdims=True) + jnp.sum(halo, axis=1, keepdims=True)
    return own, halo, 1.0 / total


def heads_of(width):
    head = width // HEADS
    return [slice(index * head, (index + 1) * head) for index in range(HEADS)]


def forward_kernel(
    half, x_ref, halo_ref, film_ref, q_ref, k_ref, v_ref, bias_ref, w_ref,
    next_ref, normed_h_ref, k_h_ref, v_h_ref, p_own_ref, p_halo_ref, attended_ref,
):
    rim, width = x_ref.shape
    rows = slice(half * rim, (half + 1) * rim)
    query, key, value, bias = q_ref[rows, :], k_ref[...], v_ref[...], bias_ref[...]
    heads = heads_of(width)
    scores = [mm_cols(query[:, cols], key[:, cols]) for cols in heads]
    normed, key_h, value_h = project_halo(halo_ref, film_ref, w_ref, 0)
    scores_h = [mm_cols(query[:, cols], key_h[:, cols]) for cols in heads]
    shares, parts = [], []
    for index, cols in enumerate(heads):
        own, halo, share = weigh(scores[index], scores_h[index], bias, width // HEADS)
        own, halo = (own * share).astype(BF16), (halo * share).astype(BF16)
        shares.append((own, halo))
        parts.append((mm(own, value[:, cols]) + mm(halo, value_h[:, cols])).astype(BF16))
    attended = side_by_side(parts)
    states = (x_ref[...].astype(F32) + mm(attended, w_ref[0, 3])).astype(BF16)
    put_all(
        (next_ref, normed_h_ref, k_h_ref, v_h_ref, attended_ref),
        (states, normed, key_h, value_h, attended),
    )
    for index, (own, halo) in enumerate(shares):
        p_own_ref[index] = own
        p_halo_ref[index] = halo


def head_backward(own, halo, own16, halo16, probs, probs_h, share, grad, query, key, key_h):
    middle = jnp.sum(own * probs, axis=1, keepdims=True) + jnp.sum(
        halo * probs_h, axis=1, keepdims=True
    )
    factor = 1.0 / math.sqrt(query.shape[1])
    if share is not None:
        middle, factor = middle * share, share * factor
    scores = (own * ((probs - middle) * factor)).astype(BF16)
    scores_h = (halo * ((probs_h - middle) * factor)).astype(BF16)
    return (
        (mm(scores, key) + mm(scores_h, key_h)).astype(BF16),
        mm_rows(scores, query),
        mm_rows(own16, grad),
        mm_rows(scores_h, query).astype(BF16),
        mm_rows(halo16, grad).astype(BF16),
    )


def joined(parts, before, kind):
    gq, gk, gv, gk_h, gv_h = [side_by_side(part) for part in zip(*parts, strict=True)]
    if before:
        gk, gv = gk + before[0][...], gv + before[1][...]
    return gq, gk.astype(kind), gv.astype(kind), gk_h, gv_h


def last_layer_kernel(half, halo_ref, film_ref, q_ref, k_ref, v_ref, ga_ref, bias_ref, w_ref, *refs):
    before = refs[:2] if half == 0 else ()
    normed_h_ref, attended_ref, *outs = refs[len(before) :]
    rim, width = halo_ref.shape
    rows = slice(half * rim, (half + 1) * rim)
    query, key, value, bias = q_ref[rows, :], k_ref[...], v_ref[...], bias_ref[...]
    grad = ga_ref[rows, :]
    heads = heads_of(width)
    scores = [mm_cols(query[:, cols], key[:, cols]) for cols in heads]
    probs = [mm_cols(grad[:, cols], value[:, cols]) for cols in heads]
    normed, key_h, value_h = project_halo(halo_ref, film_ref, w_ref, 1)
    scores_h = [mm_cols(query[:, cols], key_h[:, cols]) for cols in heads]
    probs_h = [mm_cols(grad[:, cols], value_h[:, cols]) for cols in heads]
    attended, parts = [], []
    for index, cols in enumerate(heads):
        own, halo, share = weigh(scores[index], scores_h[index], bias, width // HEADS)
        own16, halo16 = (own * share).astype(BF16), (halo * share).astype(BF16)
        attended.append((mm(own16, value[:, cols]) + mm(halo16, value_h[:, cols])).astype(BF16))
        parts.append(
            head_backward(
                own, halo, own16, halo16, probs[index], probs_h[index], share,
                grad[:, cols], query[:, cols], key[:, cols], key_h[:, cols],
            )
        )
    results = joined(parts, before, outs[1].dtype)
    results += (halo_grads(w_ref, 1, *results[3:]).astype(BF16),)
    put_all((normed_h_ref, attended_ref, *outs), (normed, side_by_side(attended), *results))


def halo_grads(w_ref, layer, gk_h, gv_h):
    return mm_cols(gk_h, w_ref[layer, 1]) + mm_cols(gv_h, w_ref[layer, 2])


def grads_kernel(
    layer, x_o_ref, x_p_ref, halo_o_ref, halo_p_ref, gq_o_ref, gq_p_ref, gk_ref, gv_ref,
    to_other_ref, to_pair_ref, w_ref, *refs,
):
    *before, gn_ref, cond_ref = refs
    _, width = x_o_ref.shape
    own = (
        mm_cols(stacked(gq_o_ref, gq_p_ref), w_ref[layer, 0])
        + mm_cols(gk_ref[...], w_ref[layer, 1])
        + mm_cols(gv_ref[...], w_ref[layer, 2])
    )
    grads = [to_other_ref[...].astype(F32), to_pair_ref[...].astype(F32), own]
    units = [unit_of(halo_o_ref[...])[0], unit_of(halo_p_ref[...])[0]]
    units.append(unit_of(stacked(x_o_ref, x_p_ref))[0])
    scaled = jnp.zeros((1, width), F32)
    plain = jnp.zeros((1, width), F32)
    for grad, unit in zip(grads, units, strict=True):
        scaled += jnp.sum(grad * unit, axis=0, keepdims=True)
        plain += jnp.sum(grad, axis=0, keepdims=True)
    gn_ref[...] = own
    cond_ref[:1, :width] = scaled
    cond_ref[:1, width:] = plain
    for row, ref in enumerate(before, 1):
        cond_ref[row : row + 1, :] = ref[...]


def upstream_of(states, up, grad, film_ref, layer):
    width = states.shape[1]
    unit, inverse = unit_of(states)
    grad = grad * (1.0 + film_ref[layer : layer + 1, :width])
    centred = (
        grad
        - jnp.mean(grad, axis=1, keepdims=True)
        - unit * jnp.mean(grad * unit, axis=1, keepdims=True)
    )
    return (up.astype(F32) + inverse * centred).astype(BF16)


def first_layer_kernel(
    half, next_ref, cot_ref, gn2_ref, back_ref, film_ref, q_ref, k_ref, v_ref, k_h_ref, v_h_ref,
    p_own_ref, p_halo_ref, w_ref, *refs,
):
    before = refs[:2] if half == 0 else ()
    up_ref, *outs = refs[len(before) :]
    rim, width = next_ref.shape
    rows = slice(half * rim, (half + 1) * rim)
    total = gn2_ref[rows, :] + back_ref[...].astype(F32)
    up = upstream_of(next_ref[...], cot_ref[rows, :], total, film_ref, 1)
    grad = mm_cols(up, w_ref[0, 3]).astype(BF16)
    query, key, value = q_ref[rows, :], k_ref[...], v_ref[...]
    key_h, value_h = k_h_ref[...], v_h_ref[...]
    heads = heads_of(width)
    probs = [mm_cols(grad[:, cols], value[:, cols]) for cols in heads]
    probs_h = [mm_cols(grad[:, cols], value_h[:, cols]) for cols in heads]
    parts = []
    for index, cols in enumerate(heads):
        own16, halo16 = p_own_ref[index], p_halo_ref[index]
        parts.append(
            head_backward(
                own16.astype(F32), halo16.astype(F32), own16, halo16, probs[index], probs_h[index],
                None, grad[:, cols], query[:, cols], key[:, cols], key_h[:, cols],
            )
        )
    results = joined(parts, before, outs[1].dtype)
    results += (halo_grads(w_ref, 0, *results[3:]).astype(BF16),)
    put_all((up_ref, *outs), (up, *results))


def end_kernel(
    x_o_ref, x_p_ref, up_o_ref, up_p_ref, gn_ref, back_o_ref, back_p_ref, film_ref, out_ref
):
    parity = lax.rem(lax.axis_index(MESH), 2)
    rim = x_o_ref.shape[0]
    total = gn_ref[...] + stacked(back_o_ref, back_p_ref).astype(F32)
    grad = upstream_of(stacked(x_o_ref, x_p_ref), stacked(up_o_ref, up_p_ref), total, film_ref, 0)
    for half in range(2):
        out_ref[half_rows(out_ref, parity, half), :] = grad[half * rim : (half + 1) * rim]


def stacked(*refs):
    return jnp.concatenate([ref[...] for ref in refs], axis=0)


def weight_products(
    normed_ref, normed_o_ref, normed_p_ref, attended_o_ref, attended_p_ref, up_o_ref, up_p_ref,
    gq_o_ref, gq_p_ref, gk_ref, gk_o_ref, gk_p_ref, gv_ref, gv_o_ref, gv_p_ref, put,
):
    put(3, mm_rows(stacked(attended_o_ref, attended_p_ref), stacked(up_o_ref, up_p_ref)))
    put(0, mm_rows(normed_ref[...], stacked(gq_o_ref, gq_p_ref)))
    normed = stacked(normed_ref, normed_o_ref, normed_p_ref)
    put(1, mm_rows(normed, stacked(gk_ref, gk_o_ref, gk_p_ref)))
    put(2, mm_rows(normed, stacked(gv_ref, gv_o_ref, gv_p_ref)))


def plain_weight_kernel(*refs):
    *ins, out_ref = refs

    def put(slot, value):
        out_ref[slot] = value

    weight_products(*ins, put)


def put_pair(value, out_ref):
    high = value.astype(BF16)
    rows = value.shape[0]
    out_ref[:rows, :] = high
    out_ref[rows:, :] = (value - high.astype(F32)).astype(BF16)


def get_pair(in_ref):
    rows = in_ref.shape[0] // 2
    return in_ref[:rows, :].astype(F32) + in_ref[rows:, :].astype(F32)


def get_noise(in_ref, start):
    parts = [in_ref[start + row : start + row + 1, :].astype(F32) for row in range(3)]
    return (parts[0] + parts[1]) + parts[2]


def put_noise(value, out_ref, start):
    for row in range(3):
        part = value.astype(BF16)
        out_ref[start + row : start + row + 1, :] = part
        value = value - part.astype(F32)


def split_weight_kernel(plan, *refs):
    (
        normed_ref, normed_o_ref, normed_p_ref, attended_o_ref, attended_p_ref, up_o_ref, up_p_ref,
        gq_o_ref, gq_p_ref, gk_ref, gk_o_ref, gk_p_ref, gv_ref, gv_o_ref, gv_p_ref,
        send_ref, keep_ref,
    ) = refs
    normed = stacked(normed_ref, normed_o_ref, normed_p_ref).T
    attended = stacked(attended_o_ref, attended_p_ref).T
    products = (
        (3, attended, (up_o_ref, up_p_ref)),
        (0, normed[:, : normed_ref.shape[0]], (gq_o_ref, gq_p_ref)),
        (1, normed, (gk_ref, gk_o_ref, gk_p_ref)),
        (2, normed, (gv_ref, gv_o_ref, gv_p_ref)),
    )
    rows = plan.rows // 2
    ens, mesh = lax.axis_index(ENS), lax.axis_index(MESH)
    for slot, left, rights in products:
        group, inner = slot // 2, slot % 2
        for core, out_ref in ((1, send_ref), (0, keep_ref)):
            right = []
            for y in range(2):
                col = pl.multiple_of(lax.bitwise_xor(mesh, y * 2 + core) * LANES, LANES)
                right.append(
                    jnp.concatenate([ref[:, pl.ds(col, LANES)] for ref in rights], axis=0)
                )
            value = mm(left, side_by_side(right)).astype(out_ref.dtype)
            for row in range(2 * plan.deep):
                place = lax.bitwise_xor(ens, row)
                x, z = lax.bitwise_and(place, 1), lax.shift_right_logical(place, 1)
                for y in range(2):
                    first, second = (y, x) if group == 0 else (x, y)
                    start = pl.multiple_of(plan.at(group, first, second, z) + inner * rows, rows)
                    out_ref[pl.ds(start, rows), :] = value[
                        row * rows : (row + 1) * rows, y * LANES : (y + 1) * LANES
                    ]


def stage_one(plan, keep_ref, came_ref, y_ref, x_ref, kept_ref):
    size = plan.weights // 4
    for group, out_ref in ((0, y_ref), (1, x_ref)):
        start = 2 * group * size
        kept_ref[group * size : (group + 1) * size, :] = keep_ref[
            start : start + size, :
        ] + came_ref[start : start + size, :].astype(F32)
        start += size
        out_ref[:size, :] = (
            keep_ref[start : start + size, :] + came_ref[start : start + size, :].astype(F32)
        ).astype(BF16)


def stage_two(plan, kept_ref, y_ref, x_ref, to_x_ref, to_y_ref, next_ref):
    size = plan.weights // 8
    for group, in_ref, out_ref in ((0, y_ref, to_x_ref), (1, x_ref, to_y_ref)):
        start = 2 * group * size
        next_ref[group * size : (group + 1) * size, :] = kept_ref[
            start : start + size, :
        ] + in_ref[:size, :].astype(F32)
        out_ref[...] = (
            kept_ref[start + size : start + 2 * size, :] + in_ref[size : 2 * size, :].astype(F32)
        ).astype(BF16)


def stage_three(plan, kept_ref, x_ref, y_ref, z_refs, last_ref):
    rows = plan.rows
    for group, in_ref in enumerate((x_ref, y_ref)):
        for z in range(plan.deep):
            start = (group * plan.deep + z) * rows
            value = kept_ref[start : start + rows, :] + in_ref[z * rows : (z + 1) * rows, :].astype(
                F32
            )
            if z:
                z_refs[z - 1][group * rows : (group + 1) * rows, :] = value.astype(BF16)
            else:
                last_ref[group * rows : (group + 1) * rows, :] = value


def stage_across(plan, kept_ref, y_ref, x_ref, z_refs, last_ref):
    rows = plan.rows
    for group, in_ref in enumerate((y_ref, x_ref)):
        for second in range(2):
            for z in range(plan.deep):
                start, inner = plan.at(0, group, second, z), plan.at(0, 0, second, z)
                value = kept_ref[start : start + rows, :] + in_ref[inner : inner + rows, :].astype(F32)
                spot = slice((group * 2 + second) * rows, (group * 2 + second + 1) * rows)
                if z:
                    z_refs[z - 1][spot, :] = value.astype(BF16)
                else:
                    last_ref[spot, :] = value


def start_scatter_kernel(plan, keep_ref, came_ref, y_ref, x_ref, kept_ref):
    stage_one(plan, keep_ref, came_ref, y_ref, x_ref, kept_ref)


def slot_a_kernel(
    plan, keep1_ref, came1_ref, conds_ref, conds_came_ref, y_ref, x_ref, kept1_ref, film_ref,
    total_ref, rows_ref,
):
    size = plan.weights // 4
    stage_one(plan, keep1_ref, came1_ref, y_ref, x_ref, kept1_ref)
    total_ref[...] = conds_ref[...] + conds_came_ref[...]
    mesh = lax.axis_index(MESH)
    part_rows = plan.film_rows // LAYERS
    for y, out_ref in enumerate((film_ref, rows_ref)):
        col = lax.bitwise_xor(mesh, y * 2) * (part_rows * LANES)
        for layer in range(LAYERS):
            for part in range(part_rows):
                start = pl.multiple_of(col + part * LANES, LANES)
                row = layer * part_rows + part
                out_ref[row : row + 1, :] = total_ref[layer : layer + 1, pl.ds(start, LANES)]
    put_pair(rows_ref[...], y_ref.at[size : size + 2 * plan.film_rows, :])


def across_kernel(plan, kept2_ref, y2_ref, x2_ref, last2_ref, *z_refs):
    stage_across(plan, kept2_ref, y2_ref, x2_ref, z_refs, last2_ref)


def slot_b_kernel(
    plan, kept1_ref, film_ref, y_ref, x_ref, embedding_ref, to_x_ref, to_y_ref, next1_ref
):
    size, small = plan.weights // 4, plan.weights // 8
    stage_two(plan, kept1_ref, y_ref, x_ref, to_x_ref.at[:small, :], to_y_ref, next1_ref)
    end = 2 * plan.film_rows
    total = film_ref[...] + get_pair(y_ref.at[size : size + end, :])
    put_pair(total, to_x_ref.at[small : small + end, :])
    put_noise(embedding_ref[:1, :], to_x_ref, small + end)


def slot_c_kernel(plan, kept1_ref, x_ref, y_ref, mine_ref, *outs):
    last1_ref, *z_refs = outs
    stage_three(plan, kept1_ref, x_ref, y_ref, z_refs, last1_ref)
    small, end = plan.weights // 8, 2 * plan.rows
    for z_ref in z_refs:
        z_ref[end : end + plan.film, :] = mine_ref[small : small + plan.film, :]
        z_ref[end + plan.film :, :] = x_ref[small : small + plan.film, :]


def late_kernel(plan, last2_ref, *refs):
    *z_refs, to_x_ref, to_y_ref, kept_ref = refs
    rows = plan.rows
    for group, out_ref in enumerate((to_x_ref, to_y_ref)):
        for second in range(2):
            spot = slice((group * 2 + second) * rows, (group * 2 + second + 1) * rows)
            total = last2_ref[spot, :]
            for z_ref in z_refs:
                total = total + z_ref[spot, :].astype(F32)
            if second:
                out_ref[...] = total.astype(BF16)
            else:
                kept_ref[group * rows : (group + 1) * rows, :] = total


def finish_kernel(plan, last1_ref, kept2_ref, late_x_ref, late_y_ref, mine_ref, x_ref, *refs):
    *z_refs, out_ref, film_ref = refs
    rows = plan.rows // 2
    for slot in range(4):
        at = slice(slot * rows, (slot + 1) * rows)
        total = last1_ref[at, :]
        for z_ref in z_refs:
            total = total + z_ref[at, :].astype(F32)
        out_ref[0, slot] = total
        late_ref = late_y_ref if slot // 2 else late_x_ref
        inner = slice(slot % 2 * rows, (slot % 2 + 1) * rows)
        out_ref[1, slot] = kept2_ref[at, :] + late_ref[inner, :].astype(F32)
    small, end = plan.weights // 8, 2 * plan.rows
    packs = [ref.at[small : small + plan.film, :] for ref in (mine_ref, x_ref)]
    for z_ref in z_refs:
        packs += [z_ref.at[end + i * plan.film : end + (i + 1) * plan.film, :] for i in range(2)]
    pair = 2 * plan.film_rows
    embedding = jnp.concatenate([get_noise(pack, pair) for pack in packs], axis=0).T
    members = [get_pair(pack.at[:pair, :]) for pack in packs]
    half = plan.film_rows // LAYERS
    for layer in range(LAYERS):
        for part in range(half):
            row = layer * half + part
            total = jnp.zeros((2 * NOISE_FREQ, LANES), F32)
            for member, value in enumerate(members):
                weight = embedding[: 2 * NOISE_FREQ, member : member + 1]
                total += weight * value[row : row + 1, :]
            film_ref[layer, :, part * LANES : (part + 1) * LANES] = total


def film_kernel(rows_ref, out_ref):
    members, _, columns = rows_ref.shape
    rows = rows_ref[...]
    lane = lax.broadcasted_iota(jnp.int32, (1, LANES), 1)
    noise = jnp.ones((1, LANES), F32)
    for member in range(members):
        noise = jnp.where(lane == member, rows[member, LAYERS:, :1], noise)
    embedding = embedding_of(jnp.broadcast_to(noise, (2 * NOISE_FREQ, LANES)), 0)
    for layer in range(LAYERS):
        total = jnp.zeros((2 * NOISE_FREQ, columns), F32)
        for member in range(members):
            total += embedding[:, member : member + 1] * rows[member, layer : layer + 1, :]
        out_ref[layer] = total


def whole():
    return pl.BlockSpec(memory_space=pltpu.VMEM)


def apart():
    return pl.BlockSpec(memory_space=pltpu.HBM)


def call(kernel, args, outs, scratch=(), flops=0, specs=None, limit=10 << 20, sems=()):
    moved = sum(a.size * a.dtype.itemsize for a in args)
    moved += sum(math.prod(shape) * jnp.dtype(kind).itemsize for shape, kind in outs)
    return pl.pallas_call(
        kernel,
        out_shape=[jax.ShapeDtypeStruct(shape, kind) for shape, kind in outs],
        in_specs=specs or [whole() for _ in args],
        out_specs=[whole() for _ in outs],
        scratch_shapes=[pltpu.VMEM(shape, kind) for shape, kind in scratch] + list(sems),
        compiler_params=pltpu.CompilerParams(vmem_limit_bytes=limit),
        cost_estimate=pl.CostEstimate(flops=flops, bytes_accessed=moved, transcendentals=0),
    )(*args)


def swap(block, axis, bit):
    count = lax.axis_size(axis)
    return lax.ppermute(block, axis, [(i, i ^ bit) for i in range(count)])


def exchange_other(to_other):
    count = lax.axis_size(MESH)
    route = []
    for i in range(1, count - 1, 2):
        route += [(i, i + 1), (i + 1, i)]
    return lax.ppermute(to_other, MESH, route)


def exchange(to_pair, to_other):
    other = exchange_other(to_other)
    return swap(to_pair, MESH, 1), other


class Plan:
    def __init__(self, width, ens_count, mesh_count):
        self.deep = ens_count // 2
        self.rows = 2 * width // ens_count
        self.weights = 8 * self.deep * self.rows
        self.film_rows = LAYERS * (2 * width // mesh_count) // LANES
        self.film = 16 * pl.cdiv(2 * self.film_rows + 3, 16)

    def at(self, group, first, second, z):
        return (((group * 2 + first) * 2 + second) * self.deep + z) * self.rows


def film_pieces(rows, noise_level, mesh_count):
    mesh = lax.axis_index(MESH)
    width = rows.shape[1] // mesh_count
    pieces = rows.reshape(LAYERS, mesh_count, width).transpose(1, 0, 2)
    pieces = jnp.take(pieces, lax.bitwise_xor(jnp.arange(mesh_count), mesh), axis=0)
    noise = jnp.where(jnp.arange(mesh_count) == 0, noise_level[0], 0.0)
    noise = jnp.broadcast_to(noise[:, None, None], (mesh_count, 1, width))
    return jnp.concatenate([pieces, noise], axis=1)


def film_mesh_step(pieces, bit):
    pieces = pieces.reshape(-1, 2, *pieces.shape[1:])
    return pieces[:, 0] + swap(pieces[:, 1], MESH, bit)


def film_ens_step(rows, bit):
    return jnp.concatenate([rows, swap(rows, ENS, bit)])


def film_end(rows):
    shape = (LAYERS, 2 * NOISE_FREQ, rows.shape[2])
    return call(film_kernel, (rows,), [(shape, F32)])[0]


def bits_of(count):
    return [1 << index for index in range(count.bit_length() - 1)]


def bind(kernel, *settings):
    return functools.partial(kernel, *settings)


def body(inputs, cotangent, noise_level, neighbours, live_slots, projections, film_weights):
    states, cot = inputs[0], cotangent[0]
    nodes, width = states.shape
    rim = nodes // 2
    mesh_count, ens_count = lax.axis_size(MESH), lax.axis_size(ENS)
    side_o, side_p = halves(lax.rem(lax.axis_index(MESH), 2), rim)
    square = 2 * nodes * width * width
    split = mesh_count == 4 and width % (mesh_count * LANES) == 0 and ens_count % 2 == 0
    plan = Plan(width, ens_count, mesh_count) if split else None

    def full(kind=BF16):
        return ((nodes, width), kind)

    def part(kind=BF16):
        return ((rim, width), kind)

    def block(rows, kind=BF16):
        return ((rows, LANES), kind)

    def hbm(value):
        return pltpu.with_memory_space_constraint(value, pltpu.HBM)

    smem = pl.BlockSpec(memory_space=pltpu.SMEM)
    cond_shape = ((1, 2 * width), F32)
    slots = neighbours.shape[1]
    table = ((slots, nodes), jnp.int32)
    x_o, x_p, near, live, film_w, emb_row = call(
        load_kernel,
        (hbm(states), hbm(neighbours.T), hbm(live_slots.T), hbm(film_weights), noise_level),
        [part(), part(), table, table, (film_weights.shape, F32), ((8, LANES), F32)],
        sems=[pltpu.SemaphoreType.DMA((5,))], specs=[apart()] * 4 + [smem],
    )
    halo_p, halo_o = exchange(x_p, x_o)
    film, bias_o, bias_p, normed1, q1, k1, v1, projections = call(
        start_kernel, (x_o, x_p, near, live, emb_row, film_w, hbm(projections)),
        [((LAYERS, 2 * width), F32)] + [((rim, 3 * rim), F32)] * 2 + [full()] * 4
        + [(projections.shape, BF16)],
        scratch=[((nodes, slots), F32)],
        sems=[pltpu.SemaphoreType.DMA((2,))], flops=3 * square,
        specs=[whole()] * 6 + [apart()],
    )
    probs_shapes = [((HEADS, rim, nodes), BF16), ((HEADS, rim, rim), BF16)]

    def forward(half, x, halo, bias):
        return call(
            bind(forward_kernel, half), (x, halo, film, q1, k1, v1, bias, projections),
            [part()] * 4 + probs_shapes + [part()], flops=2 * square,
        )

    next_o, normed1_o, k1_o, v1_o, own_o, over_o, attended1_o = forward(0, x_o, halo_o, bias_o)
    halo2_o = exchange_other(next_o)
    next_p, normed1_p, k1_p, v1_p, own_p, over_p, attended1_p = forward(1, x_p, halo_p, bias_p)
    halo2_p = swap(next_p, MESH, 1)
    normed2, q2, k2, v2, ga2, cot2 = call(
        own_kernel, (next_o, next_p, cot, film, projections), [full()] * 6, flops=4 * square
    )

    def last(half, halo, bias, parts):
        grads = [part(), full(F32), full(F32)] if half else [part(), full(), full()]
        return call(
            bind(last_layer_kernel, half),
            (halo, film, q2, k2, v2, ga2, bias, projections, *parts),
            [part()] * 2 + grads + [part()] * 3,
            flops=4 * square,
        )

    normed2_p, attended2_p, gq2_p, *parts, gk2_p, gv2_p, to_pair = last(1, halo2_p, bias_p, ())
    back_p = swap(to_pair, MESH, 1)
    normed2_o, attended2_o, gq2_o, gk2, gv2, gk2_o, gv2_o, to_other = last(
        0, halo2_o, bias_o, parts
    )
    back_o = exchange_other(to_other)
    gn2, cond2 = call(
        bind(grads_kernel, 1),
        (next_o, next_p, halo2_o, halo2_p, gq2_o, gq2_p, gk2, gv2, to_other, to_pair, projections),
        [full(F32), cond_shape], flops=4 * square,
    )

    def weight_grads(*args):
        if not split:
            return call(plain_weight_kernel, args, [((4, width, width), F32)], flops=6 * square)
        return call(
            bind(split_weight_kernel, plan), args,
            [block(plan.weights), block(plan.weights, F32)], flops=6 * square,
        )

    weights2 = weight_grads(
        normed2, normed2_o, normed2_p, attended2_o, attended2_p, cot2[:rim], cot2[rim:],
        gq2_o, gq2_p, gk2, gk2_o, gk2_p, gv2, gv2_o, gv2_p,
    )
    if split:
        sums = plan.weights
        came = swap(weights2[0], MESH, 1)
        to_y, to_x, kept2 = call(
            bind(start_scatter_kernel, plan), (weights2[1], came),
            [block(sums // 4)] * 2 + [block(sums // 2, F32)],
        )
        y2, x2 = swap(to_y, MESH, 2), swap(to_x, ENS, 1)

    def first(half, nxt, back, k_h, v_h, own, over, parts):
        grads = [part(), full(F32), full(F32)] if half else [part(), full(), full()]
        return call(
            bind(first_layer_kernel, half),
            (nxt, cot2, gn2, back, film, q1, k1, v1, k_h, v_h, own, over, projections, *parts),
            [part()] + grads + [part()] * 3,
            flops=4 * square,
        )

    up_p, gq1_p, *parts, gk1_p, gv1_p, to_pair = first(
        1, next_p, back_p, k1_p, v1_p, own_p, over_p, ()
    )
    up_o, gq1_o, gk1, gv1, gk1_o, gv1_o, to_other = first(
        0, next_o, back_o, k1_o, v1_o, own_o, over_o, parts
    )
    weights1 = weight_grads(
        normed1, normed1_o, normed1_p, attended1_o, attended1_p, up_o, up_p,
        gq1_o, gq1_p, gk1, gk1_o, gk1_p, gv1, gv1_o, gv1_p,
    )
    if split:
        came = swap(weights1[0], MESH, 1)
    back_o = exchange_other(to_other)
    back_p = swap(to_pair, MESH, 1)
    gn1, conds = call(
        bind(grads_kernel, 0),
        (x_o, x_p, halo_o, halo_p, gq1_o, gq1_p, gk1, gv1, to_other, to_pair, projections, cond2),
        [full(F32), ((LAYERS, 2 * width), F32)], flops=4 * square,
    )
    grad_input = call(end_kernel, (x_o, x_p, up_o, up_p, gn1, back_o, back_p, film), [full()])[0]
    if split:
        conds_came = swap(conds, MESH, 1)
        others = range(1, plan.deep)
        to_y, to_x, kept1, film_mine = call(
            bind(slot_a_kernel, plan), (weights1[1], came, conds, conds_came),
            [block(sums // 4 + plan.film), block(sums // 4), block(sums // 2, F32),
             block(plan.film_rows, F32)],
            scratch=[(conds.shape, F32), block(plan.film_rows, F32)],
        )
        came_y, came_x = swap(to_y, MESH, 2), swap(to_x, ENS, 1)
        last2, *to_z = call(
            bind(across_kernel, plan), (kept2, y2, x2),
            [block(4 * plan.rows, F32)] + [block(4 * plan.rows) for _ in others],
        )
        came_z2 = [swap(to_z[z - 1], ENS, 2 * z) for z in others]
        to_x, to_y, kept1 = call(
            bind(slot_b_kernel, plan), (kept1, film_mine, came_y, came_x, emb_row),
            [block(sums // 8 + plan.film), block(sums // 8), block(sums // 4, F32)],
        )
        came_x, came_y = swap(to_x, ENS, 1), swap(to_y, MESH, 2)
        last1, *to_z = call(
            bind(slot_c_kernel, plan), (kept1, came_x, came_y, to_x),
            [block(2 * plan.rows, F32)] + [block(2 * plan.rows + 2 * plan.film) for _ in others],
        )
        came_z1 = [swap(to_z[z - 1], ENS, 2 * z) for z in others]
        late_x, late_y, kept2 = call(
            bind(late_kernel, plan), (last2, *came_z2),
            [block(plan.rows)] * 2 + [block(2 * plan.rows, F32)],
        )
        late_x, late_y = swap(late_x, ENS, 1), swap(late_y, MESH, 2)
        weight_out, film_out = call(
            bind(finish_kernel, plan),
            (last1, kept2, late_x, late_y, to_x, came_x, *came_z1),
            [((LAYERS, 4, width // ens_count, LANES), F32),
             ((LAYERS, 2 * NOISE_FREQ, 2 * width // mesh_count), F32)],
        )
    else:
        film_rows = film_pieces(conds, noise_level, mesh_count)
        for bit in bits_of(mesh_count):
            film_rows = film_mesh_step(film_rows, bit)
        for bit in bits_of(ens_count):
            film_rows = film_ens_step(film_rows, bit)
        film_out = film_end(film_rows)
        total = jnp.stack([weights1[0], weights2[0]]).astype(BF16)
        total = lax.psum_scatter(total, ENS, scatter_dimension=2, tiled=True)
        weight_out = lax.psum_scatter(total, MESH, scatter_dimension=3, tiled=True).astype(F32)
    return (grad_input[None], weight_out, film_out)


def solution(mesh):
    placed = (
        P(ENS, MESH, None),
        P(ENS, MESH, None),
        P(ENS),
        P(MESH, None),
        P(MESH, None),
        P(),
        P(),
    )
    return jax.shard_map(
        body,
        mesh=mesh,
        in_specs=placed,
        out_specs=(P(ENS, MESH, None), P(None, None, ENS, MESH), P(None, None, MESH)),
        check_vma=False,
    )
```

```python
import functools
import math

import jax
import jax.numpy as jnp
from jax import lax
from jax.experimental import pallas as pl
from jax.experimental.pallas import tpu as pltpu
from jax.sharding import PartitionSpec as P


HEADS = 4
NOISE_FREQ = 16
LAYERS = 2
LANES = 128

epsilon = 1e-05

ENS, MESH = "ens", "mesh"
F32 = jnp.float32
BF16 = jnp.bfloat16
ABSENT = -1e30


def mm(left_side, right_side):
    return jnp.dot(left_side, right_side, preferred_element_type=F32)


def mm_rows(left_side, right_side):
    return lax.dot_general(
        left_side, right_side, (((0,), (0,)), ((), ())), preferred_element_type=F32
    )


def mm_cols(left_side, right_side):
    return lax.dot_general(
        left_side, right_side, (((1,), (1,)), ((), ())), preferred_element_type=F32
    )


def unit_of(states):
    values = states.astype(F32)
    centre = jnp.mean(values, axis=1, keepdims=True)
    centred = values - centre
    inverse = lax.rsqrt(jnp.mean(jnp.square(centred), axis=1, keepdims=True) + epsilon)
    return centred * inverse, inverse


def normed_of(states, film_ref, layer):
    width = states.shape[1]
    unit, _ = unit_of(states)
    scale = film_ref[layer : layer + 1, :width]
    shift = film_ref[layer : layer + 1, width:]
    return (unit * (1.0 + scale) + shift).astype(BF16)


def embedding_of(noise, axis):
    row = lax.broadcasted_iota(jnp.int32, noise.shape, axis)
    wave = row - jnp.where(row >= NOISE_FREQ, NOISE_FREQ, 0) + 1
    angle = jnp.log(noise) * wave.astype(F32)
    return jnp.where(row < NOISE_FREQ, jnp.sin(angle), jnp.cos(angle))


def project_own(normed, w_ref, layer):
    return [mm(normed, w_ref[layer, slot]).astype(BF16) for slot in range(3)]


def put_all(refs, values):
    for ref, value in zip(refs, values, strict=True):
        ref[...] = value


def side_by_side(parts):
    return jnp.concatenate(parts, axis=1)


def halves(parity, rim):
    return parity * rim, (1 - parity) * rim


def half_rows(ref, parity, half):
    rim = ref.shape[0] // 2
    return pl.ds(pl.multiple_of(halves(parity, rim)[half], rim), rim)


def load_kernel(
    x_hbm, near_hbm, live_hbm, film_w_hbm, noise_ref,
    x_o_ref, x_p_ref, near_ref, live_ref, film_w_ref, row_ref, sems,
):
    parity = lax.rem(lax.axis_index(MESH), 2)
    copies = [
        pltpu.make_async_copy(x_hbm.at[half_rows(x_hbm, parity, 0), :], x_o_ref, sems.at[0]),
        pltpu.make_async_copy(x_hbm.at[half_rows(x_hbm, parity, 1), :], x_p_ref, sems.at[1]),
        pltpu.make_async_copy(near_hbm, near_ref, sems.at[2]),
        pltpu.make_async_copy(live_hbm, live_ref, sems.at[3]),
        pltpu.make_async_copy(film_w_hbm, film_w_ref, sems.at[4]),
    ]
    for copy in copies:
        copy.start()
    row_ref[...] = embedding_of(jnp.full(row_ref.shape, noise_ref[0], F32), 1)
    for copy in copies:
        copy.wait()


def start_kernel(
    x_o_ref, x_p_ref, near_ref, live_ref, row_ref, film_w_ref, w_hbm,
    film_ref, bias_o_ref, bias_p_ref, normed_ref, q_ref, k_ref, v_ref, w_ref,
    near_t_ref, sems,
):
    copies = [
        pltpu.make_async_copy(w_hbm.at[0], w_ref.at[0], sems.at[0]),
        pltpu.make_async_copy(w_hbm.at[1:], w_ref.at[1:], sems.at[1]),
    ]
    for copy in copies:
        copy.start()
    slots, node_count = near_ref.shape
    rim = node_count // 2
    place = lax.axis_index(MESH)
    parity = lax.rem(place, 2)
    embedding = row_ref[...].T[: 2 * NOISE_FREQ, :1]
    for layer in range(LAYERS):
        film_ref[layer : layer + 1, :] = jnp.sum(
            embedding * film_w_ref[layer], axis=0, keepdims=True
        )
    normed_ref[:rim, :] = normed_of(x_o_ref[...], film_ref, 0)
    normed_ref[rim:, :] = normed_of(x_p_ref[...], film_ref, 0)
    kind = BF16 if rim + rim <= 256 else F32
    near = near_ref[...] - (place * node_count + rim)
    near = jnp.where(live_ref[...] > 0, near, -4 * node_count).astype(F32)
    column = lax.broadcasted_iota(jnp.int32, (1, 3 * rim), 1)
    side_o, side_p = halves(parity, rim)
    own = jnp.where(column < rim, column + side_o, column - rim + side_p)
    halo_o = column - 2 * rim + jnp.where(parity == 0, -rim, node_count)
    halo_p = column - 2 * rim + jnp.where(parity == 0, node_count, -rim)
    step = 32
    near_t_ref[...] = near.T
    for side, halo, out_ref in ((side_o, halo_o, bias_o_ref), (side_p, halo_p, bias_p_ref)):
        ids = (jnp.where(column < node_count, own, halo) - rim).astype(F32)
        ids = jnp.broadcast_to(ids, (step, 3 * rim)).astype(kind)

        def rows(index, carry, side=side, ids=ids, out_ref=out_ref):
            start = pl.multiple_of(index * step, step)
            near = near_t_ref[pl.ds(pl.multiple_of(side + start, step), step), :]
            bias = jnp.full((step, 3 * rim), ABSENT, kind)
            zero = jnp.zeros((step, 3 * rim), kind)
            for slot in range(slots):
                wide = jnp.broadcast_to(near[:, slot : slot + 1], (step, rim)).astype(kind)
                bias = jnp.where(jnp.concatenate([wide] * 3, axis=1) == ids, zero, bias)
            out_ref[pl.ds(start, step), :] = bias.astype(F32)
            return carry

        lax.fori_loop(0, rim // step, rows, 0)
    copies[0].wait()
    put_all((q_ref, k_ref, v_ref), project_own(normed_ref[...], w_ref, 0))
    copies[1].wait()


def own_kernel(
    x_o_ref, x_p_ref, cot_ref, film_ref, w_ref, normed_ref, q_ref, k_ref, v_ref, ga_ref, cot2_ref
):
    parity = lax.rem(lax.axis_index(MESH), 2)
    cot = jnp.concatenate([cot_ref[half_rows(cot_ref, parity, half), :] for half in range(2)])
    normed = normed_of(stacked(x_o_ref, x_p_ref), film_ref, 1)
    projected = project_own(normed, w_ref, 1)
    grad = mm_cols(cot, w_ref[1, 3]).astype(BF16)
    put_all((normed_ref, q_ref, k_ref, v_ref, ga_ref, cot2_ref), (normed, *projected, grad, cot))


def project_halo(halo_ref, film_ref, w_ref, layer):
    normed = normed_of(halo_ref[...], film_ref, layer)
    key = mm(normed, w_ref[layer, 1]).astype(BF16)
    value = mm(normed, w_ref[layer, 2]).astype(BF16)
    return normed, key, value


def weigh(scores, scores_h, bias, head):
    factor = 1.0 / math.sqrt(head)
    split = scores.shape[1]
    scores = scores * factor + bias[:, :split]
    scores_h = scores_h * factor + bias[:, split:]
    peak = jnp.maximum(
        jnp.max(scores, axis=1, keepdims=True), jnp.max(scores_h, axis=1, keepdims=True)
    )
    own, halo = jnp.exp(scores - peak), jnp.exp(scores_h - peak)
    total = jnp.sum(own, axis=1, keepdims=True) + jnp.sum(halo, axis=1, keepdims=True)
    return own, halo, 1.0 / total


def heads_of(width):
    head = width // HEADS
    return [slice(index * head, (index + 1) * head) for index in range(HEADS)]


def forward_kernel(
    half, x_ref, halo_ref, film_ref, q_ref, k_ref, v_ref, bias_ref, w_ref,
    next_ref, normed_h_ref, k_h_ref, v_h_ref, p_own_ref, p_halo_ref, attended_ref,
):
    rim, width = x_ref.shape
    rows = slice(half * rim, (half + 1) * rim)
    query, key, value, bias = q_ref[rows, :], k_ref[...], v_ref[...], bias_ref[...]
    heads = heads_of(width)
    scores = [mm_cols(query[:, cols], key[:, cols]) for cols in heads]
    normed, key_h, value_h = project_halo(halo_ref, film_ref, w_ref, 0)
    scores_h = [mm_cols(query[:, cols], key_h[:, cols]) for cols in heads]
    shares, parts = [], []
    for index, cols in enumerate(heads):
        own, halo, share = weigh(scores[index], scores_h[index], bias, width // HEADS)
        own, halo = (own * share).astype(BF16), (halo * share).astype(BF16)
        shares.append((own, halo))
        parts.append((mm(own, value[:, cols]) + mm(halo, value_h[:, cols])).astype(BF16))
    attended = side_by_side(parts)
    states = (x_ref[...].astype(F32) + mm(attended, w_ref[0, 3])).astype(BF16)
    put_all(
        (next_ref, normed_h_ref, k_h_ref, v_h_ref, attended_ref),
        (states, normed, key_h, value_h, attended),
    )
    for index, (own, halo) in enumerate(shares):
        p_own_ref[index] = own
        p_halo_ref[index] = halo


def head_backward(own, halo, own16, halo16, probs, probs_h, share, grad, query, key, key_h):
    middle = jnp.sum(own * probs, axis=1, keepdims=True) + jnp.sum(
        halo * probs_h, axis=1, keepdims=True
    )
    factor = 1.0 / math.sqrt(query.shape[1])
    if share is not None:
        middle, factor = middle * share, share * factor
    scores = (own * ((probs - middle) * factor)).astype(BF16)
    scores_h = (halo * ((probs_h - middle) * factor)).astype(BF16)
    return (
        (mm(scores, key) + mm(scores_h, key_h)).astype(BF16),
        mm_rows(scores, query),
        mm_rows(own16, grad),
        mm_rows(scores_h, query).astype(BF16),
        mm_rows(halo16, grad).astype(BF16),
    )


def joined(parts, before, kind):
    gq, gk, gv, gk_h, gv_h = [side_by_side(part) for part in zip(*parts, strict=True)]
    if before:
        gk, gv = gk + before[0][...], gv + before[1][...]
    return gq, gk.astype(kind), gv.astype(kind), gk_h, gv_h


def last_layer_kernel(half, halo_ref, film_ref, q_ref, k_ref, v_ref, ga_ref, bias_ref, w_ref, *refs):
    before = refs[:2] if half == 0 else ()
    normed_h_ref, attended_ref, *outs = refs[len(before) :]
    rim, width = halo_ref.shape
    rows = slice(half * rim, (half + 1) * rim)
    query, key, value, bias = q_ref[rows, :], k_ref[...], v_ref[...], bias_ref[...]
    grad = ga_ref[rows, :]
    heads = heads_of(width)
    scores = [mm_cols(query[:, cols], key[:, cols]) for cols in heads]
    probs = [mm_cols(grad[:, cols], value[:, cols]) for cols in heads]
    normed, key_h, value_h = project_halo(halo_ref, film_ref, w_ref, 1)
    scores_h = [mm_cols(query[:, cols], key_h[:, cols]) for cols in heads]
    probs_h = [mm_cols(grad[:, cols], value_h[:, cols]) for cols in heads]
    attended, parts = [], []
    for index, cols in enumerate(heads):
        own, halo, share = weigh(scores[index], scores_h[index], bias, width // HEADS)
        own16, halo16 = (own * share).astype(BF16), (halo * share).astype(BF16)
        attended.append((mm(own16, value[:, cols]) + mm(halo16, value_h[:, cols])).astype(BF16))
        parts.append(
            head_backward(
                own, halo, own16, halo16, probs[index], probs_h[index], share,
                grad[:, cols], query[:, cols], key[:, cols], key_h[:, cols],
            )
        )
    results = joined(parts, before, outs[1].dtype)
    results += (halo_grads(w_ref, 1, *results[3:]).astype(BF16),)
    put_all((normed_h_ref, attended_ref, *outs), (normed, side_by_side(attended), *results))


def halo_grads(w_ref, layer, gk_h, gv_h):
    return mm_cols(gk_h, w_ref[layer, 1]) + mm_cols(gv_h, w_ref[layer, 2])


def grads_kernel(
    layer, x_o_ref, x_p_ref, halo_o_ref, halo_p_ref, gq_o_ref, gq_p_ref, gk_ref, gv_ref,
    to_other_ref, to_pair_ref, w_ref, *refs,
):
    *before, gn_ref, cond_ref = refs
    _, width = x_o_ref.shape
    own = (
        mm_cols(stacked(gq_o_ref, gq_p_ref), w_ref[layer, 0])
        + mm_cols(gk_ref[...], w_ref[layer, 1])
        + mm_cols(gv_ref[...], w_ref[layer, 2])
    )
    grads = [to_other_ref[...].astype(F32), to_pair_ref[...].astype(F32), own]
    units = [unit_of(halo_o_ref[...])[0], unit_of(halo_p_ref[...])[0]]
    units.append(unit_of(stacked(x_o_ref, x_p_ref))[0])
    scaled = jnp.zeros((1, width), F32)
    plain = jnp.zeros((1, width), F32)
    for grad, unit in zip(grads, units, strict=True):
        scaled += jnp.sum(grad * unit, axis=0, keepdims=True)
        plain += jnp.sum(grad, axis=0, keepdims=True)
    gn_ref[...] = own
    cond_ref[:1, :width] = scaled
    cond_ref[:1, width:] = plain
    for row, ref in enumerate(before, 1):
        cond_ref[row : row + 1, :] = ref[...]


def upstream_of(states, up, grad, film_ref, layer):
    width = states.shape[1]
    unit, inverse = unit_of(states)
    grad = grad * (1.0 + film_ref[layer : layer + 1, :width])
    centred = (
        grad
        - jnp.mean(grad, axis=1, keepdims=True)
        - unit * jnp.mean(grad * unit, axis=1, keepdims=True)
    )
    return (up.astype(F32) + inverse * centred).astype(BF16)


def first_layer_kernel(
    half, next_ref, cot_ref, gn2_ref, back_ref, film_ref, q_ref, k_ref, v_ref, k_h_ref, v_h_ref,
    p_own_ref, p_halo_ref, w_ref, *refs,
):
    before = refs[:2] if half == 0 else ()
    up_ref, *outs = refs[len(before) :]
    rim, width = next_ref.shape
    rows = slice(half * rim, (half + 1) * rim)
    total = gn2_ref[rows, :] + back_ref[...].astype(F32)
    up = upstream_of(next_ref[...], cot_ref[rows, :], total, film_ref, 1)
    grad = mm_cols(up, w_ref[0, 3]).astype(BF16)
    query, key, value = q_ref[rows, :], k_ref[...], v_ref[...]
    key_h, value_h = k_h_ref[...], v_h_ref[...]
    heads = heads_of(width)
    probs = [mm_cols(grad[:, cols], value[:, cols]) for cols in heads]
    probs_h = [mm_cols(grad[:, cols], value_h[:, cols]) for cols in heads]
    parts = []
    for index, cols in enumerate(heads):
        own16, halo16 = p_own_ref[index], p_halo_ref[index]
        parts.append(
            head_backward(
                own16.astype(F32), halo16.astype(F32), own16, halo16, probs[index], probs_h[index],
                None, grad[:, cols], query[:, cols], key[:, cols], key_h[:, cols],
            )
        )
    results = joined(parts, before, outs[1].dtype)
    results += (halo_grads(w_ref, 0, *results[3:]).astype(BF16),)
    put_all((up_ref, *outs), (up, *results))


def end_kernel(
    x_o_ref, x_p_ref, up_o_ref, up_p_ref, gn_ref, back_o_ref, back_p_ref, film_ref, out_ref
):
    parity = lax.rem(lax.axis_index(MESH), 2)
    rim = x_o_ref.shape[0]
    total = gn_ref[...] + stacked(back_o_ref, back_p_ref).astype(F32)
    grad = upstream_of(stacked(x_o_ref, x_p_ref), stacked(up_o_ref, up_p_ref), total, film_ref, 0)
    for half in range(2):
        out_ref[half_rows(out_ref, parity, half), :] = grad[half * rim : (half + 1) * rim]


def stacked(*refs):
    return jnp.concatenate([ref[...] for ref in refs], axis=0)


def weight_products(
    normed_ref, normed_o_ref, normed_p_ref, attended_o_ref, attended_p_ref, up_o_ref, up_p_ref,
    gq_o_ref, gq_p_ref, gk_ref, gk_o_ref, gk_p_ref, gv_ref, gv_o_ref, gv_p_ref, put,
):
    put(3, mm_rows(stacked(attended_o_ref, attended_p_ref), stacked(up_o_ref, up_p_ref)))
    put(0, mm_rows(normed_ref[...], stacked(gq_o_ref, gq_p_ref)))
    normed = stacked(normed_ref, normed_o_ref, normed_p_ref)
    put(1, mm_rows(normed, stacked(gk_ref, gk_o_ref, gk_p_ref)))
    put(2, mm_rows(normed, stacked(gv_ref, gv_o_ref, gv_p_ref)))


def plain_weight_kernel(*refs):
    *ins, out_ref = refs

    def put(slot, value):
        out_ref[slot] = value

    weight_products(*ins, put)


def put_pair(value, out_ref):
    high = value.astype(BF16)
    rows = value.shape[0]
    out_ref[:rows, :] = high
    out_ref[rows:, :] = (value - high.astype(F32)).astype(BF16)


def get_pair(in_ref):
    rows = in_ref.shape[0] // 2
    return in_ref[:rows, :].astype(F32) + in_ref[rows:, :].astype(F32)


def get_noise(in_ref, start):
    parts = [in_ref[start + row : start + row + 1, :].astype(F32) for row in range(3)]
    return (parts[0] + parts[1]) + parts[2]


def put_noise(value, out_ref, start):
    for row in range(3):
        part = value.astype(BF16)
        out_ref[start + row : start + row + 1, :] = part
        value = value - part.astype(F32)


def split_weight_kernel(plan, *refs):
    (
        normed_ref, normed_o_ref, normed_p_ref, attended_o_ref, attended_p_ref, up_o_ref, up_p_ref,
        gq_o_ref, gq_p_ref, gk_ref, gk_o_ref, gk_p_ref, gv_ref, gv_o_ref, gv_p_ref,
        *send_refs, keep_ref,
    ) = refs
    normed = stacked(normed_ref, normed_o_ref, normed_p_ref).T
    attended = stacked(attended_o_ref, attended_p_ref).T
    products = (
        (3, attended, (up_o_ref, up_p_ref)),
        (0, normed[:, : normed_ref.shape[0]], (gq_o_ref, gq_p_ref)),
        (1, normed, (gk_ref, gk_o_ref, gk_p_ref)),
        (2, normed, (gv_ref, gv_o_ref, gv_p_ref)),
    )
    rows = plan.rows // 2
    ens, mesh = lax.axis_index(ENS), lax.axis_index(MESH)
    for slot, left, rights in products:
        group, inner = slot // 2, slot % 2
        send_ref, base = send_refs[0], 0
        if len(send_refs) > 1:
            send_ref, base = send_refs[group], group * (plan.weights // 2)
        for core, out_ref, base in ((1, send_ref, base), (0, keep_ref, 0)):
            right = []
            for y in range(2):
                col = pl.multiple_of(lax.bitwise_xor(mesh, y * 2 + core) * LANES, LANES)
                right.append(
                    jnp.concatenate([ref[:, pl.ds(col, LANES)] for ref in rights], axis=0)
                )
            value = mm(left, side_by_side(right)).astype(out_ref.dtype)
            for row in range(2 * plan.deep):
                place = lax.bitwise_xor(ens, row)
                x, z = lax.bitwise_and(place, 1), lax.shift_right_logical(place, 1)
                for y in range(2):
                    first, second = (y, x) if group == 0 else (x, y)
                    start = plan.at(group, first, second, z) + inner * rows - base
                    start = pl.multiple_of(start, rows)
                    out_ref[pl.ds(start, rows), :] = value[
                        row * rows : (row + 1) * rows, y * LANES : (y + 1) * LANES
                    ]


def stage_one(plan, group, keep_ref, came_ref, base, out_ref, kept_ref):
    size = plan.weights // 4
    start, inner = 2 * group * size, base
    kept_ref[...] = keep_ref[start : start + size, :] + came_ref[inner : inner + size, :].astype(F32)
    start, inner = start + size, inner + size
    out_ref[...] = (
        keep_ref[start : start + size, :] + came_ref[inner : inner + size, :].astype(F32)
    ).astype(BF16)


def stage_two(plan, kept_ref, in_ref, out_ref, next_ref):
    size = plan.weights // 8
    next_ref[...] = kept_ref[:size, :] + in_ref[:size, :].astype(F32)
    out_ref[...] = (kept_ref[size:, :] + in_ref[size : 2 * size, :].astype(F32)).astype(BF16)


def stage_three(plan, kept_refs, in_refs, z_refs, last_ref):
    rows = plan.rows
    for group, (kept_ref, in_ref) in enumerate(zip(kept_refs, in_refs, strict=True)):
        spot = slice(group * rows, (group + 1) * rows)
        for z in range(plan.deep):
            at = slice(z * rows, (z + 1) * rows)
            value = kept_ref[at, :] + in_ref[at, :].astype(F32)
            if z:
                z_refs[z - 1][spot, :] = value.astype(BF16)
            else:
                last_ref[spot, :] = value


def stage_across(plan, kept_ref, y_ref, x_ref, z_refs, last_ref):
    rows = plan.rows
    for group, in_ref in enumerate((y_ref, x_ref)):
        for second in range(2):
            for z in range(plan.deep):
                start, inner = plan.at(0, group, second, z), plan.at(0, 0, second, z)
                value = kept_ref[start : start + rows, :] + in_ref[inner : inner + rows, :].astype(F32)
                spot = slice((group * 2 + second) * rows, (group * 2 + second + 1) * rows)
                if z:
                    z_refs[z - 1][spot, :] = value.astype(BF16)
                else:
                    last_ref[spot, :] = value


def start_scatter_kernel(plan, keep_ref, came_ref, y_ref, x_ref, kept_ref):
    size = plan.weights // 4
    for group, out_ref in enumerate((y_ref, x_ref)):
        kept = kept_ref.at[group * size : (group + 1) * size, :]
        stage_one(plan, group, keep_ref, came_ref, 2 * group * size, out_ref, kept)


def slot_ax_kernel(plan, keep1_ref, came1_ref, x_ref, kept1_ref):
    stage_one(plan, 1, keep1_ref, came1_ref, 0, x_ref, kept1_ref)


def slot_ay_kernel(
    plan, keep1_ref, came1_ref, conds_ref, conds_came_ref, y_ref, kept1_ref, film_ref,
    total_ref, rows_ref,
):
    size = plan.weights // 4
    stage_one(plan, 0, keep1_ref, came1_ref, 0, y_ref.at[:size, :], kept1_ref)
    total_ref[...] = conds_ref[...] + conds_came_ref[...]
    mesh = lax.axis_index(MESH)
    part_rows = plan.film_rows // LAYERS
    for y, out_ref in enumerate((film_ref, rows_ref)):
        col = lax.bitwise_xor(mesh, y * 2) * (part_rows * LANES)
        for layer in range(LAYERS):
            for part in range(part_rows):
                start = pl.multiple_of(col + part * LANES, LANES)
                row = layer * part_rows + part
                out_ref[row : row + 1, :] = total_ref[layer : layer + 1, pl.ds(start, LANES)]
    put_pair(rows_ref[...], y_ref.at[size : size + 2 * plan.film_rows, :])


def across_kernel(plan, kept2_ref, y2_ref, x2_ref, last2_ref, *z_refs):
    stage_across(plan, kept2_ref, y2_ref, x2_ref, z_refs, last2_ref)


def slot_by_kernel(plan, kept1_ref, x_ref, to_y_ref, next1_ref):
    stage_two(plan, kept1_ref, x_ref, to_y_ref, next1_ref)


def slot_bx_kernel(plan, kept1_ref, film_ref, y_ref, embedding_ref, to_x_ref, next1_ref):
    size, small = plan.weights // 4, plan.weights // 8
    stage_two(plan, kept1_ref, y_ref, to_x_ref.at[:small, :], next1_ref)
    end = 2 * plan.film_rows
    total = film_ref[...] + get_pair(y_ref.at[size : size + end, :])
    put_pair(total, to_x_ref.at[small : small + end, :])
    put_noise(embedding_ref[:1, :], to_x_ref, small + end)


def slot_c_kernel(plan, kept_x_ref, kept_y_ref, x_ref, y_ref, mine_ref, *outs):
    last1_ref, *z_refs = outs
    stage_three(plan, (kept_x_ref, kept_y_ref), (x_ref, y_ref), z_refs, last1_ref)
    small, end = plan.weights // 8, 2 * plan.rows
    for z_ref in z_refs:
        z_ref[end : end + plan.film, :] = mine_ref[small : small + plan.film, :]
        z_ref[end + plan.film :, :] = x_ref[small : small + plan.film, :]


def late_kernel(plan, last2_ref, *refs):
    *z_refs, to_x_ref, to_y_ref, kept_ref = refs
    rows = plan.rows
    for group, out_ref in enumerate((to_x_ref, to_y_ref)):
        for second in range(2):
            spot = slice((group * 2 + second) * rows, (group * 2 + second + 1) * rows)
            total = last2_ref[spot, :]
            for z_ref in z_refs:
                total = total + z_ref[spot, :].astype(F32)
            if second:
                out_ref[...] = total.astype(BF16)
            else:
                kept_ref[group * rows : (group + 1) * rows, :] = total


def finish_kernel(plan, last1_ref, kept2_ref, late_x_ref, late_y_ref, mine_ref, x_ref, *refs):
    *z_refs, out_ref, film_ref = refs
    rows = plan.rows // 2
    for slot in range(4):
        at = slice(slot * rows, (slot + 1) * rows)
        total = last1_ref[at, :]
        for z_ref in z_refs:
            total = total + z_ref[at, :].astype(F32)
        out_ref[0, slot] = total
        late_ref = late_y_ref if slot // 2 else late_x_ref
        inner = slice(slot % 2 * rows, (slot % 2 + 1) * rows)
        out_ref[1, slot] = kept2_ref[at, :] + late_ref[inner, :].astype(F32)
    small, end = plan.weights // 8, 2 * plan.rows
    packs = [ref.at[small : small + plan.film, :] for ref in (mine_ref, x_ref)]
    for z_ref in z_refs:
        packs += [z_ref.at[end + i * plan.film : end + (i + 1) * plan.film, :] for i in range(2)]
    pair = 2 * plan.film_rows
    embedding = jnp.concatenate([get_noise(pack, pair) for pack in packs], axis=0).T
    members = [get_pair(pack.at[:pair, :]) for pack in packs]
    half = plan.film_rows // LAYERS
    for layer in range(LAYERS):
        for part in range(half):
            row = layer * half + part
            total = jnp.zeros((2 * NOISE_FREQ, LANES), F32)
            for member, value in enumerate(members):
                weight = embedding[: 2 * NOISE_FREQ, member : member + 1]
                total += weight * value[row : row + 1, :]
            film_ref[layer, :, part * LANES : (part + 1) * LANES] = total


def film_kernel(rows_ref, out_ref):
    members, _, columns = rows_ref.shape
    rows = rows_ref[...]
    lane = lax.broadcasted_iota(jnp.int32, (1, LANES), 1)
    noise = jnp.ones((1, LANES), F32)
    for member in range(members):
        noise = jnp.where(lane == member, rows[member, LAYERS:, :1], noise)
    embedding = embedding_of(jnp.broadcast_to(noise, (2 * NOISE_FREQ, LANES)), 0)
    for layer in range(LAYERS):
        total = jnp.zeros((2 * NOISE_FREQ, columns), F32)
        for member in range(members):
            total += embedding[:, member : member + 1] * rows[member, layer : layer + 1, :]
        out_ref[layer] = total


def whole():
    return pl.BlockSpec(memory_space=pltpu.VMEM)


def apart():
    return pl.BlockSpec(memory_space=pltpu.HBM)


def call(kernel, args, outs, scratch=(), flops=0, specs=None, limit=10 << 20, sems=()):
    moved = sum(a.size * a.dtype.itemsize for a in args)
    moved += sum(math.prod(shape) * jnp.dtype(kind).itemsize for shape, kind in outs)
    return pl.pallas_call(
        kernel,
        out_shape=[jax.ShapeDtypeStruct(shape, kind) for shape, kind in outs],
        in_specs=specs or [whole() for _ in args],
        out_specs=[whole() for _ in outs],
        scratch_shapes=[pltpu.VMEM(shape, kind) for shape, kind in scratch] + list(sems),
        compiler_params=pltpu.CompilerParams(vmem_limit_bytes=limit),
        cost_estimate=pl.CostEstimate(flops=flops, bytes_accessed=moved, transcendentals=0),
    )(*args)


def swap(block, axis, bit):
    count = lax.axis_size(axis)
    return lax.ppermute(block, axis, [(i, i ^ bit) for i in range(count)])


def exchange_other(to_other):
    count = lax.axis_size(MESH)
    route = []
    for i in range(1, count - 1, 2):
        route += [(i, i + 1), (i + 1, i)]
    return lax.ppermute(to_other, MESH, route)


def exchange(to_pair, to_other):
    other = exchange_other(to_other)
    return swap(to_pair, MESH, 1), other


class Plan:
    def __init__(self, width, ens_count, mesh_count):
        self.deep = ens_count // 2
        self.rows = 2 * width // ens_count
        self.weights = 8 * self.deep * self.rows
        self.film_rows = LAYERS * (2 * width // mesh_count) // LANES
        self.film = 16 * pl.cdiv(2 * self.film_rows + 3, 16)

    def at(self, group, first, second, z):
        return (((group * 2 + first) * 2 + second) * self.deep + z) * self.rows


def film_pieces(rows, noise_level, mesh_count):
    mesh = lax.axis_index(MESH)
    width = rows.shape[1] // mesh_count
    pieces = rows.reshape(LAYERS, mesh_count, width).transpose(1, 0, 2)
    pieces = jnp.take(pieces, lax.bitwise_xor(jnp.arange(mesh_count), mesh), axis=0)
    noise = jnp.where(jnp.arange(mesh_count) == 0, noise_level[0], 0.0)
    noise = jnp.broadcast_to(noise[:, None, None], (mesh_count, 1, width))
    return jnp.concatenate([pieces, noise], axis=1)


def film_mesh_step(pieces, bit):
    pieces = pieces.reshape(-1, 2, *pieces.shape[1:])
    return pieces[:, 0] + swap(pieces[:, 1], MESH, bit)


def film_ens_step(rows, bit):
    return jnp.concatenate([rows, swap(rows, ENS, bit)])


def film_end(rows):
    shape = (LAYERS, 2 * NOISE_FREQ, rows.shape[2])
    return call(film_kernel, (rows,), [(shape, F32)])[0]


def bits_of(count):
    return [1 << index for index in range(count.bit_length() - 1)]


def bind(kernel, *settings):
    return functools.partial(kernel, *settings)


def body(inputs, cotangent, noise_level, neighbours, live_slots, projections, film_weights):
    states, cot = inputs[0], cotangent[0]
    nodes, width = states.shape
    rim = nodes // 2
    mesh_count, ens_count = lax.axis_size(MESH), lax.axis_size(ENS)
    side_o, side_p = halves(lax.rem(lax.axis_index(MESH), 2), rim)
    square = 2 * nodes * width * width
    split = mesh_count == 4 and width % (mesh_count * LANES) == 0 and ens_count % 2 == 0
    plan = Plan(width, ens_count, mesh_count) if split else None

    def full(kind=BF16):
        return ((nodes, width), kind)

    def part(kind=BF16):
        return ((rim, width), kind)

    def block(rows, kind=BF16):
        return ((rows, LANES), kind)

    def hbm(value):
        return pltpu.with_memory_space_constraint(value, pltpu.HBM)

    smem = pl.BlockSpec(memory_space=pltpu.SMEM)
    cond_shape = ((1, 2 * width), F32)
    slots = neighbours.shape[1]
    table = ((slots, nodes), jnp.int32)
    x_o, x_p, near, live, film_w, emb_row = call(
        load_kernel,
        (hbm(states), hbm(neighbours.T), hbm(live_slots.T), hbm(film_weights), noise_level),
        [part(), part(), table, table, (film_weights.shape, F32), ((8, LANES), F32)],
        sems=[pltpu.SemaphoreType.DMA((5,))], specs=[apart()] * 4 + [smem],
    )
    halo_p, halo_o = exchange(x_p, x_o)
    film, bias_o, bias_p, normed1, q1, k1, v1, projections = call(
        start_kernel, (x_o, x_p, near, live, emb_row, film_w, hbm(projections)),
        [((LAYERS, 2 * width), F32)] + [((rim, 3 * rim), F32)] * 2 + [full()] * 4
        + [(projections.shape, BF16)],
        scratch=[((nodes, slots), F32)],
        sems=[pltpu.SemaphoreType.DMA((2,))], flops=3 * square,
        specs=[whole()] * 6 + [apart()],
    )
    probs_shapes = [((HEADS, rim, nodes), BF16), ((HEADS, rim, rim), BF16)]

    def forward(half, x, halo, bias):
        return call(
            bind(forward_kernel, half), (x, halo, film, q1, k1, v1, bias, projections),
            [part()] * 4 + probs_shapes + [part()], flops=2 * square,
        )

    next_o, normed1_o, k1_o, v1_o, own_o, over_o, attended1_o = forward(0, x_o, halo_o, bias_o)
    halo2_o = exchange_other(next_o)
    next_p, normed1_p, k1_p, v1_p, own_p, over_p, attended1_p = forward(1, x_p, halo_p, bias_p)
    halo2_p = swap(next_p, MESH, 1)
    normed2, q2, k2, v2, ga2, cot2 = call(
        own_kernel, (next_o, next_p, cot, film, projections), [full()] * 6, flops=4 * square
    )

    def last(half, halo, bias, parts):
        grads = [part(), full(F32), full(F32)] if half else [part(), full(), full()]
        return call(
            bind(last_layer_kernel, half),
            (halo, film, q2, k2, v2, ga2, bias, projections, *parts),
            [part()] * 2 + grads + [part()] * 3,
            flops=4 * square,
        )

    normed2_p, attended2_p, gq2_p, *parts, gk2_p, gv2_p, to_pair = last(1, halo2_p, bias_p, ())
    back_p = swap(to_pair, MESH, 1)
    normed2_o, attended2_o, gq2_o, gk2, gv2, gk2_o, gv2_o, to_other = last(
        0, halo2_o, bias_o, parts
    )
    back_o = exchange_other(to_other)
    gn2, cond2 = call(
        bind(grads_kernel, 1),
        (next_o, next_p, halo2_o, halo2_p, gq2_o, gq2_p, gk2, gv2, to_other, to_pair, projections),
        [full(F32), cond_shape], flops=4 * square,
    )

    def weight_grads(parts, *args):
        if not split:
            return call(plain_weight_kernel, args, [((4, width, width), F32)], flops=6 * square)
        return call(
            bind(split_weight_kernel, plan), args,
            [block(plan.weights // parts)] * parts + [block(plan.weights, F32)],
            flops=6 * square,
        )

    weights2 = weight_grads(
        1, normed2, normed2_o, normed2_p, attended2_o, attended2_p, cot2[:rim], cot2[rim:],
        gq2_o, gq2_p, gk2, gk2_o, gk2_p, gv2, gv2_o, gv2_p,
    )
    if split:
        sums = plan.weights
        came = swap(weights2[0], MESH, 1)
        to_y, to_x, kept2 = call(
            bind(start_scatter_kernel, plan), (weights2[1], came),
            [block(sums // 4)] * 2 + [block(sums // 2, F32)],
        )
        y2, x2 = swap(to_y, MESH, 2), swap(to_x, ENS, 1)

    def first(half, nxt, back, k_h, v_h, own, over, parts):
        grads = [part(), full(F32), full(F32)] if half else [part(), full(), full()]
        return call(
            bind(first_layer_kernel, half),
            (nxt, cot2, gn2, back, film, q1, k1, v1, k_h, v_h, own, over, projections, *parts),
            [part()] + grads + [part()] * 3,
            flops=4 * square,
        )

    up_p, gq1_p, *parts, gk1_p, gv1_p, to_pair = first(
        1, next_p, back_p, k1_p, v1_p, own_p, over_p, ()
    )
    up_o, gq1_o, gk1, gv1, gk1_o, gv1_o, to_other = first(
        0, next_o, back_o, k1_o, v1_o, own_o, over_o, parts
    )
    weights1 = weight_grads(
        2, normed1, normed1_o, normed1_p, attended1_o, attended1_p, up_o, up_p,
        gq1_o, gq1_p, gk1, gk1_o, gk1_p, gv1, gv1_o, gv1_p,
    )
    if split:
        core_x, core_y = swap(weights1[1], MESH, 1), swap(weights1[0], MESH, 1)
    back_o = exchange_other(to_other)
    back_p = swap(to_pair, MESH, 1)
    gn1, conds = call(
        bind(grads_kernel, 0),
        (x_o, x_p, halo_o, halo_p, gq1_o, gq1_p, gk1, gv1, to_other, to_pair, projections, cond2),
        [full(F32), ((LAYERS, 2 * width), F32)], flops=4 * square,
    )
    grad_input = call(end_kernel, (x_o, x_p, up_o, up_p, gn1, back_o, back_p, film), [full()])[0]
    if split:
        conds_came = swap(conds, MESH, 1)
        others = range(1, plan.deep)
        to_x, kept_x = call(
            bind(slot_ax_kernel, plan), (weights1[2], core_x),
            [block(sums // 4), block(sums // 4, F32)],
        )
        came_x = swap(to_x, ENS, 1)
        to_y, kept_y, film_mine = call(
            bind(slot_ay_kernel, plan), (weights1[2], core_y, conds, conds_came),
            [block(sums // 4 + plan.film), block(sums // 4, F32), block(plan.film_rows, F32)],
            scratch=[(conds.shape, F32), block(plan.film_rows, F32)],
        )
        came_y = swap(to_y, MESH, 2)
        last2, *to_z = call(
            bind(across_kernel, plan), (kept2, y2, x2),
            [block(4 * plan.rows, F32)] + [block(4 * plan.rows) for _ in others],
        )
        came_z2 = [swap(to_z[z - 1], ENS, 2 * z) for z in others]
        to_y, kept_y_next = call(
            bind(slot_by_kernel, plan), (kept_x, came_x),
            [block(sums // 8), block(sums // 8, F32)],
        )
        came_y2 = swap(to_y, MESH, 2)
        to_x, kept_x_next = call(
            bind(slot_bx_kernel, plan), (kept_y, film_mine, came_y, emb_row),
            [block(sums // 8 + plan.film), block(sums // 8, F32)],
        )
        came_x = swap(to_x, ENS, 1)
        last1, *to_z = call(
            bind(slot_c_kernel, plan), (kept_x_next, kept_y_next, came_x, came_y2, to_x),
            [block(2 * plan.rows, F32)] + [block(2 * plan.rows + 2 * plan.film) for _ in others],
        )
        came_z1 = [swap(to_z[z - 1], ENS, 2 * z) for z in others]
        late_x, late_y, kept2 = call(
            bind(late_kernel, plan), (last2, *came_z2),
            [block(plan.rows)] * 2 + [block(2 * plan.rows, F32)],
        )
        late_x, late_y = swap(late_x, ENS, 1), swap(late_y, MESH, 2)
        weight_out, film_out = call(
            bind(finish_kernel, plan),
            (last1, kept2, late_x, late_y, to_x, came_x, *came_z1),
            [((LAYERS, 4, width // ens_count, LANES), F32),
             ((LAYERS, 2 * NOISE_FREQ, 2 * width // mesh_count), F32)],
        )
    else:
        film_rows = film_pieces(conds, noise_level, mesh_count)
        for bit in bits_of(mesh_count):
            film_rows = film_mesh_step(film_rows, bit)
        for bit in bits_of(ens_count):
            film_rows = film_ens_step(film_rows, bit)
        film_out = film_end(film_rows)
        total = jnp.stack([weights1[0], weights2[0]]).astype(BF16)
        total = lax.psum_scatter(total, ENS, scatter_dimension=2, tiled=True)
        weight_out = lax.psum_scatter(total, MESH, scatter_dimension=3, tiled=True).astype(F32)
    return (grad_input[None], weight_out, film_out)


def solution(mesh):
    placed = (
        P(ENS, MESH, None),
        P(ENS, MESH, None),
        P(ENS),
        P(MESH, None),
        P(MESH, None),
        P(),
        P(),
    )
    return jax.shard_map(
        body,
        mesh=mesh,
        in_specs=placed,
        out_specs=(P(ENS, MESH, None), P(None, None, ENS, MESH), P(None, None, MESH)),
        check_vma=False,
    )
```
